32 devices in a mesh: context: 8 (over z, y), tensor: 4 (over x, core).
Axes of the slice: x: 2, y: 2, z: 4, core: 2. Of those that a mesh axis runs over, the one named last changes fastest.
Arguments:
- tokens: bfloat16 [4096, 4096], P(('context', 'tensor')), may hold values from -6 to 6
- norm_gain: float32 [4096], replicated, may hold values from 0.5 to 1.5
- in_weight: bfloat16 [4096, 3, 2048], P(None, None, 'tensor'), may hold values from -0.09375 to 0.09375
- short_weight: float32 [3, 3, 2048], P(None, None, 'tensor'), may hold values from -3 to 3
- long_filter: float32 [4096, 2048], P('context', 'tensor'), may hold values from -0.09375 to 0.09375
- skip_gain: float32 [2048], P('tensor'), may hold values from -4 to 4
Outputs:
- block_out: bfloat16 [4096, 2048], P('context', 'tensor')
The draws below stay inside these ranges and needn't reach their ends.
All inputs are finite; a program needn't handle non-finite values.
Results may differ from the reference program's by a relative error of at most 0.0065.
Values may be sent and summed in bfloat16 or wider, within the bound.
No kernel may reach another device: no remote copies, remote signals or barrier semaphores. Data moves between devices by JAX's collectives and lax.ppermute only.
A program may use at most 128 MiB of HBM per device.

```python
import jax
import jax.numpy as jnp
from jax import lax

D = 4096
HC = 2048
KSHORT = 3
SEQ = 4096


def block_levels(stream_key, dims, cuts, low, largest):
    factor_of, own = 1.0, jax.random.fold_in(stream_key, 6)
    for position, blocks in cuts:
        steps = jnp.exp(jax.random.uniform(jax.random.fold_in(own, position), (blocks,), jnp.float32, low / len(cuts), largest / len(cuts)))
        factor_of = factor_of * jnp.repeat(steps, dims[position] // blocks).reshape([-1 if axis == position else 1 for axis in range(len(dims))])
    return factor_of


def noise(key, extent, spread, bound, split=(), held_as=jnp.bfloat16):
    values = jax.random.normal(key, extent, jnp.float32) * spread
    if len(split) > 0:
        values = block_levels(key, extent, split, -0.22, 0.18) * values
    return jnp.clip(values, min=-bound, max=bound).astype(held_as)


def setup_inputs(seed: int = 0) -> dict:
    arg_keys = jax.random.split(jax.random.key(seed), 7)
    return {
        "tokens": noise(arg_keys[0], (SEQ, D), 1.0, 6.0, ((0, 32),)),
        "norm_gain": jnp.clip(1.0 + 0.1 * jax.random.normal(arg_keys[1], (D,), jnp.float32), 0.5, 1.5),
        "in_weight": noise(arg_keys[2], (D, 3, HC), D ** -0.5, 0.09375, ((2, 4),)),
        "short_weight": noise(arg_keys[3], (KSHORT, 3, HC), 0.6, 3.0, ((2, 4),), jnp.float32),
        "long_filter": noise(arg_keys[4], (SEQ, HC), SEQ ** -0.5, 0.09375, ((0, 8), (1, 4)), jnp.float32),
        "skip_gain": noise(arg_keys[5], (HC,), 1.0, 4.0, ((0, 4),), jnp.float32),
    }


eps = 1e-06

def reference(tokens, norm_gain, in_weight, short_weight, long_filter, skip_gain):
    values = tokens.astype(jnp.float32)
    inv_rms = lax.rsqrt(lax.optimization_barrier(jnp.mean(values * values, axis=1, keepdims=True)) + eps)
    normed = (values * inv_rms * norm_gain).astype(jnp.bfloat16)
    flat_weight = in_weight.reshape(D, 3 * HC)
    projected = jnp.dot(normed, flat_weight, preferred_element_type=jnp.float32)
    padded = jnp.concatenate([jnp.zeros((KSHORT - 1, 3 * HC), jnp.float32), projected], axis=0)
    tap_rows = short_weight.reshape(KSHORT, 3 * HC)
    mixed_rows = jnp.zeros_like(projected)
    for tap_index in range(KSHORT):
        offset = KSHORT - 1 - tap_index
        mixed_rows = mixed_rows + tap_rows[tap_index] * padded[offset:offset + SEQ]
    query_part = mixed_rows[:, :HC]
    key_part = mixed_rows[:, HC:2 * HC]
    value_part = mixed_rows[:, 2 * HC:]
    gated = key_part * value_part
    block_width = min(HC, 256)
    pieces = []
    for first_col in range(0, HC, block_width):
        gated_cols = gated[:, first_col:first_col + block_width]
        filt_cols = long_filter[:, first_col:first_col + block_width]
        product = jnp.fft.rfft(gated_cols, n=2 * SEQ, axis=0) * jnp.fft.rfft(filt_cols, n=2 * SEQ, axis=0)
        pieces.append(jnp.fft.irfft(product, n=2 * SEQ, axis=0)[:SEQ])
    conv = jnp.concatenate(pieces, axis=1)
    block_out = query_part * (conv + skip_gain * gated)
    return block_out.astype(jnp.bfloat16)
```

```python
import functools
import math

import jax
import jax.numpy as jnp
import numpy as np
from jax import lax
from jax.experimental import pallas as pl
from jax.experimental.pallas import tpu as pltpu
from jax.sharding import PartitionSpec as P

eps = 1e-06

FINE = 256
HALF = 64
LANES = 2 * HALF
PAD = 16
BIG = 60 * 1024 * 1024

f32 = jnp.float32
bf16 = jnp.bfloat16


def lane_mask():
    return lax.broadcasted_iota(jnp.int32, (1, LANES), 1) < HALF


def pack_pair(tile):
    low = lane_mask()
    top, bot = tile[:FINE], tile[FINE:]
    return (
        jnp.where(low, top, pltpu.roll(bot, HALF, 1)),
        jnp.where(low, pltpu.roll(top, HALF, 1), bot),
    )


def unpack_pair(first, second):
    low = lane_mask()
    return (
        jnp.where(low, first, pltpu.roll(second, HALF, 1)),
        jnp.where(low, pltpu.roll(first, HALF, 1), second),
    )


def pack_kernel(in_ref, out_ref):
    first, second = pack_pair(in_ref[...])
    out_ref[0] = first.astype(bf16)
    out_ref[1] = second.astype(bf16)


def pack_filter(filt):
    length, channels = filt.shape
    return pl.pallas_call(
        pack_kernel,
        grid=(channels // LANES,),
        in_specs=[pl.BlockSpec((length, LANES), lambda i: (0, i))],
        out_specs=pl.BlockSpec((2, FINE, LANES), lambda i: (i, 0, 0)),
        out_shape=jax.ShapeDtypeStruct((channels // HALF, FINE, LANES), bf16),
        name="pack_filter",
    )(filt)


def pack_any(rows, dev_count):
    length, channels = rows.shape
    each = channels // dev_count
    blocks = rows.astype(bf16).reshape(2, FINE, dev_count, each)
    blocks = jnp.transpose(blocks, (2, 1, 0, 3))
    blocks = jnp.pad(blocks, ((0, 0), (0, 0), (0, 0), (0, HALF - each)))
    return blocks.reshape(dev_count, FINE, LANES)


def project_kernel(taps, me_ref, halo_hbm, *refs):
    blocks = refs[:taps]
    w_ref, tap_ref, q_ref, g_ref, p_ref, x_ref, rows_ref, key_ref, sem = refs[taps:]
    part = pl.program_id(1)
    me = me_ref[0]
    each = blocks[0].shape[0]
    length = each * taps

    @pl.when((pl.program_id(0) == 0) & (part == 0))
    def _():
        copies = [pltpu.make_async_copy(halo_hbm, x_ref.at[pl.ds(0, PAD)], sem.at[taps])]
        for mask, block in enumerate(blocks):
            first = pl.multiple_of(PAD + (me ^ mask) * each, 16)
            copies.append(pltpu.make_async_copy(block, x_ref.at[pl.ds(first, each)], sem.at[mask]))
        for copy in copies:
            copy.start()
        for copy in copies:
            copy.wait()

    rows_ref[...] = jnp.dot(x_ref[...], w_ref[0], preferred_element_type=f32)

    def mixed(s):
        total = tap_ref[0, s][None, :] * rows_ref[PAD : PAD + length]
        for lag in (1, 2):
            total += tap_ref[lag, s][None, :] * rows_ref[PAD - lag : PAD - lag + length]
        return total

    @pl.when(part == 0)
    def _():
        q_ref[...] = mixed(0)

    @pl.when(part == 1)
    def _():
        key_ref[...] = mixed(1)

    @pl.when(part == 2)
    def _():
        gated = key_ref[...] * mixed(2)
        g_ref[...] = gated
        for i in range(gated.shape[1] // LANES):
            first, second = pack_pair(gated[:, i * LANES : (i + 1) * LANES])
            p_ref[2 * i] = first.astype(bf16)
            p_ref[2 * i + 1] = second.astype(bf16)


def project(me, halo, blocks, weight, taps):
    _, width, channels = weight.shape
    each = blocks[0].shape[0]
    length = each * len(blocks)
    cols = min(256, channels)
    flops = 2 * (length + PAD) * width * 3 * channels
    return pl.pallas_call(
        functools.partial(project_kernel, len(blocks)),
        grid_spec=pltpu.PrefetchScalarGridSpec(
            num_scalar_prefetch=1,
            grid=(channels // cols, 3),
            in_specs=[pl.BlockSpec(memory_space=pl.ANY)] * (1 + len(blocks))
            + [
                pl.BlockSpec((1, width, cols), lambda j, s, me: (s, 0, j)),
                pl.BlockSpec((3, 3, cols), lambda j, s, me: (0, 0, j)),
            ],
            out_specs=[
                pl.BlockSpec((length, cols), lambda j, s, me: (0, j)),
                pl.BlockSpec((length, cols), lambda j, s, me: (0, j)),
                pl.BlockSpec((cols // HALF, FINE, LANES), lambda j, s, me: (j, 0, 0)),
            ],
            scratch_shapes=[
                pltpu.VMEM((PAD + length, width), bf16),
                pltpu.VMEM((PAD + length, cols), f32),
                pltpu.VMEM((length, cols), f32),
                pltpu.SemaphoreType.DMA((len(blocks) + 1,)),
            ],
        ),
        out_shape=[
            jax.ShapeDtypeStruct((length, channels), f32),
            jax.ShapeDtypeStruct((length, channels), f32),
            jax.ShapeDtypeStruct((channels // HALF, FINE, LANES), bf16),
        ],
        compiler_params=pltpu.CompilerParams(vmem_limit_bytes=40 * 1024 * 1024),
        cost_estimate=pl.CostEstimate(
            flops=flops, bytes_accessed=2 * 3 * width * channels + 8 * length * channels, transcendentals=0
        ),
        name="project",
    )(me, halo, *blocks, weight, taps)


def coarse_forward(dev_count, x_ref, lane_ref, e_ref, step=16):
    count = dev_count
    half = count // 2
    low = lane_mask()
    sgn = jnp.where(low, 1.0, -1.0).astype(f32)

    def body(i, carry):
        rows = pl.ds(pl.multiple_of(i * step, step), step)
        x = [x_ref[s, rows, :].astype(f32) for s in range(count)]
        plus = [x[s] + x[count - s] for s in range(1, half)]
        minus = [x[s] - x[count - s] for s in range(1, half)]
        for k in range(count + 1):
            even = k % 2 == 0
            re = x[0]
            im = None
            mid = round(math.cos(math.pi * half * k / count))
            if mid:
                re = re + x[half] if mid > 0 else re - x[half]
            mid = round(math.sin(math.pi * half * k / count))
            if mid:
                im = -x[half] if mid > 0 else x[half]
            for s in range(1, half):
                c, d = math.cos(math.pi * s * k / count), math.sin(math.pi * s * k / count)
                if abs(c) > 1e-9:
                    re = re + c * (plus if even else minus)[s - 1]
                if abs(d) > 1e-9:
                    term = (-d) * (minus if even else plus)[s - 1]
                    im = term if im is None else im + term
            c, d = lane_ref[k, 0:1, :], lane_ref[k, 1:2, :]
            if im is None:
                re, im = re * c, re * (-d)
            else:
                re, im = re * c + im * d, im * c - re * d
            e_ref[k, rows, :LANES] = pltpu.roll(re, HALF, 1) + sgn * re
            e_ref[k, rows, LANES:] = sgn * pltpu.roll(im, HALF, 1) + im
        return carry

    lax.fori_loop(0, FINE // step, body, 0)


def coarse_inverse(dev_count, g_ref, y_ref, step=16):
    count = dev_count
    half = count // 2

    def body(i, carry):
        rows = pl.ds(pl.multiple_of(i * step, step), step)
        acc = {}

        def add(name, s, term):
            acc[name, s] = term if (name, s) not in acc else acc[name, s] + term

        for k in range(count + 1):
            even = k % 2 == 0
            re, im = g_ref[k, rows, :LANES], g_ref[k, rows, LANES:]
            add("first", 0, re)
            mid = round(math.cos(math.pi * half * k / count))
            if mid:
                add("mid", 0, re if mid > 0 else -re)
            mid = round(math.sin(math.pi * half * k / count))
            if mid:
                add("mid", 0, -im if mid > 0 else im)
            for s in range(1, half):
                c, d = math.cos(math.pi * s * k / count), math.sin(math.pi * s * k / count)
                if abs(c) > 1e-9:
                    add("a" if even else "b", s, c * re)
                if abs(d) > 1e-9:
                    add("b" if even else "a", -s, (-d) * im)
        y_ref[0, rows, :] = acc["first", 0].astype(bf16)
        y_ref[half, rows, :] = acc["mid", 0].astype(bf16)
        zero = jnp.zeros((step, LANES), f32)
        for s in range(1, half):
            same = acc.get(("a", s), zero)
            flip = acc.get(("b", s), zero)
            same_sin = acc.get(("a", -s), zero)
            flip_sin = acc.get(("b", -s), zero)
            total, diff = same + same_sin, flip + flip_sin
            y_ref[s, rows, :] = (total + diff).astype(bf16)
            y_ref[count - s, rows, :] = (total - diff).astype(bf16)
        return carry

    lax.fori_loop(0, FINE // step, body, 0)


def fine_forward(e, tr, ti, table):
    re, im = e[:, :LANES], e[:, LANES:]
    turned = jnp.concatenate([re * tr - im * ti, re * ti + im * tr], axis=1).astype(bf16)
    both = jnp.dot(table, turned, preferred_element_type=f32)
    return (
        both[:FINE, :LANES] - both[FINE:, LANES:],
        both[:FINE, LANES:] + both[FINE:, :LANES],
    )


def next_turn(turn_ref, step_ref):
    tr, ti = turn_ref[:, :LANES], turn_ref[:, LANES:]
    sr, si = step_ref[:, :LANES], step_ref[:, LANES:]
    turn_ref[:, :LANES] = tr * sr - ti * si
    turn_ref[:, LANES:] = tr * si + ti * sr


def filter_kernel(dev_count, x_ref, first_ref, step_ref, lane_ref, table_ref, h_ref, e_ref, turn_ref):
    coarse_forward(dev_count, x_ref, lane_ref, e_ref)
    turn_ref[...] = first_ref[...]
    points = 4 * dev_count * FINE

    def body(k, carry):
        re, im = fine_forward(e_ref[k], turn_ref[:, :LANES], turn_ref[:, LANES:], table_ref[...])
        scale = jnp.where((k == 0) | (k == dev_count), 1.0 / points, 2.0 / points).astype(f32)
        h_ref[k, :, :LANES] = re * scale
        h_ref[k, :, LANES:] = im * scale
        next_turn(turn_ref, step_ref)
        return carry

    lax.fori_loop(0, dev_count + 1, body, 0, unroll=dev_count <= 8)


def conv_kernel(dev_count, x_ref, h_hbm, first_ref, step_ref, lane_ref, table_ref, y_ref, h_ref, e_ref, turn_ref, sem):
    copy = pltpu.make_async_copy(h_hbm, h_ref, sem)
    copy.start()
    coarse_forward(dev_count, x_ref, lane_ref, e_ref)
    turn_ref[...] = first_ref[...]
    sgn = jnp.where(lane_mask(), 1.0, -1.0).astype(f32)
    copy.wait()

    def body(k, carry):
        tr, ti = turn_ref[:, :LANES], turn_ref[:, LANES:]
        re, im = fine_forward(e_ref[k], tr, ti, table_ref[...])
        hr, hi = h_ref[k, :, :LANES], h_ref[k, :, LANES:]
        prod = jnp.concatenate([re * hr - im * hi, re * hi + im * hr], axis=1).astype(bf16)
        both = jnp.dot(table_ref[...], prod, preferred_element_type=f32)
        re = both[:FINE, :LANES] + both[FINE:, LANES:]
        im = both[:FINE, LANES:] - both[FINE:, :LANES]
        re, im = re * tr + im * ti, (im * tr - re * ti) * sgn
        re, im = pltpu.roll(re, HALF, 1) + sgn * re, pltpu.roll(im, HALF, 1) + sgn * im
        c, d = lane_ref[k, 0:1, :], lane_ref[k, 1:2, :]
        e_ref[k, :, :LANES] = re * c - im * d
        e_ref[k, :, LANES:] = re * d + im * c
        next_turn(turn_ref, step_ref)
        return carry

    lax.fori_loop(0, dev_count + 1, body, 0, unroll=dev_count <= 8)
    coarse_inverse(dev_count, e_ref, y_ref)


def tables(dev_count):
    points = 4 * dev_count * FINE
    fine = np.arange(FINE)
    first = np.exp(-2j * np.pi * fine * (2 * dev_count) / points)[:, None] * np.ones(HALF)
    ones = np.ones((FINE, HALF))
    step = np.exp(-2j * np.pi * fine / points)[:, None] * ones
    first = np.concatenate([ones, first.real, 0 * ones, first.imag], axis=1)
    step = np.concatenate([step.real, step.real, step.imag, -step.imag], axis=1)
    turn = 2 * np.pi * np.arange(dev_count + 1)[:, None] * np.ones(HALF) / (4 * dev_count)
    lane = np.stack(
        [
            np.concatenate([np.ones_like(turn), np.cos(turn)], axis=1),
            np.concatenate([np.zeros_like(turn), np.sin(turn)], axis=1),
        ],
        axis=1,
    )
    angle = -2 * np.pi * (fine[:, None] * fine[None, :] % FINE) / FINE
    table = np.concatenate([np.cos(angle), np.sin(angle)], axis=0)
    return (
        jnp.asarray(first, f32),
        jnp.asarray(step, f32),
        jnp.asarray(lane, f32),
        jnp.asarray(table, bf16),
    )


VMEM_SPEC = pl.BlockSpec(memory_space=pltpu.VMEM)


def filter_spectrum(x, consts):
    dev_count = x.shape[0]
    return pl.pallas_call(
        functools.partial(filter_kernel, dev_count),
        in_specs=[VMEM_SPEC] * 5,
        out_specs=VMEM_SPEC,
        out_shape=jax.ShapeDtypeStruct((dev_count + 1, FINE, 2 * LANES), f32),
        scratch_shapes=[
            pltpu.VMEM((dev_count + 1, FINE, 2 * LANES), f32),
            pltpu.VMEM((FINE, 2 * LANES), f32),
        ],
        compiler_params=pltpu.CompilerParams(vmem_limit_bytes=BIG),
        name="filter_spectrum",
    )(x, *consts)


def convolve(x, spectrum, consts):
    dev_count = x.shape[0]
    return pl.pallas_call(
        functools.partial(conv_kernel, dev_count),
        in_specs=[VMEM_SPEC, pl.BlockSpec(memory_space=pl.ANY)] + [VMEM_SPEC] * 4,
        out_specs=VMEM_SPEC,
        out_shape=jax.ShapeDtypeStruct((dev_count, FINE, LANES), bf16),
        scratch_shapes=[
            pltpu.VMEM((dev_count + 1, FINE, 2 * LANES), f32),
            pltpu.VMEM((dev_count + 1, FINE, 2 * LANES), f32),
            pltpu.VMEM((FINE, 2 * LANES), f32),
            pltpu.SemaphoreType.DMA,
        ],
        compiler_params=pltpu.CompilerParams(vmem_limit_bytes=BIG),
        name="convolve",
    )(x, spectrum, *consts)


def finish_kernel(c_ref, q_ref, g_ref, skip_ref, out_ref):
    top, bot = unpack_pair(c_ref[0].astype(f32), c_ref[1].astype(f32))
    for i, conv in enumerate((top, bot)):
        rows = slice(i * FINE, (i + 1) * FINE)
        out_ref[rows, :] = (q_ref[rows, :] * (conv + skip_ref[...] * g_ref[rows, :])).astype(bf16)


def finish(conv, query, gated, skip_gain):
    length, channels = query.shape
    tile = pl.BlockSpec((length, LANES), lambda i: (0, i))
    return pl.pallas_call(
        finish_kernel,
        grid=(channels // LANES,),
        in_specs=[
            pl.BlockSpec((2, FINE, LANES), lambda i: (i, 0, 0)),
            tile,
            tile,
            pl.BlockSpec((1, LANES), lambda i: (0, i)),
        ],
        out_specs=tile,
        out_shape=jax.ShapeDtypeStruct((length, channels), bf16),
        name="finish",
    )(conv, query, gated, skip_gain.reshape(1, channels))


def local(tokens, norm_gain, in_weight, short_weight, long_filter, skip_gain):
    dev_count = lax.axis_size("context")
    tensor_count = lax.axis_size("tensor")
    channels = in_weight.shape[2]
    packed = channels // dev_count == HALF
    consts = tables(dev_count)

    values = tokens.astype(f32)
    inv_rms = lax.rsqrt(jnp.mean(values * values, axis=1, keepdims=True) + eps)
    normed = (values * inv_rms * norm_gain).astype(bf16)

    blocks = {0: normed}
    bit = tensor_count // 2
    while bit:
        pairs = [(i, i ^ bit) for i in range(tensor_count)]
        for mask in list(blocks):
            blocks[mask | bit] = lax.ppermute(blocks[mask], "tensor", pairs)
        bit //= 2
    blocks = [blocks[mask] for mask in range(tensor_count)]

    tail = normed[-8:]
    halo = jnp.zeros_like(tail)
    last = tensor_count - 1
    for t in range(tensor_count):
        pairs = [(c * tensor_count + last, (c + 1) * tensor_count + t) for c in range(dev_count - 1)]
        halo = halo + lax.ppermute(tail, ("context", "tensor"), pairs)
    halo = jnp.concatenate([jnp.zeros((PAD - 8, halo.shape[1]), bf16), halo], axis=0)

    exchange = functools.partial(
        lax.all_to_all, axis_name="context", split_axis=0, concat_axis=0, tiled=True
    )
    filt = exchange(pack_filter(long_filter) if packed else pack_any(long_filter, dev_count))
    spectrum = filter_spectrum(filt, consts)

    me = lax.axis_index("tensor").astype(jnp.int32).reshape(1)
    query, gated, sent = project(me, halo, blocks, jnp.transpose(in_weight, (1, 0, 2)), short_weight)
    if not packed:
        sent = pack_any(gated, dev_count)
    conv = exchange(convolve(exchange(sent), spectrum, consts))
    if packed:
        return finish(conv, query, gated, skip_gain)
    each = channels // dev_count
    conv = conv.reshape(dev_count, FINE, 2, HALF)[..., :each]
    conv = jnp.transpose(conv, (2, 1, 0, 3)).reshape(2 * FINE, channels).astype(f32)
    return (query * (conv + skip_gain * gated)).astype(bf16)


def solution(mesh):
    return jax.shard_map(
        local,
        mesh=mesh,
        in_specs=(
            P(("context", "tensor"), None),
            P(),
            P(None, None, "tensor"),
            P(None, None, "tensor"),
            P("context", "tensor"),
            P("tensor"),
        ),
        out_specs=P("context", "tensor"),
        check_vma=False,
    )
```

```python
import functools
import math

import jax
import jax.numpy as jnp
import numpy as np
from jax import lax
from jax.experimental import pallas as pl
from jax.experimental.pallas import tpu as pltpu
from jax.sharding import PartitionSpec as P

eps = 1e-06

FINE = 256
HALF = 64
LANES = 2 * HALF
TAIL = 8
PAD = 16
BIG = 60 * 1024 * 1024
COST = (10**8, 10**8, 10**8)

VMEM_SPEC = pl.BlockSpec(memory_space=pltpu.VMEM)
HBM_SPEC = pl.BlockSpec(memory_space=pltpu.HBM)
ANY_SPEC = pl.BlockSpec(memory_space=pl.ANY)

f32 = jnp.float32
bf16 = jnp.bfloat16


def lane_mask():
    return lax.broadcasted_iota(jnp.int32, (1, LANES), 1) < HALF


def pack_pair(tile):
    low = lane_mask()
    rows = tile.shape[0] // 2
    top, bot = tile[:rows], tile[rows:]
    return (
        jnp.where(low, top, pltpu.roll(bot, HALF, 1)),
        jnp.where(low, pltpu.roll(top, HALF, 1), bot),
    )


def unpack_pair(first, second):
    low = lane_mask()
    return (
        jnp.where(low, first, pltpu.roll(second, HALF, 1)),
        jnp.where(low, pltpu.roll(first, HALF, 1), second),
    )


def start_all(copies):
    copies = [pltpu.make_async_copy(*copy) for copy in copies]
    for copy in copies:
        copy.start()
    return copies


def pack_any(rows, dev_count):
    length, channels = rows.shape
    each = channels // dev_count
    blocks = rows.astype(bf16).reshape(2, length // 2, dev_count, each)
    blocks = jnp.transpose(blocks, (2, 1, 0, 3))
    blocks = jnp.pad(blocks, ((0, 0), (0, 0), (0, 0), (0, HALF - each)))
    return blocks.reshape(dev_count, length // 2, LANES)


def norm_rows(tokens, gain):
    rows, width = tokens.shape
    step = min(32, rows)

    def kernel(tok_hbm, gain_hbm, out_ref, tail_ref, tok_ref, gain_ref, sem):
        parts = [pl.ds(i * step, step) for i in range(rows // step)]
        copies = start_all(
            [(gain_hbm, gain_ref, sem.at[len(parts)])]
            + [(tok_hbm.at[part], tok_ref.at[part], sem.at[i]) for i, part in enumerate(parts)]
        )
        copies[0].wait()
        for part, copy in zip(parts, copies[1:]):
            copy.wait()
            values = tok_ref[part, :].astype(f32)
            inv_rms = lax.rsqrt(jnp.mean(values * values, axis=1, keepdims=True) + eps)
            normed = (values * inv_rms * gain_ref[...]).astype(bf16)
            out_ref[part, :] = normed
            tail_ref[...] = normed[step - TAIL :]

    return pl.pallas_call(
        kernel,
        in_specs=[HBM_SPEC] * 2,
        out_specs=[VMEM_SPEC] * 2,
        out_shape=[jax.ShapeDtypeStruct((rows, width), bf16), jax.ShapeDtypeStruct((TAIL, width), bf16)],
        scratch_shapes=[
            pltpu.VMEM((rows, width), bf16),
            pltpu.VMEM((1, width), f32),
            pltpu.SemaphoreType.DMA((rows // step + 1,)),
        ],
        compiler_params=pltpu.CompilerParams(vmem_limit_bytes=BIG),
        name="norm_rows",
    )(tokens, gain.reshape(1, width))


def pack_into(p_ref, at, rows_ref):
    rows = pl.ds(at, rows_ref.shape[0] // 2)
    for i in range(p_ref.shape[0] // 2):
        first, second = pack_pair(rows_ref[:, i * LANES : (i + 1) * LANES])
        p_ref[2 * i, rows, :] = first.astype(bf16)
        p_ref[2 * i + 1, rows, :] = second.astype(bf16)


def project_kernel(count, parts, splits, with_filter, me_ref, halo_any, *refs):
    blocks = refs[:count]
    w_hbm, tap_hbm = refs[count : count + 2]
    outs = list(refs[count + 2 : -8])
    w_ref, tap_ref, x_ref, rows_ref, filt_ref, sem, w_sem, tap_sem = refs[-8:]
    each = blocks[0].shape[0]
    length = each * count
    width = x_ref.shape[1]
    depth = width // splits

    sources = [(halo_any, x_ref.at[pl.ds(0, PAD)], sem.at[count])]
    for mask, block in enumerate(blocks):
        first = pl.multiple_of(PAD + (me_ref[0] ^ mask) * each, 16)
        sources.append((block, x_ref.at[pl.ds(first, each)], sem.at[mask]))
    waits = start_all(sources + [(tap_hbm, tap_ref, tap_sem)])
    loads = {}
    for at, s in enumerate(parts):
        for i in range(splits):
            chunk = pl.ds(i * depth, depth)
            loads[s, i] = start_all([(w_hbm.at[s, chunk], w_ref.at[at, chunk], w_sem.at[at, i])])[0]
    if with_filter:
        filt_hbm, outs = outs[0], outs[1:]
        filt_load = start_all([(filt_hbm, filt_ref, sem.at[count + 1])])[0]
    for wait in waits:
        wait.wait()

    def mixed(s):
        at = parts.index(s)
        total = None
        for i in range(splits):
            loads[s, i].wait()
            chunk = slice(i * depth, (i + 1) * depth)
            term = jnp.dot(x_ref[:, chunk], w_ref[at, chunk], preferred_element_type=f32)
            total = term if total is None else total + term
        rows_ref[...] = total
        total = tap_ref[0, s : s + 1] * rows_ref[PAD : PAD + length]
        for lag in (1, 2):
            total += tap_ref[lag, s : s + 1] * rows_ref[PAD - lag : PAD - lag + length]
        return total

    if 1 in parts:
        g_ref, p_ref = outs[:2]
        g_ref[...] = mixed(1)
        g_ref[...] *= mixed(2)
        pack_into(p_ref, 0, g_ref)
    if 0 in parts:
        outs[-1][...] = mixed(0)
    if with_filter:
        filt_load.wait()
        pack_into(p_ref, length // 2, filt_ref)


def project(parts, me, halo, blocks, weight, taps, cost, filt=None):
    _, width, channels = weight.shape
    length = blocks[0].shape[0] * len(blocks)
    splits = 2
    shapes = []
    if 1 in parts:
        rows = length // 2 if filt is None else length // 2 + filt.shape[0] // 2
        shapes += [
            jax.ShapeDtypeStruct((length, channels), f32),
            jax.ShapeDtypeStruct((max(channels // HALF, 2), rows, LANES), bf16),
        ]
    if 0 in parts:
        shapes.append(jax.ShapeDtypeStruct((length, channels), f32))
    extra = [] if filt is None else [filt]
    return pl.pallas_call(
        functools.partial(project_kernel, len(blocks), parts, splits, filt is not None),
        in_specs=[pl.BlockSpec(memory_space=pltpu.SMEM)]
        + [ANY_SPEC] * (1 + len(blocks))
        + [HBM_SPEC] * (2 + len(extra)),
        out_specs=[VMEM_SPEC] * len(shapes),
        out_shape=shapes,
        scratch_shapes=[
            pltpu.VMEM((len(parts), width, channels), bf16),
            pltpu.VMEM(taps.shape, f32),
            pltpu.VMEM((PAD + length, width), bf16),
            pltpu.VMEM((PAD + length, channels), f32),
            pltpu.VMEM((8, LANES) if filt is None else filt.shape, f32),
            pltpu.SemaphoreType.DMA((len(blocks) + 2,)),
            pltpu.SemaphoreType.DMA((len(parts), splits)),
            pltpu.SemaphoreType.DMA,
        ],
        compiler_params=pltpu.CompilerParams(vmem_limit_bytes=BIG),
        cost_estimate=pl.CostEstimate(flops=cost, bytes_accessed=10**5, transcendentals=0),
        name="project",
    )(me, halo, *blocks, weight, taps, *extra)


def coarse_forward(dev_count, x_ref, lane_ref, e_ref, step=16):
    count = dev_count
    half = count // 2
    low = lane_mask()
    sgn = jnp.where(low, 1.0, -1.0).astype(f32)

    def body(i, carry):
        rows = pl.ds(pl.multiple_of(i * step, step), step)
        x = [x_ref[s, rows, :].astype(f32) for s in range(count)]
        plus = [x[s] + x[count - s] for s in range(1, half)]
        minus = [x[s] - x[count - s] for s in range(1, half)]
        for k in range(count + 1):
            even = k % 2 == 0
            re = x[0]
            im = None
            mid = round(math.cos(math.pi * half * k / count))
            if mid:
                re = re + x[half] if mid > 0 else re - x[half]
            mid = round(math.sin(math.pi * half * k / count))
            if mid:
                im = -x[half] if mid > 0 else x[half]
            for s in range(1, half):
                c, d = math.cos(math.pi * s * k / count), math.sin(math.pi * s * k / count)
                if abs(c) > 1e-9:
                    re = re + c * (plus if even else minus)[s - 1]
                if abs(d) > 1e-9:
                    term = (-d) * (minus if even else plus)[s - 1]
                    im = term if im is None else im + term
            c, d = lane_ref[k, 0:1, :], lane_ref[k, 1:2, :]
            if im is None:
                re, im = re * c, re * (-d)
            else:
                re, im = re * c + im * d, im * c - re * d
            e_ref[k, rows, :LANES] = pltpu.roll(re, HALF, 1) + sgn * re
            e_ref[k, rows, LANES:] = sgn * pltpu.roll(im, HALF, 1) + im
        return carry

    lax.fori_loop(0, FINE // step, body, 0)


def coarse_inverse(dev_count, g_ref, y_ref, step=16):
    count = dev_count
    half = count // 2

    def body(i, carry):
        rows = pl.ds(pl.multiple_of(i * step, step), step)
        acc = {}

        def add(name, s, term):
            acc[name, s] = term if (name, s) not in acc else acc[name, s] + term

        for k in range(count + 1):
            even = k % 2 == 0
            re, im = g_ref[k, rows, :LANES], g_ref[k, rows, LANES:]
            add("first", 0, re)
            mid = round(math.cos(math.pi * half * k / count))
            if mid:
                add("mid", 0, re if mid > 0 else -re)
            mid = round(math.sin(math.pi * half * k / count))
            if mid:
                add("mid", 0, -im if mid > 0 else im)
            for s in range(1, half):
                c, d = math.cos(math.pi * s * k / count), math.sin(math.pi * s * k / count)
                if abs(c) > 1e-9:
                    add("a" if even else "b", s, c * re)
                if abs(d) > 1e-9:
                    add("b" if even else "a", -s, (-d) * im)
        y_ref[0, rows, :] = acc["first", 0].astype(bf16)
        y_ref[half, rows, :] = acc["mid", 0].astype(bf16)
        zero = jnp.zeros((step, LANES), f32)
        for s in range(1, half):
            same = acc.get(("a", s), zero)
            flip = acc.get(("b", s), zero)
            same_sin = acc.get(("a", -s), zero)
            flip_sin = acc.get(("b", -s), zero)
            total, diff = same + same_sin, flip + flip_sin
            y_ref[s, rows, :] = (total + diff).astype(bf16)
            y_ref[count - s, rows, :] = (total - diff).astype(bf16)
        return carry

    lax.fori_loop(0, FINE // step, body, 0)


def fine_forward(e, tr, ti, table):
    re, im = e[:, :LANES], e[:, LANES:]
    turned = jnp.concatenate([re * tr - im * ti, re * ti + im * tr], axis=1).astype(bf16)
    both = jnp.dot(table, turned, preferred_element_type=f32)
    return (
        both[:FINE, :LANES] - both[FINE:, LANES:],
        both[:FINE, LANES:] + both[FINE:, :LANES],
    )


def next_turn(turn_ref, step_ref):
    tr, ti = turn_ref[:, :LANES], turn_ref[:, LANES:]
    sr, si = step_ref[:, :LANES], step_ref[:, LANES:]
    turn_ref[:, :LANES] = tr * sr - ti * si
    turn_ref[:, LANES:] = tr * si + ti * sr


def filter_kernel(dev_count, x_any, *refs):
    const_hbm, h_ref = refs[:4], refs[4]
    x_ref, first_ref, step_ref, lane_ref, table_ref, e_ref, sem = refs[5:]
    turn_ref = first_ref
    rows = pl.ds(x_any.shape[1] - FINE, FINE)
    pairs = [(x_any.at[:, rows], x_ref)] + list(zip(const_hbm, (first_ref, step_ref, lane_ref, table_ref)))
    for copy in start_all((*pair, sem.at[i]) for i, pair in enumerate(pairs)):
        copy.wait()
    coarse_forward(dev_count, x_ref, lane_ref, e_ref)
    points = 4 * dev_count * FINE

    def body(k, carry):
        re, im = fine_forward(e_ref[k], turn_ref[:, :LANES], turn_ref[:, LANES:], table_ref[...])
        scale = jnp.where((k == 0) | (k == dev_count), 1.0 / points, 2.0 / points).astype(f32)
        h_ref[k, :, :LANES] = re * scale
        h_ref[k, :, LANES:] = im * scale
        next_turn(turn_ref, step_ref)
        return carry

    lax.fori_loop(0, dev_count + 1, body, 0, unroll=dev_count <= 8)


def merge_halves(dev_count, late_first, early_ref, late_ref, x_ref):
    pick = late_first == 1
    for s in range(dev_count):
        early, late = early_ref[s].astype(f32), late_ref[s].astype(f32)
        first, second = jnp.where(pick, late, early), jnp.where(pick, early, late)
        top, bot = pack_pair(jnp.concatenate([first, second], axis=0))
        x_ref[s, : FINE // 2] = top
        x_ref[s, FINE // 2 :] = bot


def conv_kernel(dev_count, half_ref, early_any, late_any, h_hbm, *refs):
    const_hbm, y_ref = refs[:4], refs[4]
    early_ref, late_ref, x_ref, h_ref, first_ref, step_ref, lane_ref, table_ref, e_ref, sem = refs[5:]
    turn_ref = first_ref
    pairs = [(early_any.at[:, pl.ds(0, FINE // 2)], early_ref), (late_any, late_ref)]
    pairs += list(zip(const_hbm, (first_ref, step_ref, lane_ref, table_ref))) + [(h_hbm, h_ref)]
    copies = start_all((*pair, sem.at[i]) for i, pair in enumerate(pairs))
    for copy in copies[:-1]:
        copy.wait()
    merge_halves(dev_count, half_ref[0], early_ref, late_ref, x_ref)
    coarse_forward(dev_count, x_ref, lane_ref, e_ref)
    copies[-1].wait()
    sgn = jnp.where(lane_mask(), 1.0, -1.0).astype(f32)

    def body(k, carry):
        tr, ti = turn_ref[:, :LANES], turn_ref[:, LANES:]
        re, im = fine_forward(e_ref[k], tr, ti, table_ref[...])
        hr, hi = h_ref[k, :, :LANES], h_ref[k, :, LANES:]
        prod = jnp.concatenate([re * hr - im * hi, re * hi + im * hr], axis=1).astype(bf16)
        both = jnp.dot(table_ref[...], prod, preferred_element_type=f32)
        re = both[:FINE, :LANES] + both[FINE:, LANES:]
        im = both[:FINE, LANES:] - both[FINE:, :LANES]
        re, im = re * tr + im * ti, (im * tr - re * ti) * sgn
        re, im = pltpu.roll(re, HALF, 1) + sgn * re, pltpu.roll(im, HALF, 1) + sgn * im
        c, d = lane_ref[k, 0:1, :], lane_ref[k, 1:2, :]
        e_ref[k, :, :LANES] = re * c - im * d
        e_ref[k, :, LANES:] = re * d + im * c
        next_turn(turn_ref, step_ref)
        return carry

    lax.fori_loop(0, dev_count + 1, body, 0, unroll=dev_count <= 8)
    coarse_inverse(dev_count, e_ref, y_ref)


def tables(dev_count):
    points = 4 * dev_count * FINE
    fine = np.arange(FINE)
    first = np.exp(-2j * np.pi * fine * (2 * dev_count) / points)[:, None] * np.ones(HALF)
    ones = np.ones((FINE, HALF))
    step = np.exp(-2j * np.pi * fine / points)[:, None] * ones
    first = np.concatenate([ones, first.real, 0 * ones, first.imag], axis=1)
    step = np.concatenate([step.real, step.real, step.imag, -step.imag], axis=1)
    turn = 2 * np.pi * np.arange(dev_count + 1)[:, None] * np.ones(HALF) / (4 * dev_count)
    lane = np.stack(
        [
            np.concatenate([np.ones_like(turn), np.cos(turn)], axis=1),
            np.concatenate([np.zeros_like(turn), np.sin(turn)], axis=1),
        ],
        axis=1,
    )
    angle = -2 * np.pi * (fine[:, None] * fine[None, :] % FINE) / FINE
    table = np.concatenate([np.cos(angle), np.sin(angle)], axis=0)
    return (
        jnp.asarray(first, f32),
        jnp.asarray(step, f32),
        jnp.asarray(lane, f32),
        jnp.asarray(table, bf16),
    )


def const_scratch(consts):
    return [pltpu.VMEM(const.shape, const.dtype) for const in consts]


def filter_spectrum(x, consts):
    dev_count = x.shape[0]
    return pl.pallas_call(
        functools.partial(filter_kernel, dev_count),
        in_specs=[ANY_SPEC] + [HBM_SPEC] * 4,
        out_specs=VMEM_SPEC,
        out_shape=jax.ShapeDtypeStruct((dev_count + 1, FINE, 2 * LANES), f32),
        scratch_shapes=[pltpu.VMEM((dev_count, FINE, LANES), bf16)]
        + const_scratch(consts)
        + [pltpu.VMEM((dev_count + 1, FINE, 2 * LANES), f32), pltpu.SemaphoreType.DMA((5,))],
        compiler_params=pltpu.CompilerParams(vmem_limit_bytes=BIG),
        name="filter_spectrum",
    )(x, *consts)


def convolve(half, early, late, spectrum, consts):
    dev_count = early.shape[0]
    return pl.pallas_call(
        functools.partial(conv_kernel, dev_count),
        in_specs=[pl.BlockSpec(memory_space=pltpu.SMEM)] + [ANY_SPEC] * 2 + [HBM_SPEC] * 5,
        out_specs=VMEM_SPEC,
        out_shape=jax.ShapeDtypeStruct((dev_count, FINE, LANES), bf16),
        scratch_shapes=[
            pltpu.VMEM(late.shape, bf16),
            pltpu.VMEM(late.shape, bf16),
            pltpu.VMEM((dev_count, FINE, LANES), f32),
            pltpu.VMEM(spectrum.shape, f32),
        ]
        + const_scratch(consts)
        + [pltpu.VMEM((dev_count + 1, FINE, 2 * LANES), f32), pltpu.SemaphoreType.DMA((7,))],
        compiler_params=pltpu.CompilerParams(vmem_limit_bytes=BIG),
        name="convolve",
    )(half, early, late, spectrum, *consts)


def finish(half, conv, early, late, skip_gain):
    rows, channels = early[0].shape
    tiles = channels // LANES

    def kernel(half_ref, c_any, ge_hbm, qe_hbm, gl_hbm, ql_hbm, skip_hbm, out_ref, c_ref, row_ref, skip_ref, sem, c_sem, s_sem):
        early_at = half_ref[0]
        cols = [pl.ds(i * LANES, LANES) for i in range(tiles)]
        skip_copy = start_all([(skip_hbm, skip_ref, s_sem)])[0]
        copies = []
        for i in range(tiles):
            pair = pl.ds(2 * i, 2)
            copies.append(
                start_all(
                    [(c_any.at[pair], c_ref.at[pair], c_sem.at[i])]
                    + [
                        (src.at[:, cols[i]], row_ref.at[i, j], sem.at[i, j])
                        for j, src in enumerate((ge_hbm, qe_hbm, gl_hbm, ql_hbm))
                    ]
                )
            )
        skip_copy.wait()
        for i in range(tiles):
            for copy in copies[i]:
                copy.wait()
            top, bot = unpack_pair(c_ref[2 * i].astype(f32), c_ref[2 * i + 1].astype(f32))
            skip = skip_ref[:, cols[i]]
            for at, j in ((early_at, 0), (1 - early_at, 2)):
                conv = jnp.where(at == 0, top, bot)
                value = row_ref[i, j + 1] * (conv + skip * row_ref[i, j])
                out_ref[pl.ds(pl.multiple_of(at * FINE, FINE), FINE), cols[i]] = value.astype(bf16)

    return pl.pallas_call(
        kernel,
        in_specs=[pl.BlockSpec(memory_space=pltpu.SMEM), ANY_SPEC] + [HBM_SPEC] * 5,
        out_specs=VMEM_SPEC,
        out_shape=jax.ShapeDtypeStruct((2 * rows, channels), bf16),
        scratch_shapes=[
            pltpu.VMEM(conv.shape, bf16),
            pltpu.VMEM((tiles, 4, rows, LANES), f32),
            pltpu.VMEM((1, channels), f32),
            pltpu.SemaphoreType.DMA((tiles, 4)),
            pltpu.SemaphoreType.DMA((tiles,)),
            pltpu.SemaphoreType.DMA,
        ],
        compiler_params=pltpu.CompilerParams(vmem_limit_bytes=BIG),
        name="finish",
    )(half, conv, *early, *late, skip_gain.reshape(1, channels))


def local(tokens, norm_gain, in_weight, short_weight, long_filter, skip_gain):
    dev_count = lax.axis_size("context")
    tensor_count = lax.axis_size("tensor")
    channels = in_weight.shape[2]
    packed = channels // dev_count == HALF
    consts = tables(dev_count)
    weight = jnp.transpose(in_weight, (1, 0, 2))
    exchange = functools.partial(
        lax.all_to_all, axis_name="context", split_axis=0, concat_axis=0, tiled=True
    )

    me = lax.axis_index("tensor").astype(jnp.int32)
    mid = tensor_count // 2
    half = (me // mid).reshape(1)
    place = (me % mid).reshape(1)

    def swap(x, bit):
        return lax.ppermute(x, "tensor", [(i, i ^ bit) for i in range(tensor_count)])

    def gathered(block):
        blocks = {0: block}
        bit = mid // 2
        while bit:
            for mask in list(blocks):
                blocks[mask | bit] = swap(blocks[mask], bit)
            bit //= 2
        return [blocks[mask] for mask in range(mid)]

    start = [(c * tensor_count - 1, c * tensor_count) for c in range(1, dev_count)]
    inner = [(c * tensor_count + mid - 1, c * tensor_count) for c in range(dev_count)]

    def halo(tail, first, second):
        total = jnp.zeros_like(tail)
        for j in range(mid):
            pairs = [(a, b + first + j) for a, b in start] + [(a, b + second + j) for a, b in inner]
            total = total + lax.ppermute(tail, ("context", "tensor"), pairs)
        return jnp.concatenate([jnp.zeros((PAD - TAIL, tail.shape[1]), bf16), total], axis=0)

    normed, tail = norm_rows(tokens, norm_gain)
    normed, early_halo = lax.optimization_barrier((normed, halo(tail, 0, mid)))
    crossed = swap(normed, mid)
    early_blocks = gathered(normed)
    early_halo, late_halo = lax.optimization_barrier((early_halo, halo(tail, mid, 0)))

    if packed:
        early_gated, packs = project(
            (1, 2), place, early_halo, early_blocks, weight, short_weight, COST[0], long_filter
        )
    else:
        early_gated, _ = project((1, 2), place, early_halo, early_blocks, weight, short_weight, COST[0])
        packs = [pack_any(rows, dev_count) for rows in (early_gated, long_filter)]
        packs = jnp.concatenate(packs, axis=1)
    early_sent = exchange(packs)
    crossed, _ = lax.optimization_barrier((crossed, packs))
    late_blocks = gathered(crossed)
    late_gated, packs = project((1, 2), place, late_halo, late_blocks, weight, short_weight, COST[1])
    late_sent = exchange(packs if packed else pack_any(late_gated, dev_count))
    spectrum = filter_spectrum(early_sent, consts)
    (late_query,) = project((0,), place, late_halo, late_blocks, weight, short_weight, COST[2])
    (early_query,) = project((0,), place, early_halo, early_blocks, weight, short_weight, COST[2])
    conv = exchange(convolve(half, early_sent, late_sent, spectrum, consts))
    early, late = (early_gated, early_query), (late_gated, late_query)
    if packed:
        return finish(half, conv, early, late, skip_gain)
    each = channels // dev_count
    conv = conv.reshape(dev_count, FINE, 2, HALF)[..., :each]
    conv = jnp.transpose(conv, (2, 1, 0, 3)).reshape(2 * FINE, channels).astype(f32)
    first, second = (
        [jnp.where(half == swapped, a, b) for a, b in zip(early, late)] for swapped in (0, 1)
    )
    gated, query = (jnp.concatenate([a, b], axis=0) for a, b in zip(first, second))
    return (query * (conv + skip_gain * gated)).astype(bf16)


def solution(mesh):
    return jax.shard_map(
        local,
        mesh=mesh,
        in_specs=(
            P(("context", "tensor"), None),
            P(),
            P(None, None, "tensor"),
            P(None, None, "tensor"),
            P("context", "tensor"),
            P("tensor"),
        ),
        out_specs=P("context", "tensor"),
        check_vma=False,
    )
```

```python
import functools
import math

import jax
import jax.numpy as jnp
import numpy as np
from jax import lax
from jax.experimental import pallas as pl
from jax.experimental.pallas import tpu as pltpu
from jax.sharding import PartitionSpec as P

eps = 1e-06

FINE = 256
HALF = 64
LANES = 2 * HALF
TAIL = 8
PAD = 16
BIG = 60 * 1024 * 1024
COST = (10**8, 10**8, 10**8)

VMEM_SPEC = pl.BlockSpec(memory_space=pltpu.VMEM)
HBM_SPEC = pl.BlockSpec(memory_space=pltpu.HBM)
ANY_SPEC = pl.BlockSpec(memory_space=pl.ANY)

f32 = jnp.float32
bf16 = jnp.bfloat16


def lane_mask():
    return lax.broadcasted_iota(jnp.int32, (1, LANES), 1) < HALF


def pack_pair(tile):
    low = lane_mask()
    rows = tile.shape[0] // 2
    top, bot = tile[:rows], tile[rows:]
    return (
        jnp.where(low, top, pltpu.roll(bot, HALF, 1)),
        jnp.where(low, pltpu.roll(top, HALF, 1), bot),
    )


def unpack_pair(first, second):
    low = lane_mask()
    return (
        jnp.where(low, first, pltpu.roll(second, HALF, 1)),
        jnp.where(low, pltpu.roll(first, HALF, 1), second),
    )


def start_all(copies):
    copies = [pltpu.make_async_copy(*copy) for copy in copies]
    for copy in copies:
        copy.start()
    return copies


def pack_any(rows, dev_count):
    length, channels = rows.shape
    each = channels // dev_count
    blocks = rows.astype(bf16).reshape(2, length // 2, dev_count, each)
    blocks = jnp.transpose(blocks, (2, 1, 0, 3))
    blocks = jnp.pad(blocks, ((0, 0), (0, 0), (0, 0), (0, HALF - each)))
    return blocks.reshape(dev_count, length // 2, LANES)


def norm_rows(tokens, gain):
    rows, width = tokens.shape
    step = min(32, rows)

    def kernel(tok_hbm, gain_hbm, out_ref, tail_ref, tok_ref, gain_ref, sem):
        parts = [pl.ds(i * step, step) for i in range(rows // step)]
        copies = start_all(
            [(gain_hbm, gain_ref, sem.at[len(parts)])]
            + [(tok_hbm.at[part], tok_ref.at[part], sem.at[i]) for i, part in enumerate(parts)]
        )
        copies[0].wait()
        for part, copy in zip(parts, copies[1:]):
            copy.wait()
            values = tok_ref[part, :].astype(f32)
            inv_rms = lax.rsqrt(jnp.mean(values * values, axis=1, keepdims=True) + eps)
            normed = (values * inv_rms * gain_ref[...]).astype(bf16)
            out_ref[part, :] = normed
            tail_ref[...] = normed[step - TAIL :]

    return pl.pallas_call(
        kernel,
        in_specs=[HBM_SPEC] * 2,
        out_specs=[VMEM_SPEC] * 2,
        out_shape=[jax.ShapeDtypeStruct((rows, width), bf16), jax.ShapeDtypeStruct((TAIL, width), bf16)],
        scratch_shapes=[
            pltpu.VMEM((rows, width), bf16),
            pltpu.VMEM((1, width), f32),
            pltpu.SemaphoreType.DMA((rows // step + 1,)),
        ],
        compiler_params=pltpu.CompilerParams(vmem_limit_bytes=BIG),
        name="norm_rows",
    )(tokens, gain.reshape(1, width))


def pack_into(p_ref, at, rows_ref, first, length):
    rows = pl.ds(at, length // 2)
    for i in range(p_ref.shape[0] // 2):
        one, two = pack_pair(rows_ref[first : first + length, i * LANES : (i + 1) * LANES])
        p_ref[2 * i, rows, :] = one.astype(bf16)
        p_ref[2 * i + 1, rows, :] = two.astype(bf16)


def project_kernel(count, parts, splits, ext_rows, with_filter, me_ref, *refs):
    blocks, refs = refs[:count], refs[count:]
    w_hbm, tap_hbm = refs[:2]
    extra, outs = refs[2 : 2 + bool(ext_rows) + with_filter], refs[2 + bool(ext_rows) + with_filter : -8]
    w_ref, tap_ref, x_ref, rows_ref, filt_ref, sem, w_sem, tap_sem = refs[-8:]
    each = blocks[0].shape[0]
    length = each * count
    end = PAD + length
    width = x_ref.shape[1]
    depth = width // splits

    sources = [(tap_hbm, tap_ref, tap_sem)]
    for mask, block in enumerate(blocks):
        first = pl.multiple_of(PAD + (me_ref[0] ^ mask) * each, 16)
        sources.append((block, x_ref.at[pl.ds(first, each)], sem.at[mask]))
    if ext_rows:
        sources.append((extra[0].at[pl.ds(0, PAD)], x_ref.at[pl.ds(0, PAD)], sem.at[count]))
    else:
        x_ref[:PAD] = jnp.zeros((PAD, width), bf16)
    if ext_rows > PAD:
        rest = ext_rows - PAD
        sources.append((extra[0].at[pl.ds(PAD, rest)], x_ref.at[pl.ds(end, rest)], sem.at[count + 1]))
    waits = start_all(sources)
    loads = {}
    for at, s in enumerate(parts):
        for i in range(splits):
            chunk = pl.ds(i * depth, depth)
            loads[s, i] = start_all([(w_hbm.at[s, chunk], w_ref.at[at, chunk], w_sem.at[at, i])])[0]
    if with_filter:
        filt_load = start_all([(extra[-1], filt_ref, sem.at[count + 2])])[0]
    for wait in waits:
        wait.wait()

    def mixed(s):
        at = parts.index(s)
        total = None
        for i in range(splits):
            loads[s, i].wait()
            chunk = slice(i * depth, (i + 1) * depth)
            term = jnp.dot(x_ref[:, chunk], w_ref[at, chunk], preferred_element_type=f32)
            total = term if total is None else total + term
        rows_ref[...] = total
        spans = [(PAD, length)]
        if ext_rows > PAD:
            spans.append((end + PAD, PAD))
        results = []
        for first, size in spans:
            total = tap_ref[0, s : s + 1] * rows_ref[first : first + size]
            for lag in (1, 2):
                total += tap_ref[lag, s : s + 1] * rows_ref[first - lag : first - lag + size]
            results.append(total)
        return results

    if 1 in parts:
        g_ref, p_ref = outs[:2]
        spans = [slice(0, length), slice(length, length + PAD)]
        for span, key in zip(spans, mixed(1)):
            g_ref[span, :] = key
        for span, value in zip(spans, mixed(2)):
            g_ref[span, :] *= value
        pack_into(p_ref, 0, g_ref, 0, length)
        if ext_rows > PAD:
            pack_into(p_ref, length // 2, g_ref, length, PAD)
    if 0 in parts:
        outs[-1][...] = mixed(0)[0]
    if with_filter:
        filt_load.wait()
        pack_into(p_ref, length // 2, filt_ref, 0, filt_ref.shape[0])


def project(parts, me, blocks, weight, taps, cost, ext=None, filt=None):
    _, width, channels = weight.shape
    length = blocks[0].shape[0] * len(blocks)
    splits = 2
    ext_rows = 0 if ext is None else ext.shape[0]
    more = PAD if ext_rows > PAD else 0
    shapes = []
    if 1 in parts:
        rows = (length + more) // 2 + (0 if filt is None else filt.shape[0] // 2)
        shapes += [
            jax.ShapeDtypeStruct((length + more, channels), f32),
            jax.ShapeDtypeStruct((max(channels // HALF, 2), rows, LANES), bf16),
        ]
    if 0 in parts:
        shapes.append(jax.ShapeDtypeStruct((length, channels), f32))
    extra = [x for x in (ext, filt) if x is not None]
    rows = PAD + length + (2 * PAD if more else 0)
    return pl.pallas_call(
        functools.partial(project_kernel, len(blocks), parts, splits, ext_rows, filt is not None),
        in_specs=[pl.BlockSpec(memory_space=pltpu.SMEM)] + [ANY_SPEC] * (len(blocks) + 2 + len(extra)),
        out_specs=[VMEM_SPEC] * len(shapes),
        out_shape=shapes,
        scratch_shapes=[
            pltpu.VMEM((len(parts), width, channels), bf16),
            pltpu.VMEM(taps.shape, f32),
            pltpu.VMEM((rows, width), bf16),
            pltpu.VMEM((rows, channels), f32),
            pltpu.VMEM((8, LANES) if filt is None else filt.shape, f32),
            pltpu.SemaphoreType.DMA((len(blocks) + 3,)),
            pltpu.SemaphoreType.DMA((len(parts), splits)),
            pltpu.SemaphoreType.DMA,
        ],
        compiler_params=pltpu.CompilerParams(vmem_limit_bytes=BIG),
        cost_estimate=pl.CostEstimate(flops=cost, bytes_accessed=10**5, transcendentals=0),
        name="project",
    )(me, *blocks, weight, taps, *extra)


def coarse_forward(dev_count, x_ref, lane_ref, e_ref, step=16):
    count = dev_count
    half = count // 2
    low = lane_mask()
    sgn = jnp.where(low, 1.0, -1.0).astype(f32)

    def body(i, carry):
        rows = pl.ds(pl.multiple_of(i * step, step), step)
        x = [x_ref[s, rows, :].astype(f32) for s in range(count)]
        plus = [x[s] + x[count - s] for s in range(1, half)]
        minus = [x[s] - x[count - s] for s in range(1, half)]
        for k in range(count + 1):
            even = k % 2 == 0
            re = x[0]
            im = None
            mid = round(math.cos(math.pi * half * k / count))
            if mid:
                re = re + x[half] if mid > 0 else re - x[half]
            mid = round(math.sin(math.pi * half * k / count))
            if mid:
                im = -x[half] if mid > 0 else x[half]
            for s in range(1, half):
                c, d = math.cos(math.pi * s * k / count), math.sin(math.pi * s * k / count)
                if abs(c) > 1e-9:
                    re = re + c * (plus if even else minus)[s - 1]
                if abs(d) > 1e-9:
                    term = (-d) * (minus if even else plus)[s - 1]
                    im = term if im is None else im + term
            c, d = lane_ref[k, 0:1, :], lane_ref[k, 1:2, :]
            if im is None:
                re, im = re * c, re * (-d)
            else:
                re, im = re * c + im * d, im * c - re * d
            e_ref[k, rows, :LANES] = pltpu.roll(re, HALF, 1) + sgn * re
            e_ref[k, rows, LANES:] = sgn * pltpu.roll(im, HALF, 1) + im
        return carry

    lax.fori_loop(0, FINE // step, body, 0)


def coarse_inverse(dev_count, g_ref, y_ref, step=16):
    count = dev_count
    half = count // 2

    def body(i, carry):
        rows = pl.ds(pl.multiple_of(i * step, step), step)
        acc = {}

        def add(name, s, term):
            acc[name, s] = term if (name, s) not in acc else acc[name, s] + term

        for k in range(count + 1):
            even = k % 2 == 0
            re, im = g_ref[k, rows, :LANES], g_ref[k, rows, LANES:]
            add("first", 0, re)
            mid = round(math.cos(math.pi * half * k / count))
            if mid:
                add("mid", 0, re if mid > 0 else -re)
            mid = round(math.sin(math.pi * half * k / count))
            if mid:
                add("mid", 0, -im if mid > 0 else im)
            for s in range(1, half):
                c, d = math.cos(math.pi * s * k / count), math.sin(math.pi * s * k / count)
                if abs(c) > 1e-9:
                    add("a" if even else "b", s, c * re)
                if abs(d) > 1e-9:
                    add("b" if even else "a", -s, (-d) * im)
        y_ref[0, rows, :] = acc["first", 0].astype(bf16)
        y_ref[half, rows, :] = acc["mid", 0].astype(bf16)
        zero = jnp.zeros((step, LANES), f32)
        for s in range(1, half):
            same = acc.get(("a", s), zero)
            flip = acc.get(("b", s), zero)
            same_sin = acc.get(("a", -s), zero)
            flip_sin = acc.get(("b", -s), zero)
            total, diff = same + same_sin, flip + flip_sin
            y_ref[s, rows, :] = (total + diff).astype(bf16)
            y_ref[count - s, rows, :] = (total - diff).astype(bf16)
        return carry

    lax.fori_loop(0, FINE // step, body, 0)


def fine_forward(e, tr, ti, table):
    re, im = e[:, :LANES], e[:, LANES:]
    turned = jnp.concatenate([re * tr - im * ti, re * ti + im * tr], axis=1).astype(bf16)
    both = jnp.dot(table, turned, preferred_element_type=f32)
    return (
        both[:FINE, :LANES] - both[FINE:, LANES:],
        both[:FINE, LANES:] + both[FINE:, :LANES],
    )


def next_turn(turn_ref, step_ref):
    tr, ti = turn_ref[:, :LANES], turn_ref[:, LANES:]
    sr, si = step_ref[:, :LANES], step_ref[:, LANES:]
    turn_ref[:, :LANES] = tr * sr - ti * si
    turn_ref[:, LANES:] = tr * si + ti * sr


def filter_kernel(dev_count, x_any, *refs):
    const_hbm, h_ref = refs[:4], refs[4]
    x_ref, first_ref, step_ref, lane_ref, table_ref, e_ref, sem = refs[5:]
    turn_ref = first_ref
    rows = pl.ds(x_any.shape[1] - FINE, FINE)
    pairs = [(x_any.at[:, rows], x_ref)] + list(zip(const_hbm, (first_ref, step_ref, lane_ref, table_ref)))
    for copy in start_all((*pair, sem.at[i]) for i, pair in enumerate(pairs)):
        copy.wait()
    coarse_forward(dev_count, x_ref, lane_ref, e_ref)
    points = 4 * dev_count * FINE

    def body(k, carry):
        re, im = fine_forward(e_ref[k], turn_ref[:, :LANES], turn_ref[:, LANES:], table_ref[...])
        scale = jnp.where((k == 0) | (k == dev_count), 1.0 / points, 2.0 / points).astype(f32)
        h_ref[k, :, :LANES] = re * scale
        h_ref[k, :, LANES:] = im * scale
        next_turn(turn_ref, step_ref)
        return carry

    lax.fori_loop(0, dev_count + 1, body, 0, unroll=dev_count <= 8)


def merge_halves(dev_count, late_first, early_ref, late_ref, x_ref):
    pick = late_first == 1
    low = lane_mask()
    size = FINE // 2
    for s in range(dev_count):
        early, late = early_ref[s].astype(f32), late_ref[s].astype(f32)
        fixed = jnp.where(low, late[size:], early[: PAD // 2])
        early, late = jnp.concatenate([fixed, early[PAD // 2 :]], axis=0), late[:size]
        first, second = jnp.where(pick, late, early), jnp.where(pick, early, late)
        top, bot = pack_pair(jnp.concatenate([first, second], axis=0))
        x_ref[s, :size] = top
        x_ref[s, size:] = bot


def conv_kernel(dev_count, half_ref, early_any, late_any, h_hbm, *refs):
    const_hbm, y_ref = refs[:4], refs[4]
    early_ref, late_ref, x_ref, h_ref, first_ref, step_ref, lane_ref, table_ref, e_ref, sem = refs[5:]
    turn_ref = first_ref
    pairs = [(early_any.at[:, pl.ds(0, FINE // 2)], early_ref), (late_any, late_ref)]
    pairs += list(zip(const_hbm, (first_ref, step_ref, lane_ref, table_ref))) + [(h_hbm, h_ref)]
    copies = start_all((*pair, sem.at[i]) for i, pair in enumerate(pairs))
    for copy in copies[:-1]:
        copy.wait()
    merge_halves(dev_count, half_ref[0], early_ref, late_ref, x_ref)
    coarse_forward(dev_count, x_ref, lane_ref, e_ref)
    copies[-1].wait()
    sgn = jnp.where(lane_mask(), 1.0, -1.0).astype(f32)

    def body(k, carry):
        tr, ti = turn_ref[:, :LANES], turn_ref[:, LANES:]
        re, im = fine_forward(e_ref[k], tr, ti, table_ref[...])
        hr, hi = h_ref[k, :, :LANES], h_ref[k, :, LANES:]
        prod = jnp.concatenate([re * hr - im * hi, re * hi + im * hr], axis=1).astype(bf16)
        both = jnp.dot(table_ref[...], prod, preferred_element_type=f32)
        re = both[:FINE, :LANES] + both[FINE:, LANES:]
        im = both[:FINE, LANES:] - both[FINE:, :LANES]
        re, im = re * tr + im * ti, (im * tr - re * ti) * sgn
        re, im = pltpu.roll(re, HALF, 1) + sgn * re, pltpu.roll(im, HALF, 1) + sgn * im
        c, d = lane_ref[k, 0:1, :], lane_ref[k, 1:2, :]
        e_ref[k, :, :LANES] = re * c - im * d
        e_ref[k, :, LANES:] = re * d + im * c
        next_turn(turn_ref, step_ref)
        return carry

    lax.fori_loop(0, dev_count + 1, body, 0, unroll=dev_count <= 8)
    coarse_inverse(dev_count, e_ref, y_ref)


def tables(dev_count):
    points = 4 * dev_count * FINE
    fine = np.arange(FINE)
    first = np.exp(-2j * np.pi * fine * (2 * dev_count) / points)[:, None] * np.ones(HALF)
    ones = np.ones((FINE, HALF))
    step = np.exp(-2j * np.pi * fine / points)[:, None] * ones
    first = np.concatenate([ones, first.real, 0 * ones, first.imag], axis=1)
    step = np.concatenate([step.real, step.real, step.imag, -step.imag], axis=1)
    turn = 2 * np.pi * np.arange(dev_count + 1)[:, None] * np.ones(HALF) / (4 * dev_count)
    lane = np.stack(
        [
            np.concatenate([np.ones_like(turn), np.cos(turn)], axis=1),
            np.concatenate([np.zeros_like(turn), np.sin(turn)], axis=1),
        ],
        axis=1,
    )
    angle = -2 * np.pi * (fine[:, None] * fine[None, :] % FINE) / FINE
    table = np.concatenate([np.cos(angle), np.sin(angle)], axis=0)
    return (
        jnp.asarray(first, f32),
        jnp.asarray(step, f32),
        jnp.asarray(lane, f32),
        jnp.asarray(table, bf16),
    )


def const_scratch(consts):
    return [pltpu.VMEM(const.shape, const.dtype) for const in consts]


def filter_spectrum(x, consts):
    dev_count = x.shape[0]
    return pl.pallas_call(
        functools.partial(filter_kernel, dev_count),
        in_specs=[ANY_SPEC] + [HBM_SPEC] * 4,
        out_specs=VMEM_SPEC,
        out_shape=jax.ShapeDtypeStruct((dev_count + 1, FINE, 2 * LANES), f32),
        scratch_shapes=[pltpu.VMEM((dev_count, FINE, LANES), bf16)]
        + const_scratch(consts)
        + [pltpu.VMEM((dev_count + 1, FINE, 2 * LANES), f32), pltpu.SemaphoreType.DMA((5,))],
        compiler_params=pltpu.CompilerParams(vmem_limit_bytes=BIG),
        name="filter_spectrum",
    )(x, *consts)


def convolve(half, early, late, spectrum, consts):
    dev_count = early.shape[0]
    return pl.pallas_call(
        functools.partial(conv_kernel, dev_count),
        in_specs=[pl.BlockSpec(memory_space=pltpu.SMEM)] + [ANY_SPEC] * 2 + [HBM_SPEC] * 5,
        out_specs=VMEM_SPEC,
        out_shape=jax.ShapeDtypeStruct((dev_count, FINE, LANES), bf16),
        scratch_shapes=[
            pltpu.VMEM((dev_count, FINE // 2, LANES), bf16),
            pltpu.VMEM(late.shape, bf16),
            pltpu.VMEM((dev_count, FINE, LANES), f32),
            pltpu.VMEM(spectrum.shape, f32),
        ]
        + const_scratch(consts)
        + [pltpu.VMEM((dev_count + 1, FINE, 2 * LANES), f32), pltpu.SemaphoreType.DMA((7,))],
        compiler_params=pltpu.CompilerParams(vmem_limit_bytes=BIG),
        name="convolve",
    )(half, early, late, spectrum, *consts)


def finish(half, conv, early, late, skip_gain):
    rows, channels = early[0].shape
    tiles = channels // LANES

    def kernel(half_ref, c_any, ge_hbm, qe_hbm, gl_hbm, ql_hbm, skip_hbm, out_ref, c_ref, row_ref, skip_ref, sem, c_sem, s_sem):
        early_at = half_ref[0]
        cols = [pl.ds(i * LANES, LANES) for i in range(tiles)]
        skip_copy = start_all([(skip_hbm, skip_ref, s_sem)])[0]
        copies = []
        for i in range(tiles):
            pair = pl.ds(2 * i, 2)
            copies.append(
                start_all(
                    [(c_any.at[pair], c_ref.at[pair], c_sem.at[i])]
                    + [
                        (src.at[:, cols[i]], row_ref.at[i, j, pl.ds(0, src.shape[0])], sem.at[i, j])
                        for j, src in enumerate((ge_hbm, qe_hbm, gl_hbm, ql_hbm))
                    ]
                )
            )
        skip_copy.wait()
        for i in range(tiles):
            for copy in copies[i]:
                copy.wait()
            top, bot = unpack_pair(c_ref[2 * i].astype(f32), c_ref[2 * i + 1].astype(f32))
            skip = skip_ref[:, cols[i]]
            row_ref[i, 0, :PAD] = row_ref[i, 2, rows:]
            for at, j in ((early_at, 0), (1 - early_at, 2)):
                conv = jnp.where(at == 0, top, bot)
                value = row_ref[i, j + 1, :rows] * (conv + skip * row_ref[i, j, :rows])
                out_ref[pl.ds(pl.multiple_of(at * FINE, FINE), FINE), cols[i]] = value.astype(bf16)

    return pl.pallas_call(
        kernel,
        in_specs=[pl.BlockSpec(memory_space=pltpu.SMEM), ANY_SPEC] + [HBM_SPEC] * 5,
        out_specs=VMEM_SPEC,
        out_shape=jax.ShapeDtypeStruct((2 * rows, channels), bf16),
        scratch_shapes=[
            pltpu.VMEM(conv.shape, bf16),
            pltpu.VMEM((tiles, 4, rows + PAD, LANES), f32),
            pltpu.VMEM((1, channels), f32),
            pltpu.SemaphoreType.DMA((tiles, 4)),
            pltpu.SemaphoreType.DMA((tiles,)),
            pltpu.SemaphoreType.DMA,
        ],
        compiler_params=pltpu.CompilerParams(vmem_limit_bytes=BIG),
        name="finish",
    )(half, conv, *early, *late, skip_gain.reshape(1, channels))


def local(tokens, norm_gain, in_weight, short_weight, long_filter, skip_gain):
    dev_count = lax.axis_size("context")
    tensor_count = lax.axis_size("tensor")
    channels = in_weight.shape[2]
    packed = channels // dev_count == HALF
    consts = tables(dev_count)
    weight = jnp.transpose(in_weight, (1, 0, 2))
    exchange = functools.partial(
        lax.all_to_all, axis_name="context", split_axis=0, concat_axis=0, tiled=True
    )

    me = lax.axis_index("tensor").astype(jnp.int32)
    mid = tensor_count // 2
    half = (me // mid).reshape(1)
    place = (me % mid).reshape(1)

    def swap(x, bit):
        return lax.ppermute(x, "tensor", [(i, i ^ bit) for i in range(tensor_count)])

    def gathered(block):
        blocks = {0: block}
        bit = mid // 2
        while bit:
            for mask in list(blocks):
                blocks[mask | bit] = swap(blocks[mask], bit)
            bit //= 2
        return [blocks[mask] for mask in range(mid)]

    normed, tail = norm_rows(tokens, norm_gain)
    crossed = swap(normed, mid)
    early_blocks = gathered(normed)

    late_halo = jnp.zeros_like(tail)
    for j in range(mid):
        pairs = [(c * tensor_count - 1, c * tensor_count + mid + j) for c in range(1, dev_count)]
        pairs += [(c * tensor_count + mid - 1, c * tensor_count + j) for c in range(dev_count)]
        late_halo = late_halo + lax.ppermute(tail, ("context", "tensor"), pairs)
    head = sum(jnp.where(place == mask, block[:PAD], 0) for mask, block in enumerate(early_blocks))
    early_blocks, late_halo = lax.optimization_barrier((early_blocks, late_halo))
    early_halo = swap(late_halo, mid)

    packs = None
    if packed:
        early_gated, packs = project(
            (1, 2), place, early_blocks, weight, short_weight, COST[0], filt=long_filter
        )
    else:
        early_gated, _ = project((1, 2), place, early_blocks, weight, short_weight, COST[0])
        packs = [pack_any(rows, dev_count) for rows in (early_gated, long_filter)]
        packs = jnp.concatenate(packs, axis=1)
    early_sent = exchange(packs)
    crossed, _ = lax.optimization_barrier((crossed, packs))
    late_blocks = gathered(crossed)
    gap = jnp.zeros((PAD - TAIL, tail.shape[1]), bf16)
    late_ext = jnp.concatenate([gap, late_halo, gap, early_halo, head], axis=0)
    late_gated, packs = project((1, 2), place, late_blocks, weight, short_weight, COST[1], ext=late_ext)
    if not packed:
        rows = late_gated.shape[0] - PAD
        packs = [pack_any(late_gated[:rows], dev_count), pack_any(late_gated[rows:], dev_count)]
        packs = jnp.concatenate(packs, axis=1)
    late_sent = exchange(packs)
    spectrum = filter_spectrum(early_sent, consts)
    early_ext = jnp.concatenate([gap, early_halo], axis=0)
    (early_query,) = project((0,), place, early_blocks, weight, short_weight, COST[2], ext=early_ext)
    (late_query,) = project((0,), place, late_blocks, weight, short_weight, COST[2], ext=late_ext[:PAD])
    conv = exchange(convolve(half, early_sent, late_sent, spectrum, consts))
    early, late = (early_gated, early_query), (late_gated, late_query)
    if packed:
        return finish(half, conv, early, late, skip_gain)
    early_gated = jnp.concatenate([late_gated[rows:], early_gated[PAD:]], axis=0)
    early, late = (early_gated, early_query), (late_gated[:rows], late_query)
    each = channels // dev_count
    conv = conv.reshape(dev_count, FINE, 2, HALF)[..., :each]
    conv = jnp.transpose(conv, (2, 1, 0, 3)).reshape(2 * FINE, channels).astype(f32)
    first, second = (
        [jnp.where(half == swapped, a, b) for a, b in zip(early, late)] for swapped in (0, 1)
    )
    gated, query = (jnp.concatenate([a, b], axis=0) for a, b in zip(first, second))
    return (query * (conv + skip_gain * gated)).astype(bf16)


def solution(mesh):
    return jax.shard_map(
        local,
        mesh=mesh,
        in_specs=(
            P(("context", "tensor"), None),
            P(),
            P(None, None, "tensor"),
            P(None, None, "tensor"),
            P("context", "tensor"),
            P("tensor"),
        ),
        out_specs=P("context", "tensor"),
        check_vma=False,
    )
```

```python
import functools
import math

import jax
import jax.numpy as jnp
import numpy as np
from jax import lax
from jax.experimental import pallas as pl
from jax.experimental.pallas import tpu as pltpu
from jax.sharding import PartitionSpec as P

eps = 1e-06

FINE = 256
HALF = 64
LANES = 2 * HALF
TAIL = 8
PAD = 16
BIG = 60 * 1024 * 1024
COST = (10**8, 10**8, 10**8)

VMEM_SPEC = pl.BlockSpec(memory_space=pltpu.VMEM)
HBM_SPEC = pl.BlockSpec(memory_space=pltpu.HBM)
ANY_SPEC = pl.BlockSpec(memory_space=pl.ANY)

f32 = jnp.float32
bf16 = jnp.bfloat16


def lane_mask():
    return lax.broadcasted_iota(jnp.int32, (1, LANES), 1) < HALF


def pack_pair(tile):
    low = lane_mask()
    rows = tile.shape[0] // 2
    top, bot = tile[:rows], tile[rows:]
    return (
        jnp.where(low, top, pltpu.roll(bot, HALF, 1)),
        jnp.where(low, pltpu.roll(top, HALF, 1), bot),
    )


def unpack_pair(first, second):
    low = lane_mask()
    return (
        jnp.where(low, first, pltpu.roll(second, HALF, 1)),
        jnp.where(low, pltpu.roll(first, HALF, 1), second),
    )


def start_all(copies):
    copies = [pltpu.make_async_copy(*copy) for copy in copies]
    for copy in copies:
        copy.start()
    return copies


def pack_any(rows, dev_count):
    length, channels = rows.shape
    each = channels // dev_count
    blocks = rows.astype(bf16).reshape(2, length // 2, dev_count, each)
    blocks = jnp.transpose(blocks, (2, 1, 0, 3))
    blocks = jnp.pad(blocks, ((0, 0), (0, 0), (0, 0), (0, HALF - each)))
    return blocks.reshape(dev_count, length // 2, LANES)


def norm_rows(tokens, gain):
    rows, width = tokens.shape
    step = min(32, rows)

    def kernel(tok_hbm, gain_hbm, out_any, tail_any, tok_ref, gain_ref, out_ref, sem, out_sem):
        parts = [pl.ds(i * step, step) for i in range(rows // step)]
        copies = start_all(
            [(gain_hbm, gain_ref, sem.at[len(parts)])]
            + [(tok_hbm.at[part], tok_ref.at[part], sem.at[i]) for i, part in enumerate(parts)]
        )
        copies[0].wait()
        sends = []
        for i, part in enumerate(parts):
            copies[1 + i].wait()
            values = tok_ref[part, :].astype(f32)
            inv_rms = lax.rsqrt(jnp.mean(values * values, axis=1, keepdims=True) + eps)
            out_ref[part, :] = (values * inv_rms * gain_ref[...]).astype(bf16)
            sends += start_all([(out_ref.at[part], out_any.at[part], out_sem.at[i])])
        sends += start_all([(out_ref.at[pl.ds(rows - TAIL, TAIL)], tail_any, out_sem.at[len(parts)])])
        for send in sends:
            send.wait()

    return pl.pallas_call(
        kernel,
        in_specs=[HBM_SPEC] * 2,
        out_specs=[ANY_SPEC] * 2,
        out_shape=[jax.ShapeDtypeStruct((rows, width), bf16), jax.ShapeDtypeStruct((TAIL, width), bf16)],
        scratch_shapes=[
            pltpu.VMEM((rows, width), bf16),
            pltpu.VMEM((1, width), f32),
            pltpu.VMEM((rows, width), bf16),
            pltpu.SemaphoreType.DMA((rows // step + 1,)),
            pltpu.SemaphoreType.DMA((rows // step + 1,)),
        ],
        compiler_params=pltpu.CompilerParams(vmem_limit_bytes=BIG),
        name="norm_rows",
    )(tokens, gain.reshape(1, width))


def pack_into(p_ref, at, rows_ref, first, length):
    rows = pl.ds(at, length // 2)
    for i in range(p_ref.shape[0] // 2):
        one, two = pack_pair(rows_ref[first : first + length, i * LANES : (i + 1) * LANES])
        p_ref[2 * i, rows, :] = one.astype(bf16)
        p_ref[2 * i + 1, rows, :] = two.astype(bf16)


def project_kernel(count, parts, splits, ext_rows, with_filter, me_ref, *refs):
    blocks, refs = refs[:count], refs[count:]
    w_hbm, tap_hbm = refs[:2]
    extra, refs = refs[2 : 2 + bool(ext_rows) + with_filter], refs[2 + bool(ext_rows) + with_filter :]
    number = 2 * (1 in parts) + (0 in parts)
    out_any, outs, refs = refs[:number], refs[number : 2 * number], refs[2 * number :]
    w_ref, tap_ref, x_ref, rows_ref, filt_ref, sem, w_sem, tap_sem, out_sem = refs

    def send(i):
        return start_all([(outs[i], out_any[i], out_sem.at[i])])

    each = blocks[0].shape[0]
    length = each * count
    end = PAD + length
    width = x_ref.shape[1]
    depth = width // splits

    sources = [(tap_hbm, tap_ref, tap_sem)]
    for mask, block in enumerate(blocks):
        first = pl.multiple_of(PAD + (me_ref[0] ^ mask) * each, 16)
        sources.append((block, x_ref.at[pl.ds(first, each)], sem.at[mask]))
    if ext_rows:
        sources.append((extra[0].at[pl.ds(0, PAD)], x_ref.at[pl.ds(0, PAD)], sem.at[count]))
    else:
        x_ref[:PAD] = jnp.zeros((PAD, width), bf16)
    if ext_rows > PAD:
        rest = ext_rows - PAD
        sources.append((extra[0].at[pl.ds(PAD, rest)], x_ref.at[pl.ds(end, rest)], sem.at[count + 1]))
    waits = start_all(sources)
    loads = {}
    for at, s in enumerate(parts):
        for i in range(splits):
            chunk = pl.ds(i * depth, depth)
            loads[s, i] = start_all([(w_hbm.at[s, chunk], w_ref.at[at, chunk], w_sem.at[at, i])])[0]
    if with_filter:
        filt_load = start_all([(extra[-1], filt_ref, sem.at[count + 2])])[0]
    for wait in waits:
        wait.wait()

    def mixed(s):
        at = parts.index(s)
        total = None
        for i in range(splits):
            loads[s, i].wait()
            chunk = slice(i * depth, (i + 1) * depth)
            term = jnp.dot(x_ref[:, chunk], w_ref[at, chunk], preferred_element_type=f32)
            total = term if total is None else total + term
        rows_ref[...] = total
        spans = [(PAD, length)]
        if ext_rows > PAD:
            spans.append((end + PAD, PAD))
        results = []
        for first, size in spans:
            total = tap_ref[0, s : s + 1] * rows_ref[first : first + size]
            for lag in (1, 2):
                total += tap_ref[lag, s : s + 1] * rows_ref[first - lag : first - lag + size]
            results.append(total)
        return results

    if 1 in parts:
        g_ref, p_ref = outs[:2]
        spans = [slice(0, length), slice(length, length + PAD)]
        for span, key in zip(spans, mixed(1)):
            g_ref[span, :] = key
        for span, value in zip(spans, mixed(2)):
            g_ref[span, :] *= value
        sends = send(0)
        pack_into(p_ref, 0, g_ref, 0, length)
        if ext_rows > PAD:
            pack_into(p_ref, length // 2, g_ref, length, PAD)
        if with_filter:
            filt_load.wait()
            pack_into(p_ref, length // 2, filt_ref, 0, filt_ref.shape[0])
        sends += send(1)
    if 0 in parts:
        outs[-1][...] = mixed(0)[0]
        sends = (sends if 1 in parts else []) + send(number - 1)
    for copy in sends:
        copy.wait()


def project(parts, me, blocks, weight, taps, cost, ext=None, filt=None):
    _, width, channels = weight.shape
    length = blocks[0].shape[0] * len(blocks)
    splits = 2
    ext_rows = 0 if ext is None else ext.shape[0]
    more = PAD if ext_rows > PAD else 0
    shapes = []
    if 1 in parts:
        rows = (length + more) // 2 + (0 if filt is None else filt.shape[0] // 2)
        shapes += [
            jax.ShapeDtypeStruct((length + more, channels), f32),
            jax.ShapeDtypeStruct((max(channels // HALF, 2), rows, LANES), bf16),
        ]
    if 0 in parts:
        shapes.append(jax.ShapeDtypeStruct((length, channels), f32))
    extra = [x for x in (ext, filt) if x is not None]
    rows = PAD + length + (2 * PAD if more else 0)
    return pl.pallas_call(
        functools.partial(project_kernel, len(blocks), parts, splits, ext_rows, filt is not None),
        in_specs=[pl.BlockSpec(memory_space=pltpu.SMEM)] + [ANY_SPEC] * (len(blocks) + 2 + len(extra)),
        out_specs=[ANY_SPEC] * len(shapes),
        out_shape=shapes,
        scratch_shapes=[pltpu.VMEM(x.shape, x.dtype) for x in shapes]
        + [
            pltpu.VMEM((len(parts), width, channels), bf16),
            pltpu.VMEM(taps.shape, f32),
            pltpu.VMEM((rows, width), bf16),
            pltpu.VMEM((rows, channels), f32),
            pltpu.VMEM((8, LANES) if filt is None else filt.shape, f32),
            pltpu.SemaphoreType.DMA((len(blocks) + 3,)),
            pltpu.SemaphoreType.DMA((len(parts), splits)),
            pltpu.SemaphoreType.DMA,
            pltpu.SemaphoreType.DMA((len(shapes),)),
        ],
        compiler_params=pltpu.CompilerParams(vmem_limit_bytes=BIG),
        cost_estimate=pl.CostEstimate(flops=cost, bytes_accessed=10**5, transcendentals=0),
        name="project",
    )(me, *blocks, weight, taps, *extra)


def coarse_forward(dev_count, x_ref, lane_ref, e_ref, step=32):
    count = dev_count
    half = count // 2
    low = lane_mask()
    sgn = jnp.where(low, 1.0, -1.0).astype(f32)

    def body(i, carry):
        rows = pl.ds(pl.multiple_of(i * step, step), step)
        x = [x_ref[s, rows, :].astype(f32) for s in range(count)]
        plus = [x[s] + x[count - s] for s in range(1, half)]
        minus = [x[s] - x[count - s] for s in range(1, half)]
        for k in range(count + 1):
            even = k % 2 == 0
            re = x[0]
            im = None
            mid = round(math.cos(math.pi * half * k / count))
            if mid:
                re = re + x[half] if mid > 0 else re - x[half]
            mid = round(math.sin(math.pi * half * k / count))
            if mid:
                im = -x[half] if mid > 0 else x[half]
            for s in range(1, half):
                c, d = math.cos(math.pi * s * k / count), math.sin(math.pi * s * k / count)
                if abs(c) > 1e-9:
                    re = re + c * (plus if even else minus)[s - 1]
                if abs(d) > 1e-9:
                    term = (-d) * (minus if even else plus)[s - 1]
                    im = term if im is None else im + term
            c, d = lane_ref[k, 0:1, :], lane_ref[k, 1:2, :]
            if im is None:
                re, im = re * c, re * (-d)
            else:
                re, im = re * c + im * d, im * c - re * d
            e_ref[k, rows, :LANES] = pltpu.roll(re, HALF, 1) + sgn * re
            e_ref[k, rows, LANES:] = sgn * pltpu.roll(im, HALF, 1) + im
        return carry

    lax.fori_loop(0, FINE // step, body, 0)


def coarse_inverse(dev_count, g_ref, y_ref, first, length, step=32):
    count = dev_count
    half = count // 2

    def body(i, carry):
        rows = pl.ds(pl.multiple_of(i * step, step), step)
        acc = {}

        def add(name, s, term):
            acc[name, s] = term if (name, s) not in acc else acc[name, s] + term

        for k in range(count + 1):
            even = k % 2 == 0
            re, im = g_ref[k, rows, :LANES], g_ref[k, rows, LANES:]
            add("first", 0, re)
            mid = round(math.cos(math.pi * half * k / count))
            if mid:
                add("mid", 0, re if mid > 0 else -re)
            mid = round(math.sin(math.pi * half * k / count))
            if mid:
                add("mid", 0, -im if mid > 0 else im)
            for s in range(1, half):
                c, d = math.cos(math.pi * s * k / count), math.sin(math.pi * s * k / count)
                if abs(c) > 1e-9:
                    add("a" if even else "b", s, c * re)
                if abs(d) > 1e-9:
                    add("b" if even else "a", -s, (-d) * im)
        y_ref[0, rows, :] = acc["first", 0].astype(bf16)
        y_ref[half, rows, :] = acc["mid", 0].astype(bf16)
        zero = jnp.zeros((step, LANES), f32)
        for s in range(1, half):
            same = acc.get(("a", s), zero)
            flip = acc.get(("b", s), zero)
            same_sin = acc.get(("a", -s), zero)
            flip_sin = acc.get(("b", -s), zero)
            total, diff = same + same_sin, flip + flip_sin
            y_ref[s, rows, :] = (total + diff).astype(bf16)
            y_ref[count - s, rows, :] = (total - diff).astype(bf16)
        return carry

    lax.fori_loop(first // step, (first + length) // step, body, 0)


def fine_forward(e, tr, ti, table):
    re, im = e[:, :LANES], e[:, LANES:]
    turned = jnp.concatenate([re * tr - im * ti, re * ti + im * tr], axis=1).astype(bf16)
    both = jnp.dot(table, turned, preferred_element_type=f32)
    return (
        both[:FINE, :LANES] - both[FINE:, LANES:],
        both[:FINE, LANES:] + both[FINE:, :LANES],
    )


def next_turn(turn_ref, step_ref):
    tr, ti = turn_ref[:, :LANES], turn_ref[:, LANES:]
    sr, si = step_ref[:, :LANES], step_ref[:, LANES:]
    turn_ref[:, :LANES] = tr * sr - ti * si
    turn_ref[:, LANES:] = tr * si + ti * sr


def filter_kernel(dev_count, x_any, *refs):
    const_hbm, h_ref = refs[:4], refs[4]
    x_ref, first_ref, step_ref, lane_ref, table_ref, e_ref, sem = refs[5:]
    turn_ref = first_ref
    rows = pl.ds(x_any.shape[1] - FINE, FINE)
    pairs = [(x_any.at[:, rows], x_ref)] + list(zip(const_hbm, (first_ref, step_ref, lane_ref, table_ref)))
    for copy in start_all((*pair, sem.at[i]) for i, pair in enumerate(pairs)):
        copy.wait()
    coarse_forward(dev_count, x_ref, lane_ref, e_ref)
    points = 4 * dev_count * FINE

    def body(k, carry):
        re, im = fine_forward(e_ref[k], turn_ref[:, :LANES], turn_ref[:, LANES:], table_ref[...])
        scale = jnp.where((k == 0) | (k == dev_count), 1.0 / points, 2.0 / points).astype(f32)
        h_ref[k, :, :LANES] = re * scale
        h_ref[k, :, LANES:] = im * scale
        next_turn(turn_ref, step_ref)
        return carry

    lax.fori_loop(0, dev_count + 1, body, 0, unroll=dev_count <= 8)


def merge_halves(dev_count, late_first, early_ref, late_ref, x_ref):
    pick = late_first == 1
    low = lane_mask()
    size = FINE // 2
    for s in range(dev_count):
        early, late = early_ref[s].astype(f32), late_ref[s].astype(f32)
        fixed = jnp.where(low, late[size:], early[: PAD // 2])
        early, late = jnp.concatenate([fixed, early[PAD // 2 :]], axis=0), late[:size]
        first, second = jnp.where(pick, late, early), jnp.where(pick, early, late)
        top, bot = pack_pair(jnp.concatenate([first, second], axis=0))
        x_ref[s, :size] = top
        x_ref[s, size:] = bot


def conv_kernel(dev_count, half_ref, early_any, late_any, h_hbm, *refs):
    const_hbm, y_any = refs[:4], refs[4]
    early_ref, late_ref, x_ref, h_ref, first_ref, step_ref, lane_ref, table_ref, e_ref, y_ref, sem, y_sem = refs[5:]
    turn_ref = first_ref
    pairs = [(early_any.at[:, pl.ds(0, FINE // 2)], early_ref), (late_any, late_ref), (const_hbm[2], lane_ref)]
    pairs += [(const_hbm[0], first_ref), (const_hbm[1], step_ref), (const_hbm[3], table_ref), (h_hbm, h_ref)]
    copies = start_all((*pair, sem.at[i]) for i, pair in enumerate(pairs))
    for copy in copies[:3]:
        copy.wait()
    merge_halves(dev_count, half_ref[0], early_ref, late_ref, x_ref)
    coarse_forward(dev_count, x_ref, lane_ref, e_ref)
    for copy in copies[3:]:
        copy.wait()
    sgn = jnp.where(lane_mask(), 1.0, -1.0).astype(f32)

    def body(k, carry):
        tr, ti = turn_ref[:, :LANES], turn_ref[:, LANES:]
        re, im = fine_forward(e_ref[k], tr, ti, table_ref[...])
        hr, hi = h_ref[k, :, :LANES], h_ref[k, :, LANES:]
        prod = jnp.concatenate([re * hr - im * hi, re * hi + im * hr], axis=1).astype(bf16)
        both = jnp.dot(table_ref[...], prod, preferred_element_type=f32)
        re = both[:FINE, :LANES] + both[FINE:, LANES:]
        im = both[:FINE, LANES:] - both[FINE:, :LANES]
        re, im = re * tr + im * ti, (im * tr - re * ti) * sgn
        re, im = pltpu.roll(re, HALF, 1) + sgn * re, pltpu.roll(im, HALF, 1) + sgn * im
        c, d = lane_ref[k, 0:1, :], lane_ref[k, 1:2, :]
        e_ref[k, :, :LANES] = re * c - im * d
        e_ref[k, :, LANES:] = re * d + im * c
        next_turn(turn_ref, step_ref)
        return carry

    lax.fori_loop(0, dev_count + 1, body, 0, unroll=dev_count <= 8)
    sends = []
    for i in range(2):
        rows = pl.ds(i * FINE // 2, FINE // 2)
        coarse_inverse(dev_count, e_ref, y_ref, i * FINE // 2, FINE // 2)
        sends += start_all([(y_ref.at[:, rows], y_any.at[:, rows], y_sem.at[i])])
    for send in sends:
        send.wait()


def tables(dev_count):
    points = 4 * dev_count * FINE
    fine = np.arange(FINE)
    first = np.exp(-2j * np.pi * fine * (2 * dev_count) / points)[:, None] * np.ones(HALF)
    ones = np.ones((FINE, HALF))
    step = np.exp(-2j * np.pi * fine / points)[:, None] * ones
    first = np.concatenate([ones, first.real, 0 * ones, first.imag], axis=1)
    step = np.concatenate([step.real, step.real, step.imag, -step.imag], axis=1)
    turn = 2 * np.pi * np.arange(dev_count + 1)[:, None] * np.ones(HALF) / (4 * dev_count)
    lane = np.stack(
        [
            np.concatenate([np.ones_like(turn), np.cos(turn)], axis=1),
            np.concatenate([np.zeros_like(turn), np.sin(turn)], axis=1),
        ],
        axis=1,
    )
    angle = -2 * np.pi * (fine[:, None] * fine[None, :] % FINE) / FINE
    table = np.concatenate([np.cos(angle), np.sin(angle)], axis=0)
    return (
        jnp.asarray(first, f32),
        jnp.asarray(step, f32),
        jnp.asarray(lane, f32),
        jnp.asarray(table, bf16),
    )


def const_scratch(consts):
    return [pltpu.VMEM(const.shape, const.dtype) for const in consts]


def filter_spectrum(x, consts):
    dev_count = x.shape[0]
    return pl.pallas_call(
        functools.partial(filter_kernel, dev_count),
        in_specs=[ANY_SPEC] + [HBM_SPEC] * 4,
        out_specs=VMEM_SPEC,
        out_shape=jax.ShapeDtypeStruct((dev_count + 1, FINE, 2 * LANES), f32),
        scratch_shapes=[pltpu.VMEM((dev_count, FINE, LANES), bf16)]
        + const_scratch(consts)
        + [pltpu.VMEM((dev_count + 1, FINE, 2 * LANES), f32), pltpu.SemaphoreType.DMA((5,))],
        compiler_params=pltpu.CompilerParams(vmem_limit_bytes=BIG),
        name="filter_spectrum",
    )(x, *consts)


def convolve(half, early, late, spectrum, consts):
    dev_count = early.shape[0]
    return pl.pallas_call(
        functools.partial(conv_kernel, dev_count),
        in_specs=[pl.BlockSpec(memory_space=pltpu.SMEM)] + [ANY_SPEC] * 2 + [HBM_SPEC] * 5,
        out_specs=ANY_SPEC,
        out_shape=jax.ShapeDtypeStruct((dev_count, FINE, LANES), bf16),
        scratch_shapes=[
            pltpu.VMEM((dev_count, FINE // 2, LANES), bf16),
            pltpu.VMEM(late.shape, bf16),
            pltpu.VMEM((dev_count, FINE, LANES), f32),
            pltpu.VMEM(spectrum.shape, f32),
        ]
        + const_scratch(consts)
        + [
            pltpu.VMEM((dev_count + 1, FINE, 2 * LANES), f32),
            pltpu.VMEM((dev_count, FINE, LANES), bf16),
            pltpu.SemaphoreType.DMA((7,)),
            pltpu.SemaphoreType.DMA((2,)),
        ],
        compiler_params=pltpu.CompilerParams(vmem_limit_bytes=BIG),
        name="convolve",
    )(half, early, late, spectrum, *consts)


def finish(half, conv, early, late, skip_gain):
    rows, channels = early[0].shape
    tiles = channels // LANES

    def kernel(half_ref, c_any, *refs):
        src_hbm, skip_hbm, out_any = refs[:4], refs[4], refs[5]
        c_ref, row_ref, skip_ref, out_ref, sem, c_sem, s_sem, out_sem = refs[6:]
        early_at = half_ref[0]
        cols = [pl.ds(i * LANES, LANES) for i in range(tiles)]
        skip_copy = start_all([(skip_hbm, skip_ref, s_sem)])[0]
        copies = []
        for i in range(tiles):
            pair = pl.ds(2 * i, 2)
            copies.append(
                start_all(
                    [(c_any.at[pair], c_ref.at[pair], c_sem.at[i])]
                    + [
                        (src.at[:, cols[i]], row_ref.at[i, j, pl.ds(0, src.shape[0])], sem.at[i, j])
                        for j, src in enumerate(src_hbm)
                    ]
                )
            )
        skip_copy.wait()
        sends = []
        for i in range(tiles):
            for copy in copies[i]:
                copy.wait()
            top, bot = unpack_pair(c_ref[2 * i].astype(f32), c_ref[2 * i + 1].astype(f32))
            skip = skip_ref[:, cols[i]]
            row_ref[i, 0, :PAD] = row_ref[i, 2, rows:]
            for at, j in ((early_at, 0), (1 - early_at, 2)):
                conv = jnp.where(at == 0, top, bot)
                value = row_ref[i, j + 1, :rows] * (conv + skip * row_ref[i, j, :rows])
                out_ref[i, pl.ds(pl.multiple_of(at * FINE, FINE), FINE), :] = value.astype(bf16)
            sends += start_all([(out_ref.at[i], out_any.at[:, cols[i]], out_sem.at[i])])
        for send in sends:
            send.wait()

    return pl.pallas_call(
        kernel,
        in_specs=[pl.BlockSpec(memory_space=pltpu.SMEM), ANY_SPEC] + [HBM_SPEC] * 5,
        out_specs=ANY_SPEC,
        out_shape=jax.ShapeDtypeStruct((2 * rows, channels), bf16),
        scratch_shapes=[
            pltpu.VMEM(conv.shape, bf16),
            pltpu.VMEM((tiles, 4, rows + PAD, LANES), f32),
            pltpu.VMEM((1, channels), f32),
            pltpu.VMEM((tiles, 2 * rows, LANES), bf16),
            pltpu.SemaphoreType.DMA((tiles, 4)),
            pltpu.SemaphoreType.DMA((tiles,)),
            pltpu.SemaphoreType.DMA,
            pltpu.SemaphoreType.DMA((tiles,)),
        ],
        compiler_params=pltpu.CompilerParams(vmem_limit_bytes=BIG),
        name="finish",
    )(half, conv, *early, *late, skip_gain.reshape(1, channels))


def local(tokens, norm_gain, in_weight, short_weight, long_filter, skip_gain):
    dev_count = lax.axis_size("context")
    tensor_count = lax.axis_size("tensor")
    channels = in_weight.shape[2]
    packed = channels // dev_count == HALF
    consts = tables(dev_count)
    weight = jnp.transpose(in_weight, (1, 0, 2))
    exchange = functools.partial(
        lax.all_to_all, axis_name="context", split_axis=0, concat_axis=0, tiled=True
    )

    me = lax.axis_index("tensor").astype(jnp.int32)
    mid = tensor_count // 2
    half = (me // mid).reshape(1)
    place = (me % mid).reshape(1)

    def swap(x, bit):
        return lax.ppermute(x, "tensor", [(i, i ^ bit) for i in range(tensor_count)])

    def gathered(block):
        blocks = {0: block}
        bit = mid // 2
        while bit:
            for mask in list(blocks):
                blocks[mask | bit] = swap(blocks[mask], bit)
            bit //= 2
        return [blocks[mask] for mask in range(mid)]

    normed, tail = norm_rows(tokens, norm_gain)
    crossed = swap(normed, mid)
    early_blocks = gathered(normed)

    early_blocks, tail = lax.optimization_barrier((early_blocks, tail))
    late_halo = jnp.zeros_like(tail)
    for j in range(mid):
        pairs = [(c * tensor_count - 1, c * tensor_count + mid + j) for c in range(1, dev_count)]
        pairs += [(c * tensor_count + mid - 1, c * tensor_count + j) for c in range(dev_count)]
        late_halo = late_halo + lax.ppermute(tail, ("context", "tensor"), pairs)
    head = sum(jnp.where(place == mask, block[:PAD], 0) for mask, block in enumerate(early_blocks))
    packs = None
    if packed:
        early_gated, packs = project(
            (1, 2), place, early_blocks, weight, short_weight, COST[0], filt=long_filter
        )
    else:
        early_gated, _ = project((1, 2), place, early_blocks, weight, short_weight, COST[0])
        packs = [pack_any(rows, dev_count) for rows in (early_gated, long_filter)]
        packs = jnp.concatenate(packs, axis=1)
    packs, late_halo = lax.optimization_barrier((packs, late_halo))
    early_halo = swap(late_halo, mid)
    early_sent = exchange(packs)
    crossed, _ = lax.optimization_barrier((crossed, packs))
    late_blocks = gathered(crossed)
    gap = jnp.zeros((PAD - TAIL, tail.shape[1]), bf16)
    late_ext = jnp.concatenate([gap, late_halo, gap, early_halo, head], axis=0)
    late_gated, packs = project((1, 2), place, late_blocks, weight, short_weight, COST[1], ext=late_ext)
    if not packed:
        rows = late_gated.shape[0] - PAD
        packs = [pack_any(late_gated[:rows], dev_count), pack_any(late_gated[rows:], dev_count)]
        packs = jnp.concatenate(packs, axis=1)
    late_sent = exchange(packs)
    spectrum = filter_spectrum(early_sent, consts)
    early_ext = jnp.concatenate([gap, early_halo], axis=0)
    (early_query,) = project((0,), place, early_blocks, weight, short_weight, COST[2], ext=early_ext)
    (late_query,) = project((0,), place, late_blocks, weight, short_weight, COST[2], ext=late_ext[:PAD])
    conv = exchange(convolve(half, early_sent, late_sent, spectrum, consts))
    early, late = (early_gated, early_query), (late_gated, late_query)
    if packed:
        return finish(half, conv, early, late, skip_gain)
    early_gated = jnp.concatenate([late_gated[rows:], early_gated[PAD:]], axis=0)
    early, late = (early_gated, early_query), (late_gated[:rows], late_query)
    each = channels // dev_count
    conv = conv.reshape(dev_count, FINE, 2, HALF)[..., :each]
    conv = jnp.transpose(conv, (2, 1, 0, 3)).reshape(2 * FINE, channels).astype(f32)
    first, second = (
        [jnp.where(half == swapped, a, b) for a, b in zip(early, late)] for swapped in (0, 1)
    )
    gated, query = (jnp.concatenate([a, b], axis=0) for a, b in zip(first, second))
    return (query * (conv + skip_gain * gated)).astype(bf16)


def solution(mesh):
    return jax.shard_map(
        local,
        mesh=mesh,
        in_specs=(
            P(("context", "tensor"), None),
            P(),
            P(None, None, "tensor"),
            P(None, None, "tensor"),
            P("context", "tensor"),
            P("tensor"),
        ),
        out_specs=P("context", "tensor"),
        check_vma=False,
    )
```

```python
import functools
import math

import jax
import jax.numpy as jnp
import numpy as np
from jax import lax
from jax.experimental import pallas as pl
from jax.experimental.pallas import tpu as pltpu
from jax.sharding import PartitionSpec as P

eps = 1e-06

FINE = 256
HALF = 64
LANES = 2 * HALF
TAIL = 8
PAD = 16
BIG = 60 * 1024 * 1024
FINISH_LIMIT = 50
COST = (10**8, 10**8, 10**8)

VMEM_SPEC = pl.BlockSpec(memory_space=pltpu.VMEM)
HBM_SPEC = pl.BlockSpec(memory_space=pltpu.HBM)
ANY_SPEC = pl.BlockSpec(memory_space=pl.ANY)

f32 = jnp.float32
bf16 = jnp.bfloat16


def lane_mask():
    return lax.broadcasted_iota(jnp.int32, (1, LANES), 1) < HALF


def pack_pair(tile):
    low = lane_mask()
    rows = tile.shape[0] // 2
    top, bot = tile[:rows], tile[rows:]
    return (
        jnp.where(low, top, pltpu.roll(bot, HALF, 1)),
        jnp.where(low, pltpu.roll(top, HALF, 1), bot),
    )


def unpack_pair(first, second):
    low = lane_mask()
    return (
        jnp.where(low, first, pltpu.roll(second, HALF, 1)),
        jnp.where(low, pltpu.roll(first, HALF, 1), second),
    )


def start_all(copies):
    copies = [pltpu.make_async_copy(*copy) for copy in copies]
    for copy in copies:
        copy.start()
    return copies


def pack_any(rows, dev_count):
    length, channels = rows.shape
    each = channels // dev_count
    blocks = rows.astype(bf16).reshape(2, length // 2, dev_count, each)
    blocks = jnp.transpose(blocks, (2, 1, 0, 3))
    blocks = jnp.pad(blocks, ((0, 0), (0, 0), (0, 0), (0, HALF - each)))
    return blocks.reshape(dev_count, length // 2, LANES)


def norm_rows(tokens, gain):
    rows, width = tokens.shape
    step = min(32, rows)

    def kernel(tok_hbm, gain_hbm, out_any, tail_any, tok_ref, gain_ref, out_ref, sem, out_sem):
        parts = [pl.ds(i * step, step) for i in range(rows // step)]
        copies = start_all(
            [(gain_hbm, gain_ref, sem.at[len(parts)])]
            + [(tok_hbm.at[part], tok_ref.at[part], sem.at[i]) for i, part in enumerate(parts)]
        )
        copies[0].wait()
        sends = []
        for i, part in enumerate(parts):
            copies[1 + i].wait()
            values = tok_ref[part, :].astype(f32)
            inv_rms = lax.rsqrt(jnp.mean(values * values, axis=1, keepdims=True) + eps)
            out_ref[part, :] = (values * inv_rms * gain_ref[...]).astype(bf16)
            sends += start_all([(out_ref.at[part], out_any.at[part], out_sem.at[i])])
        sends += start_all([(out_ref.at[pl.ds(rows - TAIL, TAIL)], tail_any, out_sem.at[len(parts)])])
        for send in sends:
            send.wait()

    return pl.pallas_call(
        kernel,
        in_specs=[HBM_SPEC] * 2,
        out_specs=[ANY_SPEC] * 2,
        out_shape=[jax.ShapeDtypeStruct((rows, width), bf16), jax.ShapeDtypeStruct((TAIL, width), bf16)],
        scratch_shapes=[
            pltpu.VMEM((rows, width), bf16),
            pltpu.VMEM((1, width), f32),
            pltpu.VMEM((rows, width), bf16),
            pltpu.SemaphoreType.DMA((rows // step + 1,)),
            pltpu.SemaphoreType.DMA((rows // step + 1,)),
        ],
        compiler_params=pltpu.CompilerParams(vmem_limit_bytes=BIG),
        name="norm_rows",
    )(tokens, gain.reshape(1, width))


def pack_into(p_ref, at, rows_ref, first, length):
    rows = pl.ds(at, length // 2)
    for i in range(p_ref.shape[0] // 2):
        one, two = pack_pair(rows_ref[first : first + length, i * LANES : (i + 1) * LANES])
        p_ref[2 * i, rows, :] = one.astype(bf16)
        p_ref[2 * i + 1, rows, :] = two.astype(bf16)


def project_kernel(count, parts, splits, ext_rows, with_filter, me_ref, *refs):
    blocks, refs = refs[:count], refs[count:]
    w_hbm, tap_hbm = refs[:2]
    extra, refs = refs[2 : 2 + bool(ext_rows) + with_filter], refs[2 + bool(ext_rows) + with_filter :]
    number = 2 * (1 in parts) + (0 in parts)
    out_any, outs, refs = refs[:number], refs[number : 2 * number], refs[2 * number :]
    w_ref, tap_ref, x_ref, rows_ref, filt_ref, sem, w_sem, tap_sem, out_sem = refs

    def send(i):
        return start_all([(outs[i], out_any[i], out_sem.at[i])])

    each = blocks[0].shape[0]
    length = each * count
    end = PAD + length
    width, channels = x_ref.shape[1], rows_ref.shape[1]
    each_cols = channels // splits

    sources = [(tap_hbm, tap_ref, tap_sem)]
    for mask, block in enumerate(blocks):
        first = pl.multiple_of(PAD + (me_ref[0] ^ mask) * each, 16)
        sources.append((block, x_ref.at[pl.ds(first, each)], sem.at[mask]))
    if ext_rows:
        sources.append((extra[0].at[pl.ds(0, PAD)], x_ref.at[pl.ds(0, PAD)], sem.at[count]))
    else:
        x_ref[:PAD] = jnp.zeros((PAD, width), bf16)
    if ext_rows > PAD:
        rest = ext_rows - PAD
        sources.append((extra[0].at[pl.ds(PAD, rest)], x_ref.at[pl.ds(end, rest)], sem.at[count + 1]))
    waits = start_all(sources)
    loads = {}
    for at, s in enumerate(parts):
        for i in range(splits):
            cols = pl.ds(i * each_cols, each_cols)
            loads[s, i] = start_all([(w_hbm.at[s, :, cols], w_ref.at[at, i], w_sem.at[at, i])])[0]
    if with_filter:
        filt_load = start_all([(extra[-1], filt_ref, sem.at[count + 2])])[0]
    for wait in waits:
        wait.wait()

    def mixed(s):
        at = parts.index(s)
        for i in range(splits):
            loads[s, i].wait()
            cols = slice(i * each_cols, (i + 1) * each_cols)
            rows_ref[:, cols] = jnp.dot(x_ref[...], w_ref[at, i], preferred_element_type=f32)
        spans = [(PAD, length)]
        if ext_rows > PAD:
            spans.append((end + PAD, PAD))
        results = []
        for first, size in spans:
            total = tap_ref[0, s : s + 1] * rows_ref[first : first + size]
            for lag in (1, 2):
                total += tap_ref[lag, s : s + 1] * rows_ref[first - lag : first - lag + size]
            results.append(total)
        return results

    if 1 in parts:
        g_ref, p_ref = outs[:2]
        spans = [slice(0, length), slice(length, length + PAD)]
        for span, key in zip(spans, mixed(1)):
            g_ref[span, :] = key
        for span, value in zip(spans, mixed(2)):
            g_ref[span, :] *= value
        sends = send(0)
        pack_into(p_ref, 0, g_ref, 0, length)
        if ext_rows > PAD:
            pack_into(p_ref, length // 2, g_ref, length, PAD)
        if with_filter:
            filt_load.wait()
            pack_into(p_ref, length // 2, filt_ref, 0, filt_ref.shape[0])
        sends += send(1)
    if 0 in parts:
        outs[-1][...] = mixed(0)[0]
        sends = (sends if 1 in parts else []) + send(number - 1)
    for copy in sends:
        copy.wait()


def project(parts, me, blocks, weight, taps, cost, ext=None, filt=None):
    _, width, channels = weight.shape
    length = blocks[0].shape[0] * len(blocks)
    splits = 1
    ext_rows = 0 if ext is None else ext.shape[0]
    more = PAD if ext_rows > PAD else 0
    shapes = []
    if 1 in parts:
        rows = (length + more) // 2 + (0 if filt is None else filt.shape[0] // 2)
        shapes += [
            jax.ShapeDtypeStruct((length + more, channels), f32),
            jax.ShapeDtypeStruct((max(channels // HALF, 2), rows, LANES), bf16),
        ]
    if 0 in parts:
        shapes.append(jax.ShapeDtypeStruct((length, channels), f32))
    extra = [x for x in (ext, filt) if x is not None]
    rows = PAD + length + (2 * PAD if more else 0)
    return pl.pallas_call(
        functools.partial(project_kernel, len(blocks), parts, splits, ext_rows, filt is not None),
        in_specs=[pl.BlockSpec(memory_space=pltpu.SMEM)] + [ANY_SPEC] * (len(blocks) + 2 + len(extra)),
        out_specs=[ANY_SPEC] * len(shapes),
        out_shape=shapes,
        scratch_shapes=[pltpu.VMEM(x.shape, x.dtype) for x in shapes]
        + [
            pltpu.VMEM((len(parts), splits, width, channels // splits), bf16),
            pltpu.VMEM(taps.shape, f32),
            pltpu.VMEM((rows, width), bf16),
            pltpu.VMEM((rows, channels), f32),
            pltpu.VMEM((8, LANES) if filt is None else filt.shape, f32),
            pltpu.SemaphoreType.DMA((len(blocks) + 3,)),
            pltpu.SemaphoreType.DMA((len(parts), splits)),
            pltpu.SemaphoreType.DMA,
            pltpu.SemaphoreType.DMA((len(shapes),)),
        ],
        compiler_params=pltpu.CompilerParams(vmem_limit_bytes=BIG),
        cost_estimate=pl.CostEstimate(flops=cost, bytes_accessed=10**5, transcendentals=0),
        name="project",
    )(me, *blocks, weight, taps, *extra)


def coarse_forward(dev_count, x_ref, lane_ref, e_ref, step=64):
    count = dev_count
    half = count // 2
    low = lane_mask()
    sgn = jnp.where(low, 1.0, -1.0).astype(f32)

    def body(i, carry):
        rows = pl.ds(pl.multiple_of(i * step, step), step)
        x = [x_ref[s, rows, :].astype(f32) for s in range(count)]
        plus = [x[s] + x[count - s] for s in range(1, half)]
        minus = [x[s] - x[count - s] for s in range(1, half)]
        for k in range(count + 1):
            even = k % 2 == 0
            re = x[0]
            im = None
            mid = round(math.cos(math.pi * half * k / count))
            if mid:
                re = re + x[half] if mid > 0 else re - x[half]
            mid = round(math.sin(math.pi * half * k / count))
            if mid:
                im = -x[half] if mid > 0 else x[half]
            for s in range(1, half):
                c, d = math.cos(math.pi * s * k / count), math.sin(math.pi * s * k / count)
                if abs(c) > 1e-9:
                    re = re + c * (plus if even else minus)[s - 1]
                if abs(d) > 1e-9:
                    term = (-d) * (minus if even else plus)[s - 1]
                    im = term if im is None else im + term
            c, d = lane_ref[k, 0:1, :], lane_ref[k, 1:2, :]
            if im is None:
                re, im = re * c, re * (-d)
            else:
                re, im = re * c + im * d, im * c - re * d
            e_ref[k, rows, :LANES] = pltpu.roll(re, HALF, 1) + sgn * re
            e_ref[k, rows, LANES:] = sgn * pltpu.roll(im, HALF, 1) + im
        return carry

    lax.fori_loop(0, FINE // step, body, 0)


def coarse_inverse(dev_count, g_ref, y_ref, first, length, step=64):
    count = dev_count
    half = count // 2

    def body(i, carry):
        rows = pl.ds(pl.multiple_of(i * step, step), step)
        acc = {}

        def add(name, s, term):
            acc[name, s] = term if (name, s) not in acc else acc[name, s] + term

        for k in range(count + 1):
            even = k % 2 == 0
            re, im = g_ref[k, rows, :LANES], g_ref[k, rows, LANES:]
            add("first", 0, re)
            mid = round(math.cos(math.pi * half * k / count))
            if mid:
                add("mid", 0, re if mid > 0 else -re)
            mid = round(math.sin(math.pi * half * k / count))
            if mid:
                add("mid", 0, -im if mid > 0 else im)
            for s in range(1, half):
                c, d = math.cos(math.pi * s * k / count), math.sin(math.pi * s * k / count)
                if abs(c) > 1e-9:
                    add("a" if even else "b", s, c * re)
                if abs(d) > 1e-9:
                    add("b" if even else "a", -s, (-d) * im)
        y_ref[0, rows, :] = acc["first", 0].astype(bf16)
        y_ref[half, rows, :] = acc["mid", 0].astype(bf16)
        zero = jnp.zeros((step, LANES), f32)
        for s in range(1, half):
            same = acc.get(("a", s), zero)
            flip = acc.get(("b", s), zero)
            same_sin = acc.get(("a", -s), zero)
            flip_sin = acc.get(("b", -s), zero)
            total, diff = same + same_sin, flip + flip_sin
            y_ref[s, rows, :] = (total + diff).astype(bf16)
            y_ref[count - s, rows, :] = (total - diff).astype(bf16)
        return carry

    lax.fori_loop(first // step, (first + length) // step, body, 0)


def fine_forward(e, tr, ti, table):
    re, im = e[:, :LANES], e[:, LANES:]
    turned = jnp.concatenate([re * tr - im * ti, re * ti + im * tr], axis=1).astype(bf16)
    both = jnp.dot(table, turned, preferred_element_type=f32)
    return (
        both[:FINE, :LANES] - both[FINE:, LANES:],
        both[:FINE, LANES:] + both[FINE:, :LANES],
    )


def next_turn(turn_ref, step_ref):
    tr, ti = turn_ref[:, :LANES], turn_ref[:, LANES:]
    sr, si = step_ref[:, :LANES], step_ref[:, LANES:]
    turn_ref[:, :LANES] = tr * sr - ti * si
    turn_ref[:, LANES:] = tr * si + ti * sr


def filter_kernel(dev_count, x_any, *refs):
    const_hbm, h_ref = refs[:4], refs[4]
    x_ref, first_ref, step_ref, lane_ref, table_ref, e_ref, sem = refs[5:]
    turn_ref = first_ref
    rows = pl.ds(x_any.shape[1] - FINE, FINE)
    pairs = [(x_any.at[:, rows], x_ref)] + list(zip(const_hbm, (first_ref, step_ref, lane_ref, table_ref)))
    for copy in start_all((*pair, sem.at[i]) for i, pair in enumerate(pairs)):
        copy.wait()
    coarse_forward(dev_count, x_ref, lane_ref, e_ref)
    points = 4 * dev_count * FINE

    def body(k, carry):
        re, im = fine_forward(e_ref[k], turn_ref[:, :LANES], turn_ref[:, LANES:], table_ref[...])
        scale = jnp.where((k == 0) | (k == dev_count), 1.0 / points, 2.0 / points).astype(f32)
        h_ref[k, :, :LANES] = re * scale
        h_ref[k, :, LANES:] = im * scale
        next_turn(turn_ref, step_ref)
        return carry

    lax.fori_loop(0, dev_count + 1, body, 0, unroll=dev_count <= 8)


def merge_halves(dev_count, late_first, early_ref, late_ref, x_ref):
    pick = late_first == 1
    low = lane_mask()
    size = FINE // 2
    for s in range(dev_count):
        early, late = early_ref[s].astype(f32), late_ref[s].astype(f32)
        fixed = jnp.where(low, late[size:], early[: PAD // 2])
        early, late = jnp.concatenate([fixed, early[PAD // 2 :]], axis=0), late[:size]
        first, second = jnp.where(pick, late, early), jnp.where(pick, early, late)
        top, bot = pack_pair(jnp.concatenate([first, second], axis=0))
        x_ref[s, :size] = top
        x_ref[s, size:] = bot


def conv_kernel(dev_count, half_ref, early_any, late_any, h_hbm, *refs):
    const_hbm, y_any = refs[:4], refs[4]
    early_ref, late_ref, x_ref, h_ref, first_ref, step_ref, lane_ref, table_ref, e_ref, y_ref, sem, y_sem = refs[5:]
    turn_ref = first_ref
    pairs = [(early_any.at[:, pl.ds(0, FINE // 2)], early_ref), (late_any, late_ref), (const_hbm[2], lane_ref)]
    pairs += [(const_hbm[0], first_ref), (const_hbm[1], step_ref), (const_hbm[3], table_ref), (h_hbm, h_ref)]
    copies = start_all((*pair, sem.at[i]) for i, pair in enumerate(pairs))
    for copy in copies[:3]:
        copy.wait()
    merge_halves(dev_count, half_ref[0], early_ref, late_ref, x_ref)
    coarse_forward(dev_count, x_ref, lane_ref, e_ref)
    for copy in copies[3:]:
        copy.wait()
    sgn = jnp.where(lane_mask(), 1.0, -1.0).astype(f32)

    def body(k, carry):
        tr, ti = turn_ref[:, :LANES], turn_ref[:, LANES:]
        re, im = fine_forward(e_ref[k], tr, ti, table_ref[...])
        hr, hi = h_ref[k, :, :LANES], h_ref[k, :, LANES:]
        prod = jnp.concatenate([re * hr - im * hi, re * hi + im * hr], axis=1).astype(bf16)
        both = jnp.dot(table_ref[...], prod, preferred_element_type=f32)
        re = both[:FINE, :LANES] + both[FINE:, LANES:]
        im = both[:FINE, LANES:] - both[FINE:, :LANES]
        re, im = re * tr + im * ti, (im * tr - re * ti) * sgn
        re, im = pltpu.roll(re, HALF, 1) + sgn * re, pltpu.roll(im, HALF, 1) + sgn * im
        c, d = lane_ref[k, 0:1, :], lane_ref[k, 1:2, :]
        e_ref[k, :, :LANES] = re * c - im * d
        e_ref[k, :, LANES:] = re * d + im * c
        next_turn(turn_ref, step_ref)
        return carry

    lax.fori_loop(0, dev_count + 1, body, 0, unroll=dev_count <= 8)
    sends = []
    for i in range(2):
        rows = pl.ds(i * FINE // 2, FINE // 2)
        coarse_inverse(dev_count, e_ref, y_ref, i * FINE // 2, FINE // 2)
        sends += start_all([(y_ref.at[:, rows], y_any.at[:, rows], y_sem.at[i])])
    for send in sends:
        send.wait()


def tables(dev_count):
    points = 4 * dev_count * FINE
    fine = np.arange(FINE)
    first = np.exp(-2j * np.pi * fine * (2 * dev_count) / points)[:, None] * np.ones(HALF)
    ones = np.ones((FINE, HALF))
    step = np.exp(-2j * np.pi * fine / points)[:, None] * ones
    first = np.concatenate([ones, first.real, 0 * ones, first.imag], axis=1)
    step = np.concatenate([step.real, step.real, step.imag, -step.imag], axis=1)
    turn = 2 * np.pi * np.arange(dev_count + 1)[:, None] * np.ones(HALF) / (4 * dev_count)
    lane = np.stack(
        [
            np.concatenate([np.ones_like(turn), np.cos(turn)], axis=1),
            np.concatenate([np.zeros_like(turn), np.sin(turn)], axis=1),
        ],
        axis=1,
    )
    angle = -2 * np.pi * (fine[:, None] * fine[None, :] % FINE) / FINE
    table = np.concatenate([np.cos(angle), np.sin(angle)], axis=0)
    return (
        jnp.asarray(first, f32),
        jnp.asarray(step, f32),
        jnp.asarray(lane, f32),
        jnp.asarray(table, bf16),
    )


def const_scratch(consts):
    return [pltpu.VMEM(const.shape, const.dtype) for const in consts]


def filter_spectrum(x, consts):
    dev_count = x.shape[0]
    return pl.pallas_call(
        functools.partial(filter_kernel, dev_count),
        in_specs=[ANY_SPEC] + [HBM_SPEC] * 4,
        out_specs=VMEM_SPEC,
        out_shape=jax.ShapeDtypeStruct((dev_count + 1, FINE, 2 * LANES), f32),
        scratch_shapes=[pltpu.VMEM((dev_count, FINE, LANES), bf16)]
        + const_scratch(consts)
        + [pltpu.VMEM((dev_count + 1, FINE, 2 * LANES), f32), pltpu.SemaphoreType.DMA((5,))],
        compiler_params=pltpu.CompilerParams(vmem_limit_bytes=BIG),
        name="filter_spectrum",
    )(x, *consts)


def convolve(half, early, late, spectrum, consts):
    dev_count = early.shape[0]
    return pl.pallas_call(
        functools.partial(conv_kernel, dev_count),
        in_specs=[pl.BlockSpec(memory_space=pltpu.SMEM)] + [ANY_SPEC] * 2 + [HBM_SPEC] * 5,
        out_specs=ANY_SPEC,
        out_shape=jax.ShapeDtypeStruct((dev_count, FINE, LANES), bf16),
        scratch_shapes=[
            pltpu.VMEM((dev_count, FINE // 2, LANES), bf16),
            pltpu.VMEM(late.shape, bf16),
            pltpu.VMEM((dev_count, FINE, LANES), f32),
            pltpu.VMEM(spectrum.shape, f32),
        ]
        + const_scratch(consts)
        + [
            pltpu.VMEM((dev_count + 1, FINE, 2 * LANES), f32),
            pltpu.VMEM((dev_count, FINE, LANES), bf16),
            pltpu.SemaphoreType.DMA((7,)),
            pltpu.SemaphoreType.DMA((2,)),
        ],
        compiler_params=pltpu.CompilerParams(vmem_limit_bytes=BIG),
        name="convolve",
    )(half, early, late, spectrum, *consts)


def query_kernel(count, me_ref, *refs):
    blocks, refs = refs[:count], refs[count:]
    halo_any, w_hbm, tap_hbm, early_any, late_any, skip_hbm, out_any = refs[:7]
    x_ref, w_ref, tap_ref, early_ref, late_ref, skip_ref, rows_ref, out_ref, sem, out_sem = refs[7:]
    each = blocks[0].shape[0]
    length = each * count
    half = length // 2
    early_at = me_ref[1]

    ahead = pl.ds(pl.multiple_of((1 - early_at) * PAD, PAD), PAD)
    pairs = [(halo_any.at[ahead], x_ref.at[pl.ds(0, PAD)])]
    for mask, block in enumerate(blocks):
        first = pl.multiple_of(PAD + (me_ref[0] ^ mask) * each, 16)
        pairs.append((block, x_ref.at[pl.ds(first, each)]))
    pairs += [(w_hbm.at[0], w_ref), (tap_hbm, tap_ref), (skip_hbm, skip_ref)]
    pairs += [(early_any, early_ref), (late_any, late_ref)]
    for copy in start_all((*pair, sem.at[i]) for i, pair in enumerate(pairs)):
        copy.wait()
    rows_ref[...] = jnp.dot(x_ref[...], w_ref[...], preferred_element_type=f32)
    total = tap_ref[0, 0:1] * rows_ref[PAD:]
    for lag in (1, 2):
        total += tap_ref[lag, 0:1] * rows_ref[PAD - lag : PAD - lag + length]
    out_ref[0] = total
    early_ref[:PAD] = late_ref[half:]
    for at, g_ref in ((early_at, early_ref), (1 - early_at, late_ref)):
        rows = pl.ds(pl.multiple_of(at * half, half), half)
        out_ref[1, rows, :] = out_ref[0, rows, :] * (skip_ref[...] * g_ref[:half])
    start_all([(out_ref, out_any, out_sem)])[0].wait()


def query_terms(me, blocks, halo, weight, taps, early, late, skip):
    _, width, channels = weight.shape
    length = blocks[0].shape[0] * len(blocks)
    skip = skip.reshape(1, channels)
    return pl.pallas_call(
        functools.partial(query_kernel, len(blocks)),
        in_specs=[pl.BlockSpec(memory_space=pltpu.SMEM)] + [ANY_SPEC] * (len(blocks) + 6),
        out_specs=ANY_SPEC,
        out_shape=jax.ShapeDtypeStruct((2, length, channels), f32),
        scratch_shapes=[
            pltpu.VMEM((PAD + length, width), bf16),
            pltpu.VMEM((width, channels), bf16),
            pltpu.VMEM(taps.shape, f32),
            pltpu.VMEM(early.shape, f32),
            pltpu.VMEM(late.shape, f32),
            pltpu.VMEM(skip.shape, f32),
            pltpu.VMEM((PAD + length, channels), f32),
            pltpu.VMEM((2, length, channels), f32),
            pltpu.SemaphoreType.DMA((len(blocks) + 6,)),
            pltpu.SemaphoreType.DMA,
        ],
        compiler_params=pltpu.CompilerParams(vmem_limit_bytes=BIG),
        cost_estimate=pl.CostEstimate(flops=COST[2], bytes_accessed=10**5, transcendentals=0),
        name="query_terms",
    )(me, *blocks, halo, weight, taps, early, late, skip)


def finish(conv, terms):
    _, length, channels = terms.shape
    tiles = channels // LANES

    def kernel(c_ref, term_ref, out_any, out_ref, sem):
        sends = []
        for i in range(tiles):
            cols = slice(i * LANES, (i + 1) * LANES)
            top, bot = unpack_pair(c_ref[2 * i].astype(f32), c_ref[2 * i + 1].astype(f32))
            for j, part in enumerate((top, bot)):
                rows = slice(j * FINE, (j + 1) * FINE)
                out_ref[i, rows] = (term_ref[0, rows, cols] * part + term_ref[1, rows, cols]).astype(bf16)
            sends += start_all([(out_ref.at[i], out_any.at[:, pl.ds(i * LANES, LANES)], sem.at[i])])
        for send in sends:
            send.wait()

    return pl.pallas_call(
        kernel,
        in_specs=[VMEM_SPEC] * 2,
        out_specs=ANY_SPEC,
        out_shape=jax.ShapeDtypeStruct((length, channels), bf16),
        scratch_shapes=[pltpu.VMEM((tiles, length, LANES), bf16), pltpu.SemaphoreType.DMA((tiles,))],
        compiler_params=pltpu.CompilerParams(vmem_limit_bytes=FINISH_LIMIT * 1024 * 1024),
        name="finish",
    )(conv, terms)


def local(tokens, norm_gain, in_weight, short_weight, long_filter, skip_gain):
    dev_count = lax.axis_size("context")
    tensor_count = lax.axis_size("tensor")
    channels = in_weight.shape[2]
    packed = channels // dev_count == HALF
    consts = tables(dev_count)
    weight = jnp.transpose(in_weight, (1, 0, 2))
    exchange = functools.partial(
        lax.all_to_all, axis_name="context", split_axis=0, concat_axis=0, tiled=True
    )

    me = lax.axis_index("tensor").astype(jnp.int32)
    mid = tensor_count // 2
    half = (me // mid).reshape(1)
    place = (me % mid).reshape(1)

    def swap(x, bit):
        return lax.ppermute(x, "tensor", [(i, i ^ bit) for i in range(tensor_count)])

    def gathered(block):
        blocks = {0: block}
        bit = mid // 2
        while bit:
            for mask in list(blocks):
                blocks[mask | bit] = swap(blocks[mask], bit)
            bit //= 2
        return [blocks[mask] for mask in range(mid)]

    normed, tail = norm_rows(tokens, norm_gain)
    crossed = swap(normed, mid)
    early_blocks = gathered(normed)

    early_blocks, tail = lax.optimization_barrier((early_blocks, tail))
    late_halo = jnp.zeros_like(tail)
    for j in range(mid):
        pairs = [(c * tensor_count - 1, c * tensor_count + mid + j) for c in range(1, dev_count)]
        pairs += [(c * tensor_count + mid - 1, c * tensor_count + j) for c in range(dev_count)]
        late_halo = late_halo + lax.ppermute(tail, ("context", "tensor"), pairs)
    head = sum(jnp.where(place == mask, block[:PAD], 0) for mask, block in enumerate(early_blocks))
    packs = None
    if packed:
        early_gated, packs = project(
            (1, 2), place, early_blocks, weight, short_weight, COST[0], filt=long_filter
        )
    else:
        early_gated, _ = project((1, 2), place, early_blocks, weight, short_weight, COST[0])
        packs = [pack_any(rows, dev_count) for rows in (early_gated, long_filter)]
        packs = jnp.concatenate(packs, axis=1)
    packs, late_halo = lax.optimization_barrier((packs, late_halo))
    early_halo = swap(late_halo, mid)
    early_sent = exchange(packs)
    crossed, _ = lax.optimization_barrier((crossed, packs))
    late_blocks = gathered(crossed)
    gap = jnp.zeros((PAD - TAIL, tail.shape[1]), bf16)
    late_ext = jnp.concatenate([gap, late_halo, gap, early_halo, head], axis=0)
    late_gated, packs = project((1, 2), place, late_blocks, weight, short_weight, COST[1], ext=late_ext)
    if not packed:
        rows = late_gated.shape[0] - PAD
        packs = [pack_any(late_gated[:rows], dev_count), pack_any(late_gated[rows:], dev_count)]
        packs = jnp.concatenate(packs, axis=1)
    late_sent = exchange(packs)
    spectrum = filter_spectrum(early_sent, consts)
    conv = exchange(convolve(half, early_sent, late_sent, spectrum, consts))
    terms = query_terms(
        jnp.concatenate([me.reshape(1), half]),
        early_blocks + late_blocks,
        late_ext,
        weight,
        short_weight,
        early_gated,
        late_gated,
        skip_gain,
    )
    if packed:
        return finish(conv, terms)
    each = channels // dev_count
    conv = conv.reshape(dev_count, FINE, 2, HALF)[..., :each]
    conv = jnp.transpose(conv, (2, 1, 0, 3)).reshape(2 * FINE, channels).astype(f32)
    return (terms[0] * conv + terms[1]).astype(bf16)


def solution(mesh):
    return jax.shard_map(
        local,
        mesh=mesh,
        in_specs=(
            P(("context", "tensor"), None),
            P(),
            P(None, None, "tensor"),
            P(None, None, "tensor"),
            P("context", "tensor"),
            P("tensor"),
        ),
        out_specs=P("context", "tensor"),
        check_vma=False,
    )
```

```python
import functools
import math

import jax
import jax.numpy as jnp
import numpy as np
from jax import lax
from jax.experimental import pallas as pl
from jax.experimental.pallas import tpu as pltpu
from jax.sharding import PartitionSpec as P

eps = 1e-06

FINE = 256
HALF = 64
LANES = 2 * HALF
TAIL = 8
PAD = 16
BIG = 60 * 1024 * 1024
FINISH_LIMIT = 53
COST = (10**8, 10**8, 10**8)

VMEM_SPEC = pl.BlockSpec(memory_space=pltpu.VMEM)
HBM_SPEC = pl.BlockSpec(memory_space=pltpu.HBM)
ANY_SPEC = pl.BlockSpec(memory_space=pl.ANY)

f32 = jnp.float32
bf16 = jnp.bfloat16


def lane_mask():
    return lax.broadcasted_iota(jnp.int32, (1, LANES), 1) < HALF


def pack_pair(tile):
    low = lane_mask()
    rows = tile.shape[0] // 2
    top, bot = tile[:rows], tile[rows:]
    return (
        jnp.where(low, top, pltpu.roll(bot, HALF, 1)),
        jnp.where(low, pltpu.roll(top, HALF, 1), bot),
    )


def unpack_pair(first, second):
    low = lane_mask()
    return (
        jnp.where(low, first, pltpu.roll(second, HALF, 1)),
        jnp.where(low, pltpu.roll(first, HALF, 1), second),
    )


def start_all(copies):
    copies = [pltpu.make_async_copy(*copy) for copy in copies]
    for copy in copies:
        copy.start()
    return copies


def pack_any(rows, dev_count):
    length, channels = rows.shape
    each = channels // dev_count
    blocks = rows.astype(bf16).reshape(2, length // 2, dev_count, each)
    blocks = jnp.transpose(blocks, (2, 1, 0, 3))
    blocks = jnp.pad(blocks, ((0, 0), (0, 0), (0, 0), (0, HALF - each)))
    return blocks.reshape(dev_count, length // 2, LANES)


def norm_rows(tokens, gain):
    rows, width = tokens.shape
    step = min(32, rows)

    def kernel(tok_hbm, gain_hbm, out_any, tail_any, tok_ref, gain_ref, out_ref, sem, out_sem):
        parts = [pl.ds(i * step, step) for i in range(rows // step)]
        copies = start_all(
            [(gain_hbm, gain_ref, sem.at[len(parts)])]
            + [(tok_hbm.at[part], tok_ref.at[part], sem.at[i]) for i, part in enumerate(parts)]
        )
        copies[0].wait()
        sends = []
        for i, part in enumerate(parts):
            copies[1 + i].wait()
            values = tok_ref[part, :].astype(f32)
            inv_rms = lax.rsqrt(jnp.mean(values * values, axis=1, keepdims=True) + eps)
            out_ref[part, :] = (values * inv_rms * gain_ref[...]).astype(bf16)
            sends += start_all([(out_ref.at[part], out_any.at[part], out_sem.at[i])])
        sends += start_all([(out_ref.at[pl.ds(rows - TAIL, TAIL)], tail_any, out_sem.at[len(parts)])])
        for send in sends:
            send.wait()

    return pl.pallas_call(
        kernel,
        in_specs=[HBM_SPEC] * 2,
        out_specs=[ANY_SPEC] * 2,
        out_shape=[jax.ShapeDtypeStruct((rows, width), bf16), jax.ShapeDtypeStruct((TAIL, width), bf16)],
        scratch_shapes=[
            pltpu.VMEM((rows, width), bf16),
            pltpu.VMEM((1, width), f32),
            pltpu.VMEM((rows, width), bf16),
            pltpu.SemaphoreType.DMA((rows // step + 1,)),
            pltpu.SemaphoreType.DMA((rows // step + 1,)),
        ],
        compiler_params=pltpu.CompilerParams(vmem_limit_bytes=BIG),
        name="norm_rows",
    )(tokens, gain.reshape(1, width))


def pack_into(p_ref, at, rows_ref, first, length):
    rows = pl.ds(at, length // 2)
    for i in range(p_ref.shape[0] // 2):
        one, two = pack_pair(rows_ref[first : first + length, i * LANES : (i + 1) * LANES])
        p_ref[2 * i, rows, :] = one.astype(bf16)
        p_ref[2 * i + 1, rows, :] = two.astype(bf16)


def project_kernel(count, parts, splits, ext_rows, with_filter, me_ref, *refs):
    blocks, refs = refs[:count], refs[count:]
    w_hbm, tap_hbm = refs[:2]
    extra, refs = refs[2 : 2 + bool(ext_rows) + with_filter], refs[2 + bool(ext_rows) + with_filter :]
    number = 2 * (1 in parts) + (0 in parts)
    out_any, outs, refs = refs[:number], refs[number : 2 * number], refs[2 * number :]
    w_ref, tap_ref, x_ref, rows_ref, filt_ref, sem, w_sem, tap_sem, out_sem = refs

    def send(i):
        return start_all([(outs[i], out_any[i], out_sem.at[i])])

    each = blocks[0].shape[0]
    length = each * count
    end = PAD + length
    width, channels = x_ref.shape[1], rows_ref.shape[1]
    each_cols = channels // splits

    sources = [(tap_hbm, tap_ref, tap_sem)]
    for mask, block in enumerate(blocks):
        first = pl.multiple_of(PAD + (me_ref[0] ^ mask) * each, 16)
        sources.append((block, x_ref.at[pl.ds(first, each)], sem.at[mask]))
    if ext_rows:
        sources.append((extra[0].at[pl.ds(0, PAD)], x_ref.at[pl.ds(0, PAD)], sem.at[count]))
    else:
        x_ref[:PAD] = jnp.zeros((PAD, width), bf16)
    if ext_rows > PAD:
        rest = ext_rows - PAD
        sources.append((extra[0].at[pl.ds(PAD, rest)], x_ref.at[pl.ds(end, rest)], sem.at[count + 1]))
    if with_filter:
        filt_load = start_all([(extra[-1], filt_ref, sem.at[count + 2])])[0]
    waits = start_all(sources)
    loads = {}
    for at, s in enumerate(parts):
        for i in range(splits):
            cols = pl.ds(i * each_cols, each_cols)
            loads[s, i] = start_all([(w_hbm.at[s, :, cols], w_ref.at[at, i], w_sem.at[at, i])])[0]
    if with_filter:
        filt_load.wait()
        pack_into(outs[1], length // 2, filt_ref, 0, filt_ref.shape[0])
    for wait in waits:
        wait.wait()

    def mixed(s):
        at = parts.index(s)
        for i in range(splits):
            loads[s, i].wait()
            cols = slice(i * each_cols, (i + 1) * each_cols)
            rows_ref[:, cols] = jnp.dot(x_ref[...], w_ref[at, i], preferred_element_type=f32)
        spans = [(PAD, length)]
        if ext_rows > PAD:
            spans.append((end + PAD, PAD))
        results = []
        for first, size in spans:
            total = tap_ref[0, s : s + 1] * rows_ref[first : first + size]
            for lag in (1, 2):
                total += tap_ref[lag, s : s + 1] * rows_ref[first - lag : first - lag + size]
            results.append(total)
        return results

    if 1 in parts:
        g_ref, p_ref = outs[:2]
        spans = [slice(0, length), slice(length, length + PAD)]
        for span, key in zip(spans, mixed(1)):
            g_ref[span, :] = key
        for span, value in zip(spans, mixed(2)):
            g_ref[span, :] *= value
        sends = send(0)
        pack_into(p_ref, 0, g_ref, 0, length)
        if ext_rows > PAD:
            pack_into(p_ref, length // 2, g_ref, length, PAD)
        sends += send(1)
    if 0 in parts:
        outs[-1][...] = mixed(0)[0]
        sends = (sends if 1 in parts else []) + send(number - 1)
    for copy in sends:
        copy.wait()


def project(parts, me, blocks, weight, taps, cost, ext=None, filt=None):
    _, width, channels = weight.shape
    length = blocks[0].shape[0] * len(blocks)
    splits = 1
    ext_rows = 0 if ext is None else ext.shape[0]
    more = PAD if ext_rows > PAD else 0
    shapes = []
    if 1 in parts:
        rows = (length + more) // 2 + (0 if filt is None else filt.shape[0] // 2)
        shapes += [
            jax.ShapeDtypeStruct((length + more, channels), f32),
            jax.ShapeDtypeStruct((max(channels // HALF, 2), rows, LANES), bf16),
        ]
    if 0 in parts:
        shapes.append(jax.ShapeDtypeStruct((length, channels), f32))
    extra = [x for x in (ext, filt) if x is not None]
    rows = PAD + length + (2 * PAD if more else 0)
    return pl.pallas_call(
        functools.partial(project_kernel, len(blocks), parts, splits, ext_rows, filt is not None),
        in_specs=[pl.BlockSpec(memory_space=pltpu.SMEM)] + [ANY_SPEC] * (len(blocks) + 2 + len(extra)),
        out_specs=[ANY_SPEC] * len(shapes),
        out_shape=shapes,
        scratch_shapes=[pltpu.VMEM(x.shape, x.dtype) for x in shapes]
        + [
            pltpu.VMEM((len(parts), splits, width, channels // splits), bf16),
            pltpu.VMEM(taps.shape, f32),
            pltpu.VMEM((rows, width), bf16),
            pltpu.VMEM((rows, channels), f32),
            pltpu.VMEM((8, LANES) if filt is None else filt.shape, f32),
            pltpu.SemaphoreType.DMA((len(blocks) + 3,)),
            pltpu.SemaphoreType.DMA((len(parts), splits)),
            pltpu.SemaphoreType.DMA,
            pltpu.SemaphoreType.DMA((len(shapes),)),
        ],
        compiler_params=pltpu.CompilerParams(vmem_limit_bytes=BIG),
        cost_estimate=pl.CostEstimate(flops=cost, bytes_accessed=10**5, transcendentals=0),
        name="project",
    )(me, *blocks, weight, taps, *extra)


def coarse_forward(dev_count, x_ref, lane_ref, e_ref, step=64):
    count = dev_count
    half = count // 2
    low = lane_mask()
    sgn = jnp.where(low, 1.0, -1.0).astype(f32)

    def body(i, carry):
        rows = pl.ds(pl.multiple_of(i * step, step), step)
        x = [x_ref[s, rows, :].astype(f32) for s in range(count)]
        plus = [x[s] + x[count - s] for s in range(1, half)]
        minus = [x[s] - x[count - s] for s in range(1, half)]
        for k in range(count + 1):
            even = k % 2 == 0
            re = x[0]
            im = None
            mid = round(math.cos(math.pi * half * k / count))
            if mid:
                re = re + x[half] if mid > 0 else re - x[half]
            mid = round(math.sin(math.pi * half * k / count))
            if mid:
                im = -x[half] if mid > 0 else x[half]
            for s in range(1, half):
                c, d = math.cos(math.pi * s * k / count), math.sin(math.pi * s * k / count)
                if abs(c) > 1e-9:
                    re = re + c * (plus if even else minus)[s - 1]
                if abs(d) > 1e-9:
                    term = (-d) * (minus if even else plus)[s - 1]
                    im = term if im is None else im + term
            c, d = lane_ref[k, 0:1, :], lane_ref[k, 1:2, :]
            if im is None:
                re, im = re * c, re * (-d)
            else:
                re, im = re * c + im * d, im * c - re * d
            e_ref[k, rows, :LANES] = pltpu.roll(re, HALF, 1) + sgn * re
            e_ref[k, rows, LANES:] = sgn * pltpu.roll(im, HALF, 1) + im
        return carry

    lax.fori_loop(0, FINE // step, body, 0)


def coarse_inverse(dev_count, g_ref, y_ref, first, length, step=64):
    count = dev_count
    half = count // 2

    def body(i, carry):
        rows = pl.ds(pl.multiple_of(i * step, step), step)
        acc = {}

        def add(name, s, term):
            acc[name, s] = term if (name, s) not in acc else acc[name, s] + term

        for k in range(count + 1):
            even = k % 2 == 0
            re, im = g_ref[k, rows, :LANES], g_ref[k, rows, LANES:]
            add("first", 0, re)
            mid = round(math.cos(math.pi * half * k / count))
            if mid:
                add("mid", 0, re if mid > 0 else -re)
            mid = round(math.sin(math.pi * half * k / count))
            if mid:
                add("mid", 0, -im if mid > 0 else im)
            for s in range(1, half):
                c, d = math.cos(math.pi * s * k / count), math.sin(math.pi * s * k / count)
                if abs(c) > 1e-9:
                    add("a" if even else "b", s, c * re)
                if abs(d) > 1e-9:
                    add("b" if even else "a", -s, (-d) * im)
        y_ref[0, rows, :] = acc["first", 0].astype(bf16)
        y_ref[half, rows, :] = acc["mid", 0].astype(bf16)
        zero = jnp.zeros((step, LANES), f32)
        for s in range(1, half):
            same = acc.get(("a", s), zero)
            flip = acc.get(("b", s), zero)
            same_sin = acc.get(("a", -s), zero)
            flip_sin = acc.get(("b", -s), zero)
            total, diff = same + same_sin, flip + flip_sin
            y_ref[s, rows, :] = (total + diff).astype(bf16)
            y_ref[count - s, rows, :] = (total - diff).astype(bf16)
        return carry

    lax.fori_loop(first // step, (first + length) // step, body, 0)


def fine_forward(e, tr, ti, table):
    re, im = e[:, :LANES], e[:, LANES:]
    turned = jnp.concatenate([re * tr - im * ti, re * ti + im * tr], axis=1).astype(bf16)
    both = jnp.dot(table, turned, preferred_element_type=f32)
    return (
        both[:FINE, :LANES] - both[FINE:, LANES:],
        both[:FINE, LANES:] + both[FINE:, :LANES],
    )


def next_turn(turn_ref, step_ref):
    tr, ti = turn_ref[:, :LANES], turn_ref[:, LANES:]
    sr, si = step_ref[:, :LANES], step_ref[:, LANES:]
    turn_ref[:, :LANES] = tr * sr - ti * si
    turn_ref[:, LANES:] = tr * si + ti * sr


def filter_kernel(dev_count, x_any, *refs):
    const_hbm, h_ref = refs[:4], refs[4]
    x_ref, first_ref, step_ref, lane_ref, table_ref, e_ref, sem = refs[5:]
    turn_ref = first_ref
    rows = pl.ds(x_any.shape[1] - FINE, FINE)
    pairs = [(x_any.at[:, rows], x_ref)] + list(zip(const_hbm, (first_ref, step_ref, lane_ref, table_ref)))
    for copy in start_all((*pair, sem.at[i]) for i, pair in enumerate(pairs)):
        copy.wait()
    coarse_forward(dev_count, x_ref, lane_ref, e_ref)
    points = 4 * dev_count * FINE

    def body(k, carry):
        re, im = fine_forward(e_ref[k], turn_ref[:, :LANES], turn_ref[:, LANES:], table_ref[...])
        scale = jnp.where((k == 0) | (k == dev_count), 1.0 / points, 2.0 / points).astype(f32)
        h_ref[k, :, :LANES] = re * scale
        h_ref[k, :, LANES:] = im * scale
        next_turn(turn_ref, step_ref)
        return carry

    lax.fori_loop(0, dev_count + 1, body, 0, unroll=dev_count <= 8)


def merge_halves(dev_count, late_first, early_ref, late_ref, x_ref):
    pick = late_first == 1
    low = lane_mask()
    size = FINE // 2
    for s in range(dev_count):
        early, late = early_ref[s].astype(f32), late_ref[s].astype(f32)
        fixed = jnp.where(low, late[size:], early[: PAD // 2])
        early, late = jnp.concatenate([fixed, early[PAD // 2 :]], axis=0), late[:size]
        first, second = jnp.where(pick, late, early), jnp.where(pick, early, late)
        top, bot = pack_pair(jnp.concatenate([first, second], axis=0))
        x_ref[s, :size] = top
        x_ref[s, size:] = bot


def conv_kernel(dev_count, half_ref, early_any, late_any, h_hbm, *refs):
    const_hbm, y_any = refs[:4], refs[4]
    early_ref, late_ref, x_ref, h_ref, first_ref, step_ref, lane_ref, table_ref, e_ref, y_ref, sem, y_sem = refs[5:]
    turn_ref = first_ref
    pairs = [(early_any.at[:, pl.ds(0, FINE // 2)], early_ref), (late_any, late_ref), (const_hbm[2], lane_ref)]
    pairs += [(const_hbm[0], first_ref), (const_hbm[1], step_ref), (const_hbm[3], table_ref), (h_hbm, h_ref)]
    copies = start_all((*pair, sem.at[i]) for i, pair in enumerate(pairs))
    for copy in copies[:3]:
        copy.wait()
    merge_halves(dev_count, half_ref[0], early_ref, late_ref, x_ref)
    coarse_forward(dev_count, x_ref, lane_ref, e_ref)
    for copy in copies[3:]:
        copy.wait()
    sgn = jnp.where(lane_mask(), 1.0, -1.0).astype(f32)

    def body(k, carry):
        tr, ti = turn_ref[:, :LANES], turn_ref[:, LANES:]
        re, im = fine_forward(e_ref[k], tr, ti, table_ref[...])
        hr, hi = h_ref[k, :, :LANES], h_ref[k, :, LANES:]
        prod = jnp.concatenate([re * hr - im * hi, re * hi + im * hr], axis=1).astype(bf16)
        both = jnp.dot(table_ref[...], prod, preferred_element_type=f32)
        re = both[:FINE, :LANES] + both[FINE:, LANES:]
        im = both[:FINE, LANES:] - both[FINE:, :LANES]
        re, im = re * tr + im * ti, (im * tr - re * ti) * sgn
        re, im = pltpu.roll(re, HALF, 1) + sgn * re, pltpu.roll(im, HALF, 1) + sgn * im
        c, d = lane_ref[k, 0:1, :], lane_ref[k, 1:2, :]
        e_ref[k, :, :LANES] = re * c - im * d
        e_ref[k, :, LANES:] = re * d + im * c
        next_turn(turn_ref, step_ref)
        return carry

    lax.fori_loop(0, dev_count + 1, body, 0, unroll=dev_count <= 8)
    sends = []
    for i in range(2):
        rows = pl.ds(i * FINE // 2, FINE // 2)
        coarse_inverse(dev_count, e_ref, y_ref, i * FINE // 2, FINE // 2)
        sends += start_all([(y_ref.at[:, rows], y_any.at[:, rows], y_sem.at[i])])
    for send in sends:
        send.wait()


def tables(dev_count):
    points = 4 * dev_count * FINE
    fine = np.arange(FINE)
    first = np.exp(-2j * np.pi * fine * (2 * dev_count) / points)[:, None] * np.ones(HALF)
    ones = np.ones((FINE, HALF))
    step = np.exp(-2j * np.pi * fine / points)[:, None] * ones
    first = np.concatenate([ones, first.real, 0 * ones, first.imag], axis=1)
    step = np.concatenate([step.real, step.real, step.imag, -step.imag], axis=1)
    turn = 2 * np.pi * np.arange(dev_count + 1)[:, None] * np.ones(HALF) / (4 * dev_count)
    lane = np.stack(
        [
            np.concatenate([np.ones_like(turn), np.cos(turn)], axis=1),
            np.concatenate([np.zeros_like(turn), np.sin(turn)], axis=1),
        ],
        axis=1,
    )
    angle = -2 * np.pi * (fine[:, None] * fine[None, :] % FINE) / FINE
    table = np.concatenate([np.cos(angle), np.sin(angle)], axis=0)
    return (
        jnp.asarray(first, f32),
        jnp.asarray(step, f32),
        jnp.asarray(lane, f32),
        jnp.asarray(table, bf16),
    )


def const_scratch(consts):
    return [pltpu.VMEM(const.shape, const.dtype) for const in consts]


def filter_spectrum(x, consts):
    dev_count = x.shape[0]
    return pl.pallas_call(
        functools.partial(filter_kernel, dev_count),
        in_specs=[ANY_SPEC] + [HBM_SPEC] * 4,
        out_specs=VMEM_SPEC,
        out_shape=jax.ShapeDtypeStruct((dev_count + 1, FINE, 2 * LANES), f32),
        scratch_shapes=[pltpu.VMEM((dev_count, FINE, LANES), bf16)]
        + const_scratch(consts)
        + [pltpu.VMEM((dev_count + 1, FINE, 2 * LANES), f32), pltpu.SemaphoreType.DMA((5,))],
        compiler_params=pltpu.CompilerParams(vmem_limit_bytes=BIG),
        name="filter_spectrum",
    )(x, *consts)


def convolve(half, early, late, spectrum, consts):
    dev_count = early.shape[0]
    return pl.pallas_call(
        functools.partial(conv_kernel, dev_count),
        in_specs=[pl.BlockSpec(memory_space=pltpu.SMEM)] + [ANY_SPEC] * 2 + [HBM_SPEC] * 5,
        out_specs=ANY_SPEC,
        out_shape=jax.ShapeDtypeStruct((dev_count, FINE, LANES), bf16),
        scratch_shapes=[
            pltpu.VMEM((dev_count, FINE // 2, LANES), bf16),
            pltpu.VMEM(late.shape, bf16),
            pltpu.VMEM((dev_count, FINE, LANES), f32),
            pltpu.VMEM(spectrum.shape, f32),
        ]
        + const_scratch(consts)
        + [
            pltpu.VMEM((dev_count + 1, FINE, 2 * LANES), f32),
            pltpu.VMEM((dev_count, FINE, LANES), bf16),
            pltpu.SemaphoreType.DMA((7,)),
            pltpu.SemaphoreType.DMA((2,)),
        ],
        compiler_params=pltpu.CompilerParams(vmem_limit_bytes=BIG),
        name="convolve",
    )(half, early, late, spectrum, *consts)


def query_kernel(count, me_ref, *refs):
    blocks, refs = refs[:count], refs[count:]
    halo_any, w_hbm, tap_hbm, early_any, late_any, skip_hbm, out_any = refs[:7]
    x_ref, w_ref, tap_ref, early_ref, late_ref, skip_ref, rows_ref, out_ref, sem, out_sem = refs[7:]
    each = blocks[0].shape[0]
    length = each * count
    half = length // 2
    early_at = me_ref[1]

    ahead = pl.ds(pl.multiple_of((1 - early_at) * PAD, PAD), PAD)
    pairs = [(halo_any.at[ahead], x_ref.at[pl.ds(0, PAD)])]
    for mask, block in enumerate(blocks):
        first = pl.multiple_of(PAD + (me_ref[0] ^ mask) * each, 16)
        pairs.append((block, x_ref.at[pl.ds(first, each)]))
    pairs += [(w_hbm.at[0], w_ref), (tap_hbm, tap_ref), (skip_hbm, skip_ref)]
    pairs += [(early_any, early_ref), (late_any, late_ref)]
    for copy in start_all((*pair, sem.at[i]) for i, pair in enumerate(pairs)):
        copy.wait()
    rows_ref[...] = jnp.dot(x_ref[...], w_ref[...], preferred_element_type=f32)
    total = tap_ref[0, 0:1] * rows_ref[PAD:]
    for lag in (1, 2):
        total += tap_ref[lag, 0:1] * rows_ref[PAD - lag : PAD - lag + length]
    out_ref[0] = total
    early_ref[:PAD] = late_ref[half:]
    for at, g_ref in ((early_at, early_ref), (1 - early_at, late_ref)):
        rows = pl.ds(pl.multiple_of(at * half, half), half)
        out_ref[1, rows, :] = out_ref[0, rows, :] * (skip_ref[...] * g_ref[:half])
    start_all([(out_ref, out_any, out_sem)])[0].wait()


def query_terms(me, blocks, halo, weight, taps, early, late, skip):
    _, width, channels = weight.shape
    length = blocks[0].shape[0] * len(blocks)
    skip = skip.reshape(1, channels)
    return pl.pallas_call(
        functools.partial(query_kernel, len(blocks)),
        in_specs=[pl.BlockSpec(memory_space=pltpu.SMEM)] + [ANY_SPEC] * (len(blocks) + 6),
        out_specs=ANY_SPEC,
        out_shape=jax.ShapeDtypeStruct((2, length, channels), f32),
        scratch_shapes=[
            pltpu.VMEM((PAD + length, width), bf16),
            pltpu.VMEM((width, channels), bf16),
            pltpu.VMEM(taps.shape, f32),
            pltpu.VMEM(early.shape, f32),
            pltpu.VMEM(late.shape, f32),
            pltpu.VMEM(skip.shape, f32),
            pltpu.VMEM((PAD + length, channels), f32),
            pltpu.VMEM((2, length, channels), f32),
            pltpu.SemaphoreType.DMA((len(blocks) + 6,)),
            pltpu.SemaphoreType.DMA,
        ],
        compiler_params=pltpu.CompilerParams(vmem_limit_bytes=BIG),
        cost_estimate=pl.CostEstimate(flops=COST[2], bytes_accessed=10**5, transcendentals=0),
        name="query_terms",
    )(me, *blocks, halo, weight, taps, early, late, skip)


def finish(conv, terms):
    _, length, channels = terms.shape
    tiles = channels // LANES

    def kernel(c_ref, term_any, out_any, term_ref, out_ref, in_sem, sem):
        cols = [pl.ds(i * LANES, LANES) for i in range(tiles)]
        loads = start_all((term_any.at[:, :, cols[i]], term_ref.at[i], in_sem.at[i]) for i in range(tiles))
        sends = []
        for i in range(tiles):
            top, bot = unpack_pair(c_ref[2 * i].astype(f32), c_ref[2 * i + 1].astype(f32))
            loads[i].wait()
            for j, part in enumerate((top, bot)):
                rows = slice(j * FINE, (j + 1) * FINE)
                out_ref[i, rows] = (term_ref[i, 0, rows] * part + term_ref[i, 1, rows]).astype(bf16)
            sends += start_all([(out_ref.at[i], out_any.at[:, cols[i]], sem.at[i])])
        for send in sends:
            send.wait()

    return pl.pallas_call(
        kernel,
        in_specs=[VMEM_SPEC, ANY_SPEC],
        out_specs=ANY_SPEC,
        out_shape=jax.ShapeDtypeStruct((length, channels), bf16),
        scratch_shapes=[
            pltpu.VMEM((tiles, 2, length, LANES), f32),
            pltpu.VMEM((tiles, length, LANES), bf16),
            pltpu.SemaphoreType.DMA((tiles,)),
            pltpu.SemaphoreType.DMA((tiles,)),
        ],
        compiler_params=pltpu.CompilerParams(vmem_limit_bytes=FINISH_LIMIT * 1024 * 1024),
        name="finish",
    )(conv, terms)


def local(tokens, norm_gain, in_weight, short_weight, long_filter, skip_gain):
    dev_count = lax.axis_size("context")
    tensor_count = lax.axis_size("tensor")
    channels = in_weight.shape[2]
    packed = channels // dev_count == HALF
    consts = tables(dev_count)
    weight = jnp.transpose(in_weight, (1, 0, 2))
    exchange = functools.partial(
        lax.all_to_all, axis_name="context", split_axis=0, concat_axis=0, tiled=True
    )

    me = lax.axis_index("tensor").astype(jnp.int32)
    mid = tensor_count // 2
    half = (me // mid).reshape(1)
    place = (me % mid).reshape(1)

    def swap(x, bit):
        return lax.ppermute(x, "tensor", [(i, i ^ bit) for i in range(tensor_count)])

    def gathered(block):
        blocks = {0: block}
        bit = mid // 2
        while bit:
            for mask in list(blocks):
                blocks[mask | bit] = swap(blocks[mask], bit)
            bit //= 2
        return [blocks[mask] for mask in range(mid)]

    normed, tail = norm_rows(tokens, norm_gain)
    crossed = swap(normed, mid)
    early_blocks = gathered(normed)

    early_blocks, tail = lax.optimization_barrier((early_blocks, tail))
    late_halo = jnp.zeros_like(tail)
    for j in range(mid):
        pairs = [(c * tensor_count - 1, c * tensor_count + mid + j) for c in range(1, dev_count)]
        pairs += [(c * tensor_count + mid - 1, c * tensor_count + j) for c in range(dev_count)]
        late_halo = late_halo + lax.ppermute(tail, ("context", "tensor"), pairs)
    head = sum(jnp.where(place == mask, block[:PAD], 0) for mask, block in enumerate(early_blocks))
    packs = None
    if packed:
        early_gated, packs = project(
            (1, 2), place, early_blocks, weight, short_weight, COST[0], filt=long_filter
        )
    else:
        early_gated, _ = project((1, 2), place, early_blocks, weight, short_weight, COST[0])
        packs = [pack_any(rows, dev_count) for rows in (early_gated, long_filter)]
        packs = jnp.concatenate(packs, axis=1)
    packs, late_halo = lax.optimization_barrier((packs, late_halo))
    early_halo = swap(late_halo, mid)
    early_sent = exchange(packs)
    crossed, _ = lax.optimization_barrier((crossed, packs))
    late_blocks = gathered(crossed)
    gap = jnp.zeros((PAD - TAIL, tail.shape[1]), bf16)
    late_ext = jnp.concatenate([gap, late_halo, gap, early_halo, head], axis=0)
    late_gated, packs = project((1, 2), place, late_blocks, weight, short_weight, COST[1], ext=late_ext)
    if not packed:
        rows = late_gated.shape[0] - PAD
        packs = [pack_any(late_gated[:rows], dev_count), pack_any(late_gated[rows:], dev_count)]
        packs = jnp.concatenate(packs, axis=1)
    late_sent = exchange(packs)
    spectrum = filter_spectrum(early_sent, consts)
    conv = exchange(convolve(half, early_sent, late_sent, spectrum, consts))
    terms = query_terms(
        jnp.concatenate([me.reshape(1), half]),
        early_blocks + late_blocks,
        late_ext,
        weight,
        short_weight,
        early_gated,
        late_gated,
        skip_gain,
    )
    if packed:
        return finish(conv, terms)
    each = channels // dev_count
    conv = conv.reshape(dev_count, FINE, 2, HALF)[..., :each]
    conv = jnp.transpose(conv, (2, 1, 0, 3)).reshape(2 * FINE, channels).astype(f32)
    return (terms[0] * conv + terms[1]).astype(bf16)


def solution(mesh):
    return jax.shard_map(
        local,
        mesh=mesh,
        in_specs=(
            P(("context", "tensor"), None),
            P(),
            P(None, None, "tensor"),
            P(None, None, "tensor"),
            P("context", "tensor"),
            P("tensor"),
        ),
        out_specs=P("context", "tensor"),
        check_vma=False,
    )
```

```python
import functools
import math

import jax
import jax.numpy as jnp
import numpy as np
from jax import lax
from jax.experimental import pallas as pl
from jax.experimental.pallas import tpu as pltpu
from jax.sharding import PartitionSpec as P

eps = 1e-06

FINE = 256
HALF = 64
LANES = 2 * HALF
TAIL = 8
PAD = 16
BIG = 60 * 1024 * 1024
FINISH_LIMIT = 53
COST = (10**8, 10**8, 10**8)

VMEM_SPEC = pl.BlockSpec(memory_space=pltpu.VMEM)
HBM_SPEC = pl.BlockSpec(memory_space=pltpu.HBM)
ANY_SPEC = pl.BlockSpec(memory_space=pl.ANY)

f32 = jnp.float32
bf16 = jnp.bfloat16


def lane_mask():
    return lax.broadcasted_iota(jnp.int32, (1, LANES), 1) < HALF


def pack_pair(tile):
    low = lane_mask()
    rows = tile.shape[0] // 2
    top, bot = tile[:rows], tile[rows:]
    return (
        jnp.where(low, top, pltpu.roll(bot, HALF, 1)),
        jnp.where(low, pltpu.roll(top, HALF, 1), bot),
    )


def unpack_pair(first, second):
    low = lane_mask()
    return (
        jnp.where(low, first, pltpu.roll(second, HALF, 1)),
        jnp.where(low, pltpu.roll(first, HALF, 1), second),
    )


def start_all(copies):
    copies = [pltpu.make_async_copy(*copy) for copy in copies]
    for copy in copies:
        copy.start()
    return copies


def pack_any(rows, dev_count):
    length, channels = rows.shape
    each = channels // dev_count
    blocks = rows.astype(bf16).reshape(2, length // 2, dev_count, each)
    blocks = jnp.transpose(blocks, (2, 1, 0, 3))
    blocks = jnp.pad(blocks, ((0, 0), (0, 0), (0, 0), (0, HALF - each)))
    return blocks.reshape(dev_count, length // 2, LANES)


def norm_rows(tokens, gain):
    rows, width = tokens.shape
    step = min(64, rows)

    def kernel(tok_hbm, gain_hbm, out_any, tail_any, tok_ref, gain_ref, out_ref, sem, out_sem):
        parts = [pl.ds(i * step, step) for i in range(rows // step)]
        copies = start_all(
            [(gain_hbm, gain_ref, sem.at[len(parts)])]
            + [(tok_hbm.at[part], tok_ref.at[part], sem.at[i]) for i, part in enumerate(parts)]
        )
        copies[0].wait()
        sends = []
        for i, part in enumerate(parts):
            copies[1 + i].wait()
            values = tok_ref[part, :].astype(f32)
            inv_rms = lax.rsqrt(jnp.mean(values * values, axis=1, keepdims=True) + eps)
            out_ref[part, :] = (values * inv_rms * gain_ref[...]).astype(bf16)
            sends += start_all([(out_ref.at[part], out_any.at[part], out_sem.at[i])])
        sends += start_all([(out_ref.at[pl.ds(rows - TAIL, TAIL)], tail_any, out_sem.at[len(parts)])])
        for send in sends:
            send.wait()

    return pl.pallas_call(
        kernel,
        in_specs=[HBM_SPEC] * 2,
        out_specs=[ANY_SPEC] * 2,
        out_shape=[jax.ShapeDtypeStruct((rows, width), bf16), jax.ShapeDtypeStruct((TAIL, width), bf16)],
        scratch_shapes=[
            pltpu.VMEM((rows, width), bf16),
            pltpu.VMEM((1, width), f32),
            pltpu.VMEM((rows, width), bf16),
            pltpu.SemaphoreType.DMA((rows // step + 1,)),
            pltpu.SemaphoreType.DMA((rows // step + 1,)),
        ],
        compiler_params=pltpu.CompilerParams(vmem_limit_bytes=BIG),
        name="norm_rows",
    )(tokens, gain.reshape(1, width))


def pack_into(p_ref, at, rows_ref, first, length):
    rows = pl.ds(at, length // 2)
    for i in range(p_ref.shape[0] // 2):
        one, two = pack_pair(rows_ref[first : first + length, i * LANES : (i + 1) * LANES])
        p_ref[2 * i, rows, :] = one.astype(bf16)
        p_ref[2 * i + 1, rows, :] = two.astype(bf16)


def project_kernel(count, parts, splits, ext_rows, with_filter, me_ref, *refs):
    blocks, refs = refs[:count], refs[count:]
    w_hbm, tap_hbm = refs[:2]
    extra, refs = refs[2 : 2 + bool(ext_rows) + with_filter], refs[2 + bool(ext_rows) + with_filter :]
    number = 2 * (1 in parts) + (0 in parts)
    out_any, outs, refs = refs[:number], refs[number : 2 * number], refs[2 * number :]
    w_ref, tap_ref, x_ref, rows_ref, filt_ref, sem, w_sem, tap_sem, out_sem = refs

    def send(i):
        return start_all([(outs[i], out_any[i], out_sem.at[i])])

    each = blocks[0].shape[0]
    length = each * count
    end = PAD + length
    width, channels = x_ref.shape[1], rows_ref.shape[1]
    each_cols = channels // splits

    sources = [(tap_hbm, tap_ref, tap_sem)]
    for mask, block in enumerate(blocks):
        first = pl.multiple_of(PAD + (me_ref[0] ^ mask) * each, 16)
        sources.append((block, x_ref.at[pl.ds(first, each)], sem.at[mask]))
    if ext_rows:
        sources.append((extra[0].at[pl.ds(0, PAD)], x_ref.at[pl.ds(0, PAD)], sem.at[count]))
    else:
        x_ref[:PAD] = jnp.zeros((PAD, width), bf16)
    if ext_rows > PAD:
        rest = ext_rows - PAD
        sources.append((extra[0].at[pl.ds(PAD, rest)], x_ref.at[pl.ds(end, rest)], sem.at[count + 1]))
    if with_filter:
        filt_load = start_all([(extra[-1], filt_ref, sem.at[count + 2])])[0]
    waits = start_all(sources)
    loads = {}
    for at, s in enumerate(parts):
        for i in range(splits):
            cols = pl.ds(i * each_cols, each_cols)
            loads[s, i] = start_all([(w_hbm.at[s, :, cols], w_ref.at[at, i], w_sem.at[at, i])])[0]
    if with_filter:
        filt_load.wait()
        pack_into(outs[1], length // 2, filt_ref, 0, filt_ref.shape[0])
    for wait in waits:
        wait.wait()

    def mixed(s):
        at = parts.index(s)
        for i in range(splits):
            loads[s, i].wait()
            cols = slice(i * each_cols, (i + 1) * each_cols)
            rows_ref[:, cols] = jnp.dot(x_ref[...], w_ref[at, i], preferred_element_type=f32)
        spans = [(PAD, length)]
        if ext_rows > PAD:
            spans.append((end + PAD, PAD))
        results = []
        for first, size in spans:
            total = tap_ref[0, s : s + 1] * rows_ref[first : first + size]
            for lag in (1, 2):
                total += tap_ref[lag, s : s + 1] * rows_ref[first - lag : first - lag + size]
            results.append(total)
        return results

    if 1 in parts:
        g_ref, p_ref = outs[:2]
        spans = [slice(0, length), slice(length, length + PAD)]
        for span, key in zip(spans, mixed(1)):
            g_ref[span, :] = key
        for span, value in zip(spans, mixed(2)):
            g_ref[span, :] *= value
        sends = send(0)
        pack_into(p_ref, 0, g_ref, 0, length)
        if ext_rows > PAD:
            pack_into(p_ref, length // 2, g_ref, length, PAD)
        sends += send(1)
    if 0 in parts:
        outs[-1][...] = mixed(0)[0]
        sends = (sends if 1 in parts else []) + send(number - 1)
    for copy in sends:
        copy.wait()


def project(parts, me, blocks, weight, taps, cost, ext=None, filt=None):
    _, width, channels = weight.shape
    length = blocks[0].shape[0] * len(blocks)
    splits = 1
    ext_rows = 0 if ext is None else ext.shape[0]
    more = PAD if ext_rows > PAD else 0
    shapes = []
    if 1 in parts:
        rows = (length + more) // 2 + (0 if filt is None else filt.shape[0] // 2)
        shapes += [
            jax.ShapeDtypeStruct((length + more, channels), f32),
            jax.ShapeDtypeStruct((max(channels // HALF, 2), rows, LANES), bf16),
        ]
    if 0 in parts:
        shapes.append(jax.ShapeDtypeStruct((length, channels), f32))
    extra = [x for x in (ext, filt) if x is not None]
    rows = PAD + length + (2 * PAD if more else 0)
    return pl.pallas_call(
        functools.partial(project_kernel, len(blocks), parts, splits, ext_rows, filt is not None),
        in_specs=[pl.BlockSpec(memory_space=pltpu.SMEM)] + [ANY_SPEC] * (len(blocks) + 2 + len(extra)),
        out_specs=[ANY_SPEC] * len(shapes),
        out_shape=shapes,
        scratch_shapes=[pltpu.VMEM(x.shape, x.dtype) for x in shapes]
        + [
            pltpu.VMEM((len(parts), splits, width, channels // splits), bf16),
            pltpu.VMEM(taps.shape, f32),
            pltpu.VMEM((rows, width), bf16),
            pltpu.VMEM((rows, channels), f32),
            pltpu.VMEM((8, LANES) if filt is None else filt.shape, f32),
            pltpu.SemaphoreType.DMA((len(blocks) + 3,)),
            pltpu.SemaphoreType.DMA((len(parts), splits)),
            pltpu.SemaphoreType.DMA,
            pltpu.SemaphoreType.DMA((len(shapes),)),
        ],
        compiler_params=pltpu.CompilerParams(vmem_limit_bytes=BIG),
        cost_estimate=pl.CostEstimate(flops=cost, bytes_accessed=10**5, transcendentals=0),
        name="project",
    )(me, *blocks, weight, taps, *extra)


def coarse_forward(dev_count, x_ref, lane_ref, e_ref, step=64):
    count = dev_count
    half = count // 2
    low = lane_mask()
    sgn = jnp.where(low, 1.0, -1.0).astype(f32)

    def body(i, carry):
        rows = pl.ds(pl.multiple_of(i * step, step), step)
        x = [x_ref[s, rows, :].astype(f32) for s in range(count)]
        plus = [x[s] + x[count - s] for s in range(1, half)]
        minus = [x[s] - x[count - s] for s in range(1, half)]
        for k in range(count + 1):
            even = k % 2 == 0
            re = x[0]
            im = None
            mid = round(math.cos(math.pi * half * k / count))
            if mid:
                re = re + x[half] if mid > 0 else re - x[half]
            mid = round(math.sin(math.pi * half * k / count))
            if mid:
                im = -x[half] if mid > 0 else x[half]
            for s in range(1, half):
                c, d = math.cos(math.pi * s * k / count), math.sin(math.pi * s * k / count)
                if abs(c) > 1e-9:
                    re = re + c * (plus if even else minus)[s - 1]
                if abs(d) > 1e-9:
                    term = (-d) * (minus if even else plus)[s - 1]
                    im = term if im is None else im + term
            c, d = lane_ref[k, 0:1, :], lane_ref[k, 1:2, :]
            if im is None:
                re, im = re * c, re * (-d)
            else:
                re, im = re * c + im * d, im * c - re * d
            e_ref[k, rows, :LANES] = pltpu.roll(re, HALF, 1) + sgn * re
            e_ref[k, rows, LANES:] = sgn * pltpu.roll(im, HALF, 1) + im
        return carry

    lax.fori_loop(0, FINE // step, body, 0)


def coarse_inverse(dev_count, g_ref, y_ref, first, length, step=64):
    count = dev_count
    half = count // 2

    def body(i, carry):
        rows = pl.ds(pl.multiple_of(i * step, step), step)
        acc = {}

        def add(name, s, term):
            acc[name, s] = term if (name, s) not in acc else acc[name, s] + term

        for k in range(count + 1):
            even = k % 2 == 0
            re, im = g_ref[k, rows, :LANES], g_ref[k, rows, LANES:]
            add("first", 0, re)
            mid = round(math.cos(math.pi * half * k / count))
            if mid:
                add("mid", 0, re if mid > 0 else -re)
            mid = round(math.sin(math.pi * half * k / count))
            if mid:
                add("mid", 0, -im if mid > 0 else im)
            for s in range(1, half):
                c, d = math.cos(math.pi * s * k / count), math.sin(math.pi * s * k / count)
                if abs(c) > 1e-9:
                    add("a" if even else "b", s, c * re)
                if abs(d) > 1e-9:
                    add("b" if even else "a", -s, (-d) * im)
        y_ref[0, rows, :] = acc["first", 0].astype(bf16)
        y_ref[half, rows, :] = acc["mid", 0].astype(bf16)
        zero = jnp.zeros((step, LANES), f32)
        for s in range(1, half):
            same = acc.get(("a", s), zero)
            flip = acc.get(("b", s), zero)
            same_sin = acc.get(("a", -s), zero)
            flip_sin = acc.get(("b", -s), zero)
            total, diff = same + same_sin, flip + flip_sin
            y_ref[s, rows, :] = (total + diff).astype(bf16)
            y_ref[count - s, rows, :] = (total - diff).astype(bf16)
        return carry

    lax.fori_loop(first // step, (first + length) // step, body, 0)


def fine_forward(e, tr, ti, table):
    re, im = e[:, :LANES], e[:, LANES:]
    turned = jnp.concatenate([re * tr - im * ti, re * ti + im * tr], axis=1).astype(bf16)
    both = jnp.dot(table, turned, preferred_element_type=f32)
    return (
        both[:FINE, :LANES] - both[FINE:, LANES:],
        both[:FINE, LANES:] + both[FINE:, :LANES],
    )


def next_turn(turn_ref, step_ref):
    tr, ti = turn_ref[:, :LANES], turn_ref[:, LANES:]
    sr, si = step_ref[:, :LANES], step_ref[:, LANES:]
    turn_ref[:, :LANES] = tr * sr - ti * si
    turn_ref[:, LANES:] = tr * si + ti * sr


def filter_kernel(dev_count, x_any, *refs):
    const_hbm, h_ref = refs[:4], refs[4]
    x_ref, first_ref, step_ref, lane_ref, table_ref, e_ref, sem = refs[5:]
    turn_ref = first_ref
    rows = pl.ds(x_any.shape[1] - FINE, FINE)
    pairs = [(x_any.at[:, rows], x_ref)] + list(zip(const_hbm, (first_ref, step_ref, lane_ref, table_ref)))
    for copy in start_all((*pair, sem.at[i]) for i, pair in enumerate(pairs)):
        copy.wait()
    coarse_forward(dev_count, x_ref, lane_ref, e_ref)
    points = 4 * dev_count * FINE

    def body(k, carry):
        re, im = fine_forward(e_ref[k], turn_ref[:, :LANES], turn_ref[:, LANES:], table_ref[...])
        scale = jnp.where((k == 0) | (k == dev_count), 1.0 / points, 2.0 / points).astype(f32)
        h_ref[k, :, :LANES] = re * scale
        h_ref[k, :, LANES:] = im * scale
        next_turn(turn_ref, step_ref)
        return carry

    lax.fori_loop(0, dev_count + 1, body, 0, unroll=dev_count <= 8)


def merge_halves(dev_count, late_first, early_ref, late_ref, x_ref):
    pick = late_first == 1
    low = lane_mask()
    size = FINE // 2
    for s in range(dev_count):
        early, late = early_ref[s].astype(f32), late_ref[s].astype(f32)
        fixed = jnp.where(low, late[size:], early[: PAD // 2])
        early, late = jnp.concatenate([fixed, early[PAD // 2 :]], axis=0), late[:size]
        first, second = jnp.where(pick, late, early), jnp.where(pick, early, late)
        top, bot = pack_pair(jnp.concatenate([first, second], axis=0))
        x_ref[s, :size] = top
        x_ref[s, size:] = bot


def conv_kernel(dev_count, half_ref, early_any, late_any, h_hbm, *refs):
    const_hbm, y_any = refs[:4], refs[4]
    early_ref, late_ref, x_ref, h_ref, first_ref, step_ref, lane_ref, table_ref, e_ref, y_ref, sem, y_sem = refs[5:]
    turn_ref = first_ref
    pairs = [(early_any.at[:, pl.ds(0, FINE // 2)], early_ref), (late_any, late_ref), (const_hbm[2], lane_ref)]
    pairs += [(const_hbm[0], first_ref), (const_hbm[1], step_ref), (const_hbm[3], table_ref), (h_hbm, h_ref)]
    copies = start_all((*pair, sem.at[i]) for i, pair in enumerate(pairs))
    for copy in copies[:3]:
        copy.wait()
    merge_halves(dev_count, half_ref[0], early_ref, late_ref, x_ref)
    coarse_forward(dev_count, x_ref, lane_ref, e_ref)
    for copy in copies[3:]:
        copy.wait()
    sgn = jnp.where(lane_mask(), 1.0, -1.0).astype(f32)

    def body(k, carry):
        tr, ti = turn_ref[:, :LANES], turn_ref[:, LANES:]
        re, im = fine_forward(e_ref[k], tr, ti, table_ref[...])
        hr, hi = h_ref[k, :, :LANES], h_ref[k, :, LANES:]
        prod = jnp.concatenate([re * hr - im * hi, re * hi + im * hr], axis=1).astype(bf16)
        both = jnp.dot(table_ref[...], prod, preferred_element_type=f32)
        re = both[:FINE, :LANES] + both[FINE:, LANES:]
        im = both[:FINE, LANES:] - both[FINE:, :LANES]
        re, im = re * tr + im * ti, (im * tr - re * ti) * sgn
        re, im = pltpu.roll(re, HALF, 1) + sgn * re, pltpu.roll(im, HALF, 1) + sgn * im
        c, d = lane_ref[k, 0:1, :], lane_ref[k, 1:2, :]
        e_ref[k, :, :LANES] = re * c - im * d
        e_ref[k, :, LANES:] = re * d + im * c
        next_turn(turn_ref, step_ref)
        return carry

    lax.fori_loop(0, dev_count + 1, body, 0, unroll=dev_count <= 8)
    sends = []
    size = FINE // 4
    for i in range(4):
        rows = pl.ds(i * size, size)
        coarse_inverse(dev_count, e_ref, y_ref, i * size, size)
        sends += start_all([(y_ref.at[:, rows], y_any.at[:, rows], y_sem.at[i])])
    for send in sends:
        send.wait()


def tables(dev_count):
    points = 4 * dev_count * FINE
    fine = np.arange(FINE)
    first = np.exp(-2j * np.pi * fine * (2 * dev_count) / points)[:, None] * np.ones(HALF)
    ones = np.ones((FINE, HALF))
    step = np.exp(-2j * np.pi * fine / points)[:, None] * ones
    first = np.concatenate([ones, first.real, 0 * ones, first.imag], axis=1)
    step = np.concatenate([step.real, step.real, step.imag, -step.imag], axis=1)
    turn = 2 * np.pi * np.arange(dev_count + 1)[:, None] * np.ones(HALF) / (4 * dev_count)
    lane = np.stack(
        [
            np.concatenate([np.ones_like(turn), np.cos(turn)], axis=1),
            np.concatenate([np.zeros_like(turn), np.sin(turn)], axis=1),
        ],
        axis=1,
    )
    angle = -2 * np.pi * (fine[:, None] * fine[None, :] % FINE) / FINE
    table = np.concatenate([np.cos(angle), np.sin(angle)], axis=0)
    return (
        jnp.asarray(first, f32),
        jnp.asarray(step, f32),
        jnp.asarray(lane, f32),
        jnp.asarray(table, bf16),
    )


def const_scratch(consts):
    return [pltpu.VMEM(const.shape, const.dtype) for const in consts]


def filter_spectrum(x, consts):
    dev_count = x.shape[0]
    return pl.pallas_call(
        functools.partial(filter_kernel, dev_count),
        in_specs=[ANY_SPEC] + [HBM_SPEC] * 4,
        out_specs=VMEM_SPEC,
        out_shape=jax.ShapeDtypeStruct((dev_count + 1, FINE, 2 * LANES), f32),
        scratch_shapes=[pltpu.VMEM((dev_count, FINE, LANES), bf16)]
        + const_scratch(consts)
        + [pltpu.VMEM((dev_count + 1, FINE, 2 * LANES), f32), pltpu.SemaphoreType.DMA((5,))],
        compiler_params=pltpu.CompilerParams(vmem_limit_bytes=BIG),
        name="filter_spectrum",
    )(x, *consts)


def convolve(half, early, late, spectrum, consts):
    dev_count = early.shape[0]
    return pl.pallas_call(
        functools.partial(conv_kernel, dev_count),
        in_specs=[pl.BlockSpec(memory_space=pltpu.SMEM)] + [ANY_SPEC] * 2 + [HBM_SPEC] * 5,
        out_specs=ANY_SPEC,
        out_shape=jax.ShapeDtypeStruct((dev_count, FINE, LANES), bf16),
        scratch_shapes=[
            pltpu.VMEM((dev_count, FINE // 2, LANES), bf16),
            pltpu.VMEM(late.shape, bf16),
            pltpu.VMEM((dev_count, FINE, LANES), f32),
            pltpu.VMEM(spectrum.shape, f32),
        ]
        + const_scratch(consts)
        + [
            pltpu.VMEM((dev_count + 1, FINE, 2 * LANES), f32),
            pltpu.VMEM((dev_count, FINE, LANES), bf16),
            pltpu.SemaphoreType.DMA((7,)),
            pltpu.SemaphoreType.DMA((4,)),
        ],
        compiler_params=pltpu.CompilerParams(vmem_limit_bytes=BIG),
        name="convolve",
    )(half, early, late, spectrum, *consts)


def query_kernel(count, me_ref, *refs):
    blocks, refs = refs[:count], refs[count:]
    halo_any, w_hbm, tap_hbm, early_any, late_any, skip_hbm, out_any = refs[:7]
    x_ref, w_ref, tap_ref, early_ref, late_ref, skip_ref, rows_ref, out_ref, sem, out_sem = refs[7:]
    each = blocks[0].shape[0]
    length = each * count
    half = length // 2
    early_at = me_ref[1]

    ahead = pl.ds(pl.multiple_of((1 - early_at) * PAD, PAD), PAD)
    pairs = [(halo_any.at[ahead], x_ref.at[pl.ds(0, PAD)])]
    for mask, block in enumerate(blocks):
        first = pl.multiple_of(PAD + (me_ref[0] ^ mask) * each, 16)
        pairs.append((block, x_ref.at[pl.ds(first, each)]))
    pairs += [(w_hbm.at[0], w_ref), (tap_hbm, tap_ref), (skip_hbm, skip_ref)]
    pairs += [(early_any, early_ref), (late_any, late_ref)]
    for copy in start_all((*pair, sem.at[i]) for i, pair in enumerate(pairs)):
        copy.wait()
    rows_ref[...] = jnp.dot(x_ref[...], w_ref[...], preferred_element_type=f32)
    total = tap_ref[0, 0:1] * rows_ref[PAD:]
    for lag in (1, 2):
        total += tap_ref[lag, 0:1] * rows_ref[PAD - lag : PAD - lag + length]
    out_ref[0] = total
    early_ref[:PAD] = late_ref[half:]
    for at, g_ref in ((early_at, early_ref), (1 - early_at, late_ref)):
        rows = pl.ds(pl.multiple_of(at * half, half), half)
        out_ref[1, rows, :] = out_ref[0, rows, :] * (skip_ref[...] * g_ref[:half])
    start_all([(out_ref, out_any, out_sem)])[0].wait()


def query_terms(me, blocks, halo, weight, taps, early, late, skip):
    _, width, channels = weight.shape
    length = blocks[0].shape[0] * len(blocks)
    skip = skip.reshape(1, channels)
    return pl.pallas_call(
        functools.partial(query_kernel, len(blocks)),
        in_specs=[pl.BlockSpec(memory_space=pltpu.SMEM)] + [ANY_SPEC] * (len(blocks) + 6),
        out_specs=ANY_SPEC,
        out_shape=jax.ShapeDtypeStruct((2, length, channels), f32),
        scratch_shapes=[
            pltpu.VMEM((PAD + length, width), bf16),
            pltpu.VMEM((width, channels), bf16),
            pltpu.VMEM(taps.shape, f32),
            pltpu.VMEM(early.shape, f32),
            pltpu.VMEM(late.shape, f32),
            pltpu.VMEM(skip.shape, f32),
            pltpu.VMEM((PAD + length, channels), f32),
            pltpu.VMEM((2, length, channels), f32),
            pltpu.SemaphoreType.DMA((len(blocks) + 6,)),
            pltpu.SemaphoreType.DMA,
        ],
        compiler_params=pltpu.CompilerParams(vmem_limit_bytes=BIG),
        cost_estimate=pl.CostEstimate(flops=COST[2], bytes_accessed=10**5, transcendentals=0),
        name="query_terms",
    )(me, *blocks, halo, weight, taps, early, late, skip)


def finish(conv, terms):
    _, length, channels = terms.shape
    tiles = channels // LANES

    def kernel(c_ref, term_any, out_any, term_ref, out_ref, in_sem, sem):
        cols = [pl.ds(i * LANES, LANES) for i in range(tiles)]
        loads = start_all((term_any.at[:, :, cols[i]], term_ref.at[i], in_sem.at[i]) for i in range(tiles))
        sends = []
        for i in range(tiles):
            top, bot = unpack_pair(c_ref[2 * i].astype(f32), c_ref[2 * i + 1].astype(f32))
            loads[i].wait()
            for j, part in enumerate((top, bot)):
                rows = slice(j * FINE, (j + 1) * FINE)
                out_ref[i, rows] = (term_ref[i, 0, rows] * part + term_ref[i, 1, rows]).astype(bf16)
            sends += start_all([(out_ref.at[i], out_any.at[:, cols[i]], sem.at[i])])
        for send in sends:
            send.wait()

    return pl.pallas_call(
        kernel,
        in_specs=[VMEM_SPEC, ANY_SPEC],
        out_specs=ANY_SPEC,
        out_shape=jax.ShapeDtypeStruct((length, channels), bf16),
        scratch_shapes=[
            pltpu.VMEM((tiles, 2, length, LANES), f32),
            pltpu.VMEM((tiles, length, LANES), bf16),
            pltpu.SemaphoreType.DMA((tiles,)),
            pltpu.SemaphoreType.DMA((tiles,)),
        ],
        compiler_params=pltpu.CompilerParams(vmem_limit_bytes=FINISH_LIMIT * 1024 * 1024),
        name="finish",
    )(conv, terms)


def local(tokens, norm_gain, in_weight, short_weight, long_filter, skip_gain):
    dev_count = lax.axis_size("context")
    tensor_count = lax.axis_size("tensor")
    channels = in_weight.shape[2]
    packed = channels // dev_count == HALF
    consts = tables(dev_count)
    weight = jnp.transpose(in_weight, (1, 0, 2))
    exchange = functools.partial(
        lax.all_to_all, axis_name="context", split_axis=0, concat_axis=0, tiled=True
    )

    me = lax.axis_index("tensor").astype(jnp.int32)
    mid = tensor_count // 2
    half = (me // mid).reshape(1)
    place = (me % mid).reshape(1)

    def swap(x, bit):
        return lax.ppermute(x, "tensor", [(i, i ^ bit) for i in range(tensor_count)])

    def gathered(block):
        blocks = {0: block}
        bit = mid // 2
        while bit:
            for mask in list(blocks):
                blocks[mask | bit] = swap(blocks[mask], bit)
            bit //= 2
        return [blocks[mask] for mask in range(mid)]

    normed, tail = norm_rows(tokens, norm_gain)
    crossed = swap(normed, mid)
    early_blocks = gathered(normed)

    early_blocks, tail = lax.optimization_barrier((early_blocks, tail))
    late_halo = jnp.zeros_like(tail)
    for j in range(mid):
        pairs = [(c * tensor_count - 1, c * tensor_count + mid + j) for c in range(1, dev_count)]
        pairs += [(c * tensor_count + mid - 1, c * tensor_count + j) for c in range(dev_count)]
        late_halo = late_halo + lax.ppermute(tail, ("context", "tensor"), pairs)
    head = sum(jnp.where(place == mask, block[:PAD], 0) for mask, block in enumerate(early_blocks))
    packs = None
    if packed:
        early_gated, packs = project(
            (1, 2), place, early_blocks, weight, short_weight, COST[0], filt=long_filter
        )
    else:
        early_gated, _ = project((1, 2), place, early_blocks, weight, short_weight, COST[0])
        packs = [pack_any(rows, dev_count) for rows in (early_gated, long_filter)]
        packs = jnp.concatenate(packs, axis=1)
    packs, late_halo = lax.optimization_barrier((packs, late_halo))
    early_halo = swap(late_halo, mid)
    early_sent = exchange(packs)
    crossed, _ = lax.optimization_barrier((crossed, packs))
    late_blocks = gathered(crossed)
    gap = jnp.zeros((PAD - TAIL, tail.shape[1]), bf16)
    late_ext = jnp.concatenate([gap, late_halo, gap, early_halo, head], axis=0)
    late_gated, packs = project((1, 2), place, late_blocks, weight, short_weight, COST[1], ext=late_ext)
    if not packed:
        rows = late_gated.shape[0] - PAD
        packs = [pack_any(late_gated[:rows], dev_count), pack_any(late_gated[rows:], dev_count)]
        packs = jnp.concatenate(packs, axis=1)
    late_sent = exchange(packs)
    spectrum = filter_spectrum(early_sent, consts)
    conv = exchange(convolve(half, early_sent, late_sent, spectrum, consts))
    terms = query_terms(
        jnp.concatenate([me.reshape(1), half]),
        early_blocks + late_blocks,
        late_ext,
        weight,
        short_weight,
        early_gated,
        late_gated,
        skip_gain,
    )
    if packed:
        return finish(conv, terms)
    each = channels // dev_count
    conv = conv.reshape(dev_count, FINE, 2, HALF)[..., :each]
    conv = jnp.transpose(conv, (2, 1, 0, 3)).reshape(2 * FINE, channels).astype(f32)
    return (terms[0] * conv + terms[1]).astype(bf16)


def solution(mesh):
    return jax.shard_map(
        local,
        mesh=mesh,
        in_specs=(
            P(("context", "tensor"), None),
            P(),
            P(None, None, "tensor"),
            P(None, None, "tensor"),
            P("context", "tensor"),
            P("tensor"),
        ),
        out_specs=P("context", "tensor"),
        check_vma=False,
    )
```

```python
import functools
import math

import jax
import jax.numpy as jnp
import numpy as np
from jax import lax
from jax.experimental import pallas as pl
from jax.experimental.pallas import tpu as pltpu
from jax.sharding import PartitionSpec as P

eps = 1e-06

FINE = 256
HALF = 64
LANES = 2 * HALF
TAIL = 8
PAD = 16
BIG = 60 * 1024 * 1024
FINISH_LIMIT = 53
COST = (10**8, 10**8, 10**8)

VMEM_SPEC = pl.BlockSpec(memory_space=pltpu.VMEM)
HBM_SPEC = pl.BlockSpec(memory_space=pltpu.HBM)
ANY_SPEC = pl.BlockSpec(memory_space=pl.ANY)

f32 = jnp.float32
bf16 = jnp.bfloat16


def lane_mask():
    return lax.broadcasted_iota(jnp.int32, (1, LANES), 1) < HALF


def pack_pair(tile):
    low = lane_mask()
    rows = tile.shape[0] // 2
    top, bot = tile[:rows], tile[rows:]
    return (
        jnp.where(low, top, pltpu.roll(bot, HALF, 1)),
        jnp.where(low, pltpu.roll(top, HALF, 1), bot),
    )


def unpack_pair(first, second):
    low = lane_mask()
    return (
        jnp.where(low, first, pltpu.roll(second, HALF, 1)),
        jnp.where(low, pltpu.roll(first, HALF, 1), second),
    )


def start_all(copies):
    copies = [pltpu.make_async_copy(*copy) for copy in copies]
    for copy in copies:
        copy.start()
    return copies


def pack_any(rows, dev_count):
    length, channels = rows.shape
    each = channels // dev_count
    blocks = rows.astype(bf16).reshape(2, length // 2, dev_count, each)
    blocks = jnp.transpose(blocks, (2, 1, 0, 3))
    blocks = jnp.pad(blocks, ((0, 0), (0, 0), (0, 0), (0, HALF - each)))
    return blocks.reshape(dev_count, length // 2, LANES)


def norm_rows(tokens, gain):
    rows, width = tokens.shape
    step = min(32, rows)

    def kernel(tok_hbm, gain_hbm, out_any, tail_any, tok_ref, gain_ref, out_ref, sem, out_sem):
        parts = [pl.ds(i * step, step) for i in range(rows // step)]
        copies = start_all(
            [(gain_hbm, gain_ref, sem.at[len(parts)])]
            + [(tok_hbm.at[part], tok_ref.at[part], sem.at[i]) for i, part in enumerate(parts)]
        )
        copies[0].wait()
        sends = []
        for i, part in enumerate(parts):
            copies[1 + i].wait()
            values = tok_ref[part, :].astype(f32)
            inv_rms = lax.rsqrt(jnp.mean(values * values, axis=1, keepdims=True) + eps)
            out_ref[part, :] = (values * inv_rms * gain_ref[...]).astype(bf16)
            sends += start_all([(out_ref.at[part], out_any.at[part], out_sem.at[i])])
        sends += start_all([(out_ref.at[pl.ds(rows - TAIL, TAIL)], tail_any, out_sem.at[len(parts)])])
        for send in sends:
            send.wait()

    return pl.pallas_call(
        kernel,
        in_specs=[HBM_SPEC] * 2,
        out_specs=[ANY_SPEC] * 2,
        out_shape=[jax.ShapeDtypeStruct((rows, width), bf16), jax.ShapeDtypeStruct((TAIL, width), bf16)],
        scratch_shapes=[
            pltpu.VMEM((rows, width), bf16),
            pltpu.VMEM((1, width), f32),
            pltpu.VMEM((rows, width), bf16),
            pltpu.SemaphoreType.DMA((rows // step + 1,)),
            pltpu.SemaphoreType.DMA((rows // step + 1,)),
        ],
        compiler_params=pltpu.CompilerParams(vmem_limit_bytes=BIG),
        name="norm_rows",
    )(tokens, gain.reshape(1, width))


def pack_into(p_ref, at, rows_ref, first, length):
    rows = pl.ds(at, length // 2)
    for i in range(p_ref.shape[0] // 2):
        one, two = pack_pair(rows_ref[first : first + length, i * LANES : (i + 1) * LANES])
        p_ref[2 * i, rows, :] = one.astype(bf16)
        p_ref[2 * i + 1, rows, :] = two.astype(bf16)


def project_kernel(count, parts, splits, ext_rows, with_filter, me_ref, *refs):
    blocks, refs = refs[:count], refs[count:]
    w_hbm, tap_hbm = refs[:2]
    extra, refs = refs[2 : 2 + bool(ext_rows) + with_filter], refs[2 + bool(ext_rows) + with_filter :]
    number = 2 * (1 in parts) + (0 in parts)
    out_any, outs, refs = refs[:number], refs[number : 2 * number], refs[2 * number :]
    w_ref, tap_ref, x_ref, rows_ref, filt_ref, sem, w_sem, tap_sem, out_sem = refs

    def send(i):
        return start_all([(outs[i], out_any[i], out_sem.at[i])])

    each = blocks[0].shape[0]
    length = each * count
    end = PAD + length
    width, channels = x_ref.shape[1], rows_ref.shape[1]
    each_cols = channels // splits

    sources = [(tap_hbm, tap_ref, tap_sem)]
    for mask, block in enumerate(blocks):
        first = pl.multiple_of(PAD + (me_ref[0] ^ mask) * each, 16)
        sources.append((block, x_ref.at[pl.ds(first, each)], sem.at[mask]))
    if ext_rows:
        sources.append((extra[0].at[pl.ds(0, PAD)], x_ref.at[pl.ds(0, PAD)], sem.at[count]))
    else:
        x_ref[:PAD] = jnp.zeros((PAD, width), bf16)
    if ext_rows > PAD:
        rest = ext_rows - PAD
        sources.append((extra[0].at[pl.ds(PAD, rest)], x_ref.at[pl.ds(end, rest)], sem.at[count + 1]))
    if with_filter:
        filt_load = start_all([(extra[-1], filt_ref, sem.at[count + 2])])[0]
    waits = start_all(sources)
    loads = {}
    for at, s in enumerate(parts):
        for i in range(splits):
            cols = pl.ds(i * each_cols, each_cols)
            loads[s, i] = start_all([(w_hbm.at[s, :, cols], w_ref.at[at, i], w_sem.at[at, i])])[0]
    if with_filter:
        filt_load.wait()
        pack_into(outs[1], length // 2, filt_ref, 0, filt_ref.shape[0])
    for wait in waits:
        wait.wait()

    def mixed(s):
        at = parts.index(s)
        for i in range(splits):
            loads[s, i].wait()
            cols = slice(i * each_cols, (i + 1) * each_cols)
            rows_ref[:, cols] = jnp.dot(x_ref[...], w_ref[at, i], preferred_element_type=f32)
        spans = [(PAD, length)]
        if ext_rows > PAD:
            spans.append((end + PAD, PAD))
        results = []
        for first, size in spans:
            total = tap_ref[0, s : s + 1] * rows_ref[first : first + size]
            for lag in (1, 2):
                total += tap_ref[lag, s : s + 1] * rows_ref[first - lag : first - lag + size]
            results.append(total)
        return results

    if 1 in parts:
        g_ref, p_ref = outs[:2]
        spans = [slice(0, length), slice(length, length + PAD)]
        for span, key in zip(spans, mixed(1)):
            g_ref[span, :] = key
        for span, value in zip(spans, mixed(2)):
            g_ref[span, :] *= value
        sends = send(0)
        pack_into(p_ref, 0, g_ref, 0, length)
        if ext_rows > PAD:
            pack_into(p_ref, length // 2, g_ref, length, PAD)
        sends += send(1)
    if 0 in parts:
        outs[-1][...] = mixed(0)[0]
        sends = (sends if 1 in parts else []) + send(number - 1)
    for copy in sends:
        copy.wait()


def project(parts, me, blocks, weight, taps, cost, ext=None, filt=None):
    _, width, channels = weight.shape
    length = blocks[0].shape[0] * len(blocks)
    splits = 1
    ext_rows = 0 if ext is None else ext.shape[0]
    more = PAD if ext_rows > PAD else 0
    shapes = []
    if 1 in parts:
        rows = (length + more) // 2 + (0 if filt is None else filt.shape[0] // 2)
        shapes += [
            jax.ShapeDtypeStruct((length + more, channels), f32),
            jax.ShapeDtypeStruct((max(channels // HALF, 2), rows, LANES), bf16),
        ]
    if 0 in parts:
        shapes.append(jax.ShapeDtypeStruct((length, channels), f32))
    extra = [x for x in (ext, filt) if x is not None]
    rows = PAD + length + (2 * PAD if more else 0)
    return pl.pallas_call(
        functools.partial(project_kernel, len(blocks), parts, splits, ext_rows, filt is not None),
        in_specs=[pl.BlockSpec(memory_space=pltpu.SMEM)] + [ANY_SPEC] * (len(blocks) + 2 + len(extra)),
        out_specs=[ANY_SPEC] * len(shapes),
        out_shape=shapes,
        scratch_shapes=[pltpu.VMEM(x.shape, x.dtype) for x in shapes]
        + [
            pltpu.VMEM((len(parts), splits, width, channels // splits), bf16),
            pltpu.VMEM(taps.shape, f32),
            pltpu.VMEM((rows, width), bf16),
            pltpu.VMEM((rows, channels), f32),
            pltpu.VMEM((8, LANES) if filt is None else filt.shape, f32),
            pltpu.SemaphoreType.DMA((len(blocks) + 3,)),
            pltpu.SemaphoreType.DMA((len(parts), splits)),
            pltpu.SemaphoreType.DMA,
            pltpu.SemaphoreType.DMA((len(shapes),)),
        ],
        compiler_params=pltpu.CompilerParams(vmem_limit_bytes=BIG),
        cost_estimate=pl.CostEstimate(flops=cost, bytes_accessed=10**5, transcendentals=0),
        name="project",
    )(me, *blocks, weight, taps, *extra)


def coarse_forward(dev_count, x_ref, lane_ref, e_ref, step=64):
    count = dev_count
    half = count // 2
    low = lane_mask()
    sgn = jnp.where(low, 1.0, -1.0).astype(f32)

    def body(i, carry):
        rows = pl.ds(pl.multiple_of(i * step, step), step)
        x = [x_ref[s, rows, :].astype(f32) for s in range(count)]
        plus = [x[s] + x[count - s] for s in range(1, half)]
        minus = [x[s] - x[count - s] for s in range(1, half)]
        for k in range(count + 1):
            even = k % 2 == 0
            re = x[0]
            im = None
            mid = round(math.cos(math.pi * half * k / count))
            if mid:
                re = re + x[half] if mid > 0 else re - x[half]
            mid = round(math.sin(math.pi * half * k / count))
            if mid:
                im = -x[half] if mid > 0 else x[half]
            for s in range(1, half):
                c, d = math.cos(math.pi * s * k / count), math.sin(math.pi * s * k / count)
                if abs(c) > 1e-9:
                    re = re + c * (plus if even else minus)[s - 1]
                if abs(d) > 1e-9:
                    term = (-d) * (minus if even else plus)[s - 1]
                    im = term if im is None else im + term
            c, d = lane_ref[k, 0:1, :], lane_ref[k, 1:2, :]
            if im is None:
                re, im = re * c, re * (-d)
            else:
                re, im = re * c + im * d, im * c - re * d
            e_ref[k, rows, :LANES] = pltpu.roll(re, HALF, 1) + sgn * re
            e_ref[k, rows, LANES:] = sgn * pltpu.roll(im, HALF, 1) + im
        return carry

    lax.fori_loop(0, FINE // step, body, 0)


def coarse_inverse(dev_count, g_ref, y_ref, first, length, step=64):
    count = dev_count
    half = count // 2

    def body(i, carry):
        rows = pl.ds(pl.multiple_of(i * step, step), step)
        acc = {}

        def add(name, s, term):
            acc[name, s] = term if (name, s) not in acc else acc[name, s] + term

        for k in range(count + 1):
            even = k % 2 == 0
            re, im = g_ref[k, rows, :LANES], g_ref[k, rows, LANES:]
            add("first", 0, re)
            mid = round(math.cos(math.pi * half * k / count))
            if mid:
                add("mid", 0, re if mid > 0 else -re)
            mid = round(math.sin(math.pi * half * k / count))
            if mid:
                add("mid", 0, -im if mid > 0 else im)
            for s in range(1, half):
                c, d = math.cos(math.pi * s * k / count), math.sin(math.pi * s * k / count)
                if abs(c) > 1e-9:
                    add("a" if even else "b", s, c * re)
                if abs(d) > 1e-9:
                    add("b" if even else "a", -s, (-d) * im)
        y_ref[0, rows, :] = acc["first", 0].astype(bf16)
        y_ref[half, rows, :] = acc["mid", 0].astype(bf16)
        zero = jnp.zeros((step, LANES), f32)
        for s in range(1, half):
            same = acc.get(("a", s), zero)
            flip = acc.get(("b", s), zero)
            same_sin = acc.get(("a", -s), zero)
            flip_sin = acc.get(("b", -s), zero)
            total, diff = same + same_sin, flip + flip_sin
            y_ref[s, rows, :] = (total + diff).astype(bf16)
            y_ref[count - s, rows, :] = (total - diff).astype(bf16)
        return carry

    lax.fori_loop(first // step, (first + length) // step, body, 0)


def fine_forward(e, tr, ti, table):
    re, im = e[:, :LANES], e[:, LANES:]
    turned = jnp.concatenate([re * tr - im * ti, re * ti + im * tr], axis=1).astype(bf16)
    both = jnp.dot(table, turned, preferred_element_type=f32)
    return (
        both[:FINE, :LANES] - both[FINE:, LANES:],
        both[:FINE, LANES:] + both[FINE:, :LANES],
    )


def next_turn(turn_ref, step_ref):
    tr, ti = turn_ref[:, :LANES], turn_ref[:, LANES:]
    sr, si = step_ref[:, :LANES], step_ref[:, LANES:]
    turn_ref[:, :LANES] = tr * sr - ti * si
    turn_ref[:, LANES:] = tr * si + ti * sr


def filter_kernel(dev_count, x_any, *refs):
    const_hbm, h_ref = refs[:4], refs[4]
    x_ref, first_ref, step_ref, lane_ref, table_ref, e_ref, sem = refs[5:]
    turn_ref = first_ref
    rows = pl.ds(x_any.shape[1] - FINE, FINE)
    pairs = [(x_any.at[:, rows], x_ref)] + list(zip(const_hbm, (first_ref, step_ref, lane_ref, table_ref)))
    for copy in start_all((*pair, sem.at[i]) for i, pair in enumerate(pairs)):
        copy.wait()
    coarse_forward(dev_count, x_ref, lane_ref, e_ref)
    points = 4 * dev_count * FINE

    def body(k, carry):
        re, im = fine_forward(e_ref[k], turn_ref[:, :LANES], turn_ref[:, LANES:], table_ref[...])
        scale = jnp.where((k == 0) | (k == dev_count), 1.0 / points, 2.0 / points).astype(f32)
        h_ref[k, :, :LANES] = re * scale
        h_ref[k, :, LANES:] = im * scale
        next_turn(turn_ref, step_ref)
        return carry

    lax.fori_loop(0, dev_count + 1, body, 0, unroll=dev_count <= 8)


def merge_halves(dev_count, late_first, early_ref, late_ref, x_ref):
    pick = late_first == 1
    low = lane_mask()
    size = FINE // 2
    for s in range(dev_count):
        early, late = early_ref[s].astype(f32), late_ref[s].astype(f32)
        fixed = jnp.where(low, late[size:], early[: PAD // 2])
        early, late = jnp.concatenate([fixed, early[PAD // 2 :]], axis=0), late[:size]
        first, second = jnp.where(pick, late, early), jnp.where(pick, early, late)
        top, bot = pack_pair(jnp.concatenate([first, second], axis=0))
        x_ref[s, :size] = top
        x_ref[s, size:] = bot


def conv_kernel(dev_count, half_ref, early_any, late_any, h_hbm, *refs):
    const_hbm, y_any = refs[:4], refs[4]
    early_ref, late_ref, x_ref, h_ref, first_ref, step_ref, lane_ref, table_ref, e_ref, y_ref, sem, y_sem = refs[5:]
    turn_ref = first_ref
    pairs = [(early_any.at[:, pl.ds(0, FINE // 2)], early_ref), (late_any, late_ref), (const_hbm[2], lane_ref)]
    pairs += [(const_hbm[0], first_ref), (const_hbm[1], step_ref), (const_hbm[3], table_ref), (h_hbm, h_ref)]
    copies = start_all((*pair, sem.at[i]) for i, pair in enumerate(pairs))
    for copy in copies[:3]:
        copy.wait()
    merge_halves(dev_count, half_ref[0], early_ref, late_ref, x_ref)
    coarse_forward(dev_count, x_ref, lane_ref, e_ref)
    for copy in copies[3:]:
        copy.wait()
    sgn = jnp.where(lane_mask(), 1.0, -1.0).astype(f32)

    def body(k, carry):
        tr, ti = turn_ref[:, :LANES], turn_ref[:, LANES:]
        re, im = fine_forward(e_ref[k], tr, ti, table_ref[...])
        hr, hi = h_ref[k, :, :LANES], h_ref[k, :, LANES:]
        prod = jnp.concatenate([re * hr - im * hi, re * hi + im * hr], axis=1).astype(bf16)
        both = jnp.dot(table_ref[...], prod, preferred_element_type=f32)
        re = both[:FINE, :LANES] + both[FINE:, LANES:]
        im = both[:FINE, LANES:] - both[FINE:, :LANES]
        re, im = re * tr + im * ti, (im * tr - re * ti) * sgn
        re, im = pltpu.roll(re, HALF, 1) + sgn * re, pltpu.roll(im, HALF, 1) + sgn * im
        c, d = lane_ref[k, 0:1, :], lane_ref[k, 1:2, :]
        e_ref[k, :, :LANES] = re * c - im * d
        e_ref[k, :, LANES:] = re * d + im * c
        next_turn(turn_ref, step_ref)
        return carry

    lax.fori_loop(0, dev_count + 1, body, 0, unroll=dev_count <= 8)
    sends = []
    for i in range(2):
        rows = pl.ds(i * FINE // 2, FINE // 2)
        coarse_inverse(dev_count, e_ref, y_ref, i * FINE // 2, FINE // 2)
        sends += start_all([(y_ref.at[:, rows], y_any.at[:, rows], y_sem.at[i])])
    for send in sends:
        send.wait()


def tables(dev_count):
    points = 4 * dev_count * FINE
    fine = np.arange(FINE)
    first = np.exp(-2j * np.pi * fine * (2 * dev_count) / points)[:, None] * np.ones(HALF)
    ones = np.ones((FINE, HALF))
    step = np.exp(-2j * np.pi * fine / points)[:, None] * ones
    first = np.concatenate([ones, first.real, 0 * ones, first.imag], axis=1)
    step = np.concatenate([step.real, step.real, step.imag, -step.imag], axis=1)
    turn = 2 * np.pi * np.arange(dev_count + 1)[:, None] * np.ones(HALF) / (4 * dev_count)
    lane = np.stack(
        [
            np.concatenate([np.ones_like(turn), np.cos(turn)], axis=1),
            np.concatenate([np.zeros_like(turn), np.sin(turn)], axis=1),
        ],
        axis=1,
    )
    angle = -2 * np.pi * (fine[:, None] * fine[None, :] % FINE) / FINE
    table = np.concatenate([np.cos(angle), np.sin(angle)], axis=0)
    return (
        jnp.asarray(first, f32),
        jnp.asarray(step, f32),
        jnp.asarray(lane, f32),
        jnp.asarray(table, bf16),
    )


def const_scratch(consts):
    return [pltpu.VMEM(const.shape, const.dtype) for const in consts]


def filter_spectrum(x, consts):
    dev_count = x.shape[0]
    return pl.pallas_call(
        functools.partial(filter_kernel, dev_count),
        in_specs=[ANY_SPEC] + [HBM_SPEC] * 4,
        out_specs=VMEM_SPEC,
        out_shape=jax.ShapeDtypeStruct((dev_count + 1, FINE, 2 * LANES), f32),
        scratch_shapes=[pltpu.VMEM((dev_count, FINE, LANES), bf16)]
        + const_scratch(consts)
        + [pltpu.VMEM((dev_count + 1, FINE, 2 * LANES), f32), pltpu.SemaphoreType.DMA((5,))],
        compiler_params=pltpu.CompilerParams(vmem_limit_bytes=BIG),
        name="filter_spectrum",
    )(x, *consts)


def convolve(half, early, late, spectrum, consts):
    dev_count = early.shape[0]
    return pl.pallas_call(
        functools.partial(conv_kernel, dev_count),
        in_specs=[pl.BlockSpec(memory_space=pltpu.SMEM)] + [ANY_SPEC] * 2 + [HBM_SPEC] * 5,
        out_specs=ANY_SPEC,
        out_shape=jax.ShapeDtypeStruct((dev_count, FINE, LANES), bf16),
        scratch_shapes=[
            pltpu.VMEM((dev_count, FINE // 2, LANES), bf16),
            pltpu.VMEM(late.shape, bf16),
            pltpu.VMEM((dev_count, FINE, LANES), f32),
            pltpu.VMEM(spectrum.shape, f32),
        ]
        + const_scratch(consts)
        + [
            pltpu.VMEM((dev_count + 1, FINE, 2 * LANES), f32),
            pltpu.VMEM((dev_count, FINE, LANES), bf16),
            pltpu.SemaphoreType.DMA((7,)),
            pltpu.SemaphoreType.DMA((2,)),
        ],
        compiler_params=pltpu.CompilerParams(vmem_limit_bytes=BIG),
        name="convolve",
    )(half, early, late, spectrum, *consts)


def query_kernel(count, me_ref, *refs):
    blocks, refs = refs[:count], refs[count:]
    halo_any, w_hbm, tap_hbm, early_any, late_any, skip_hbm, out_any = refs[:7]
    x_ref, w_ref, tap_ref, early_ref, late_ref, skip_ref, rows_ref, out_ref, sem, out_sem = refs[7:]
    each = blocks[0].shape[0]
    length = each * count
    half = length // 2
    early_at = me_ref[1]

    ahead = pl.ds(pl.multiple_of((1 - early_at) * PAD, PAD), PAD)
    pairs = [(halo_any.at[ahead], x_ref.at[pl.ds(0, PAD)])]
    for mask, block in enumerate(blocks):
        first = pl.multiple_of(PAD + (me_ref[0] ^ mask) * each, 16)
        pairs.append((block, x_ref.at[pl.ds(first, each)]))
    pairs += [(w_hbm.at[0], w_ref), (tap_hbm, tap_ref), (skip_hbm, skip_ref)]
    pairs += [(early_any, early_ref), (late_any, late_ref)]
    for copy in start_all((*pair, sem.at[i]) for i, pair in enumerate(pairs)):
        copy.wait()
    rows_ref[...] = jnp.dot(x_ref[...], w_ref[...], preferred_element_type=f32)
    total = tap_ref[0, 0:1] * rows_ref[PAD:]
    for lag in (1, 2):
        total += tap_ref[lag, 0:1] * rows_ref[PAD - lag : PAD - lag + length]
    out_ref[0] = total.astype(bf16)
    rows_ref[PAD:] = total
    early_ref[:PAD] = late_ref[half:]
    for at, g_ref in ((early_at, early_ref), (1 - early_at, late_ref)):
        rows = pl.ds(pl.multiple_of(at * half, half), half)
        query = rows_ref[pl.ds(pl.multiple_of(PAD + at * half, 16), half), :]
        out_ref[1, rows, :] = (query * (skip_ref[...] * g_ref[:half])).astype(bf16)
    start_all([(out_ref, out_any, out_sem)])[0].wait()


def query_terms(me, blocks, halo, weight, taps, early, late, skip):
    _, width, channels = weight.shape
    length = blocks[0].shape[0] * len(blocks)
    skip = skip.reshape(1, channels)
    return pl.pallas_call(
        functools.partial(query_kernel, len(blocks)),
        in_specs=[pl.BlockSpec(memory_space=pltpu.SMEM)] + [ANY_SPEC] * (len(blocks) + 6),
        out_specs=ANY_SPEC,
        out_shape=jax.ShapeDtypeStruct((2, length, channels), bf16),
        scratch_shapes=[
            pltpu.VMEM((PAD + length, width), bf16),
            pltpu.VMEM((width, channels), bf16),
            pltpu.VMEM(taps.shape, f32),
            pltpu.VMEM(early.shape, f32),
            pltpu.VMEM(late.shape, f32),
            pltpu.VMEM(skip.shape, f32),
            pltpu.VMEM((PAD + length, channels), f32),
            pltpu.VMEM((2, length, channels), bf16),
            pltpu.SemaphoreType.DMA((len(blocks) + 6,)),
            pltpu.SemaphoreType.DMA,
        ],
        compiler_params=pltpu.CompilerParams(vmem_limit_bytes=BIG),
        cost_estimate=pl.CostEstimate(flops=COST[2], bytes_accessed=10**5, transcendentals=0),
        name="query_terms",
    )(me, *blocks, halo, weight, taps, early, late, skip)


def finish(conv, terms):
    _, length, channels = terms.shape
    tiles = channels // LANES

    def kernel(c_ref, term_any, out_any, term_ref, out_ref, in_sem, sem):
        cols = [pl.ds(i * LANES, LANES) for i in range(tiles)]
        loads = start_all((term_any.at[:, :, cols[i]], term_ref.at[i], in_sem.at[i]) for i in range(tiles))
        sends = []
        for i in range(tiles):
            top, bot = unpack_pair(c_ref[2 * i].astype(f32), c_ref[2 * i + 1].astype(f32))
            loads[i].wait()
            for j, part in enumerate((top, bot)):
                rows = slice(j * FINE, (j + 1) * FINE)
                out_ref[i, rows] = (term_ref[i, 0, rows].astype(f32) * part + term_ref[i, 1, rows].astype(f32)).astype(bf16)
            sends += start_all([(out_ref.at[i], out_any.at[:, cols[i]], sem.at[i])])
        for send in sends:
            send.wait()

    return pl.pallas_call(
        kernel,
        in_specs=[VMEM_SPEC, ANY_SPEC],
        out_specs=ANY_SPEC,
        out_shape=jax.ShapeDtypeStruct((length, channels), bf16),
        scratch_shapes=[
            pltpu.VMEM((tiles, 2, length, LANES), bf16),
            pltpu.VMEM((tiles, length, LANES), bf16),
            pltpu.SemaphoreType.DMA((tiles,)),
            pltpu.SemaphoreType.DMA((tiles,)),
        ],
        compiler_params=pltpu.CompilerParams(vmem_limit_bytes=FINISH_LIMIT * 1024 * 1024),
        name="finish",
    )(conv, terms)


def local(tokens, norm_gain, in_weight, short_weight, long_filter, skip_gain):
    dev_count = lax.axis_size("context")
    tensor_count = lax.axis_size("tensor")
    channels = in_weight.shape[2]
    packed = channels // dev_count == HALF
    consts = tables(dev_count)
    weight = jnp.transpose(in_weight, (1, 0, 2))
    exchange = functools.partial(
        lax.all_to_all, axis_name="context", split_axis=0, concat_axis=0, tiled=True
    )

    me = lax.axis_index("tensor").astype(jnp.int32)
    mid = tensor_count // 2
    half = (me // mid).reshape(1)
    place = (me % mid).reshape(1)

    def swap(x, bit):
        return lax.ppermute(x, "tensor", [(i, i ^ bit) for i in range(tensor_count)])

    def gathered(block):
        blocks = {0: block}
        bit = mid // 2
        while bit:
            for mask in list(blocks):
                blocks[mask | bit] = swap(blocks[mask], bit)
            bit //= 2
        return [blocks[mask] for mask in range(mid)]

    normed, tail = norm_rows(tokens, norm_gain)
    crossed = swap(normed, mid)
    early_blocks = gathered(normed)

    early_blocks, tail = lax.optimization_barrier((early_blocks, tail))
    late_halo = jnp.zeros_like(tail)
    for j in range(mid):
        pairs = [(c * tensor_count - 1, c * tensor_count + mid + j) for c in range(1, dev_count)]
        pairs += [(c * tensor_count + mid - 1, c * tensor_count + j) for c in range(dev_count)]
        late_halo = late_halo + lax.ppermute(tail, ("context", "tensor"), pairs)
    head = sum(jnp.where(place == mask, block[:PAD], 0) for mask, block in enumerate(early_blocks))
    packs = None
    if packed:
        early_gated, packs = project(
            (1, 2), place, early_blocks, weight, short_weight, COST[0], filt=long_filter
        )
    else:
        early_gated, _ = project((1, 2), place, early_blocks, weight, short_weight, COST[0])
        packs = [pack_any(rows, dev_count) for rows in (early_gated, long_filter)]
        packs = jnp.concatenate(packs, axis=1)
    packs, late_halo = lax.optimization_barrier((packs, late_halo))
    early_halo = swap(late_halo, mid)
    early_sent = exchange(packs)
    crossed, _ = lax.optimization_barrier((crossed, packs))
    late_blocks = gathered(crossed)
    gap = jnp.zeros((PAD - TAIL, tail.shape[1]), bf16)
    late_ext = jnp.concatenate([gap, late_halo, gap, early_halo, head], axis=0)
    late_gated, packs = project((1, 2), place, late_blocks, weight, short_weight, COST[1], ext=late_ext)
    if not packed:
        rows = late_gated.shape[0] - PAD
        packs = [pack_any(late_gated[:rows], dev_count), pack_any(late_gated[rows:], dev_count)]
        packs = jnp.concatenate(packs, axis=1)
    late_sent = exchange(packs)
    spectrum = filter_spectrum(early_sent, consts)
    conv = exchange(convolve(half, early_sent, late_sent, spectrum, consts))
    terms = query_terms(
        jnp.concatenate([me.reshape(1), half]),
        early_blocks + late_blocks,
        late_ext,
        weight,
        short_weight,
        early_gated,
        late_gated,
        skip_gain,
    )
    if packed:
        return finish(conv, terms)
    each = channels // dev_count
    conv = conv.reshape(dev_count, FINE, 2, HALF)[..., :each]
    conv = jnp.transpose(conv, (2, 1, 0, 3)).reshape(2 * FINE, channels).astype(f32)
    return (terms[0].astype(f32) * conv + terms[1].astype(f32)).astype(bf16)


def solution(mesh):
    return jax.shard_map(
        local,
        mesh=mesh,
        in_specs=(
            P(("context", "tensor"), None),
            P(),
            P(None, None, "tensor"),
            P(None, None, "tensor"),
            P("context", "tensor"),
            P("tensor"),
        ),
        out_specs=P("context", "tensor"),
        check_vma=False,
    )
```

```python
import functools
import math

import jax
import jax.numpy as jnp
import numpy as np
from jax import lax
from jax.experimental import pallas as pl
from jax.experimental.pallas import tpu as pltpu
from jax.sharding import PartitionSpec as P

eps = 1e-06

FINE = 256
HALF = 64
LANES = 2 * HALF
TAIL = 8
PAD = 16
BIG = 60 * 1024 * 1024
FINISH_LIMIT = 53
COST = (10**8, 10**8, 10**8)

VMEM_SPEC = pl.BlockSpec(memory_space=pltpu.VMEM)
HBM_SPEC = pl.BlockSpec(memory_space=pltpu.HBM)
ANY_SPEC = pl.BlockSpec(memory_space=pl.ANY)

f32 = jnp.float32
bf16 = jnp.bfloat16


def lane_mask():
    return lax.broadcasted_iota(jnp.int32, (1, LANES), 1) < HALF


def pack_pair(tile):
    low = lane_mask()
    rows = tile.shape[0] // 2
    top, bot = tile[:rows], tile[rows:]
    return (
        jnp.where(low, top, pltpu.roll(bot, HALF, 1)),
        jnp.where(low, pltpu.roll(top, HALF, 1), bot),
    )


def unpack_pair(first, second):
    low = lane_mask()
    return (
        jnp.where(low, first, pltpu.roll(second, HALF, 1)),
        jnp.where(low, pltpu.roll(first, HALF, 1), second),
    )


def start_all(copies):
    copies = [pltpu.make_async_copy(*copy) for copy in copies]
    for copy in copies:
        copy.start()
    return copies


def pack_any(rows, dev_count):
    length, channels = rows.shape
    each = channels // dev_count
    blocks = rows.astype(bf16).reshape(2, length // 2, dev_count, each)
    blocks = jnp.transpose(blocks, (2, 1, 0, 3))
    blocks = jnp.pad(blocks, ((0, 0), (0, 0), (0, 0), (0, HALF - each)))
    return blocks.reshape(dev_count, length // 2, LANES)


def norm_rows(tokens, gain):
    rows, width = tokens.shape
    step = min(64, rows)

    def kernel(tok_hbm, gain_hbm, out_any, tail_any, tok_ref, gain_ref, out_ref, sem, out_sem):
        parts = [pl.ds(i * step, step) for i in range(rows // step)]
        copies = start_all(
            [(gain_hbm, gain_ref, sem.at[len(parts)])]
            + [(tok_hbm.at[part], tok_ref.at[part], sem.at[i]) for i, part in enumerate(parts)]
        )
        copies[0].wait()
        sends = []
        for i, part in enumerate(parts):
            copies[1 + i].wait()
            values = tok_ref[part, :].astype(f32)
            inv_rms = lax.rsqrt(jnp.mean(values * values, axis=1, keepdims=True) + eps)
            out_ref[part, :] = (values * inv_rms * gain_ref[...]).astype(bf16)
            sends += start_all([(out_ref.at[part], out_any.at[part], out_sem.at[i])])
        sends += start_all([(out_ref.at[pl.ds(rows - TAIL, TAIL)], tail_any, out_sem.at[len(parts)])])
        for send in sends:
            send.wait()

    return pl.pallas_call(
        kernel,
        in_specs=[HBM_SPEC] * 2,
        out_specs=[ANY_SPEC] * 2,
        out_shape=[jax.ShapeDtypeStruct((rows, width), bf16), jax.ShapeDtypeStruct((TAIL, width), bf16)],
        scratch_shapes=[
            pltpu.VMEM((rows, width), bf16),
            pltpu.VMEM((1, width), f32),
            pltpu.VMEM((rows, width), bf16),
            pltpu.SemaphoreType.DMA((rows // step + 1,)),
            pltpu.SemaphoreType.DMA((rows // step + 1,)),
        ],
        compiler_params=pltpu.CompilerParams(vmem_limit_bytes=BIG),
        name="norm_rows",
    )(tokens, gain.reshape(1, width))


def pack_into(p_ref, at, rows_ref, first, length):
    rows = pl.ds(at, length // 2)
    for i in range(p_ref.shape[0] // 2):
        one, two = pack_pair(rows_ref[first : first + length, i * LANES : (i + 1) * LANES])
        p_ref[2 * i, rows, :] = one.astype(bf16)
        p_ref[2 * i + 1, rows, :] = two.astype(bf16)


def project_kernel(count, parts, splits, ext_rows, with_filter, me_ref, *refs):
    blocks, refs = refs[:count], refs[count:]
    w_hbm, tap_hbm = refs[:2]
    extra, refs = refs[2 : 2 + bool(ext_rows) + with_filter], refs[2 + bool(ext_rows) + with_filter :]
    number = 2 * (1 in parts) + (0 in parts)
    out_any, outs, refs = refs[:number], refs[number : 2 * number], refs[2 * number :]
    w_ref, tap_ref, x_ref, rows_ref, filt_ref, sem, w_sem, tap_sem, out_sem = refs

    def send(i):
        return start_all([(outs[i], out_any[i], out_sem.at[i])])

    each = blocks[0].shape[0]
    length = each * count
    end = PAD + length
    width, channels = x_ref.shape[1], rows_ref.shape[1]
    each_cols = channels // splits

    sources = [(tap_hbm, tap_ref, tap_sem)]
    for mask, block in enumerate(blocks):
        first = pl.multiple_of(PAD + (me_ref[0] ^ mask) * each, 16)
        sources.append((block, x_ref.at[pl.ds(first, each)], sem.at[mask]))
    if ext_rows:
        sources.append((extra[0].at[pl.ds(0, PAD)], x_ref.at[pl.ds(0, PAD)], sem.at[count]))
    else:
        x_ref[:PAD] = jnp.zeros((PAD, width), bf16)
    if ext_rows > PAD:
        rest = ext_rows - PAD
        sources.append((extra[0].at[pl.ds(PAD, rest)], x_ref.at[pl.ds(end, rest)], sem.at[count + 1]))
    if with_filter:
        filt_load = start_all([(extra[-1], filt_ref, sem.at[count + 2])])[0]
    waits = start_all(sources)
    loads = {}
    for at, s in enumerate(parts):
        for i in range(splits):
            cols = pl.ds(i * each_cols, each_cols)
            loads[s, i] = start_all([(w_hbm.at[s, :, cols], w_ref.at[at, i], w_sem.at[at, i])])[0]
    if with_filter:
        filt_load.wait()
        pack_into(outs[1], length // 2, filt_ref, 0, filt_ref.shape[0])
    for wait in waits:
        wait.wait()

    def mixed(s):
        at = parts.index(s)
        for i in range(splits):
            loads[s, i].wait()
            cols = slice(i * each_cols, (i + 1) * each_cols)
            rows_ref[:, cols] = jnp.dot(x_ref[...], w_ref[at, i], preferred_element_type=f32)
        spans = [(PAD, length)]
        if ext_rows > PAD:
            spans.append((end + PAD, PAD))
        results = []
        for first, size in spans:
            total = tap_ref[0, s : s + 1] * rows_ref[first : first + size]
            for lag in (1, 2):
                total += tap_ref[lag, s : s + 1] * rows_ref[first - lag : first - lag + size]
            results.append(total)
        return results

    if 1 in parts:
        g_ref, p_ref = outs[:2]
        spans = [slice(0, length), slice(length, length + PAD)]
        for span, key in zip(spans, mixed(1)):
            g_ref[span, :] = key
        for span, value in zip(spans, mixed(2)):
            g_ref[span, :] *= value
        sends = send(0)
        pack_into(p_ref, 0, g_ref, 0, length)
        if ext_rows > PAD:
            pack_into(p_ref, length // 2, g_ref, length, PAD)
        sends += send(1)
    if 0 in parts:
        outs[-1][...] = mixed(0)[0]
        sends = (sends if 1 in parts else []) + send(number - 1)
    for copy in sends:
        copy.wait()


def project(parts, me, blocks, weight, taps, cost, ext=None, filt=None):
    _, width, channels = weight.shape
    length = blocks[0].shape[0] * len(blocks)
    splits = 1
    ext_rows = 0 if ext is None else ext.shape[0]
    more = PAD if ext_rows > PAD else 0
    shapes = []
    if 1 in parts:
        rows = (length + more) // 2 + (0 if filt is None else filt.shape[0] // 2)
        shapes += [
            jax.ShapeDtypeStruct((length + more, channels), f32),
            jax.ShapeDtypeStruct((max(channels // HALF, 2), rows, LANES), bf16),
        ]
    if 0 in parts:
        shapes.append(jax.ShapeDtypeStruct((length, channels), f32))
    extra = [x for x in (ext, filt) if x is not None]
    rows = PAD + length + (2 * PAD if more else 0)
    return pl.pallas_call(
        functools.partial(project_kernel, len(blocks), parts, splits, ext_rows, filt is not None),
        in_specs=[pl.BlockSpec(memory_space=pltpu.SMEM)] + [ANY_SPEC] * (len(blocks) + 2 + len(extra)),
        out_specs=[ANY_SPEC] * len(shapes),
        out_shape=shapes,
        scratch_shapes=[pltpu.VMEM(x.shape, x.dtype) for x in shapes]
        + [
            pltpu.VMEM((len(parts), splits, width, channels // splits), bf16),
            pltpu.VMEM(taps.shape, f32),
            pltpu.VMEM((rows, width), bf16),
            pltpu.VMEM((rows, channels), f32),
            pltpu.VMEM((8, LANES) if filt is None else filt.shape, f32),
            pltpu.SemaphoreType.DMA((len(blocks) + 3,)),
            pltpu.SemaphoreType.DMA((len(parts), splits)),
            pltpu.SemaphoreType.DMA,
            pltpu.SemaphoreType.DMA((len(shapes),)),
        ],
        compiler_params=pltpu.CompilerParams(vmem_limit_bytes=BIG),
        cost_estimate=pl.CostEstimate(flops=cost, bytes_accessed=10**5, transcendentals=0),
        name="project",
    )(me, *blocks, weight, taps, *extra)


def coarse_forward(dev_count, x_ref, lane_ref, e_ref, step=64):
    count = dev_count
    half = count // 2
    low = lane_mask()
    sgn = jnp.where(low, 1.0, -1.0).astype(f32)

    def body(i, carry):
        rows = pl.ds(pl.multiple_of(i * step, step), step)
        x = [x_ref[s, rows, :].astype(f32) for s in range(count)]
        plus = [x[s] + x[count - s] for s in range(1, half)]
        minus = [x[s] - x[count - s] for s in range(1, half)]
        for k in range(count + 1):
            even = k % 2 == 0
            re = x[0]
            im = None
            mid = round(math.cos(math.pi * half * k / count))
            if mid:
                re = re + x[half] if mid > 0 else re - x[half]
            mid = round(math.sin(math.pi * half * k / count))
            if mid:
                im = -x[half] if mid > 0 else x[half]
            for s in range(1, half):
                c, d = math.cos(math.pi * s * k / count), math.sin(math.pi * s * k / count)
                if abs(c) > 1e-9:
                    re = re + c * (plus if even else minus)[s - 1]
                if abs(d) > 1e-9:
                    term = (-d) * (minus if even else plus)[s - 1]
                    im = term if im is None else im + term
            c, d = lane_ref[k, 0:1, :], lane_ref[k, 1:2, :]
            if im is None:
                re, im = re * c, re * (-d)
            else:
                re, im = re * c + im * d, im * c - re * d
            e_ref[k, rows, :LANES] = pltpu.roll(re, HALF, 1) + sgn * re
            e_ref[k, rows, LANES:] = sgn * pltpu.roll(im, HALF, 1) + im
        return carry

    lax.fori_loop(0, FINE // step, body, 0)


def coarse_inverse(dev_count, g_ref, y_ref, first, length, step=64):
    count = dev_count
    half = count // 2

    def body(i, carry):
        rows = pl.ds(pl.multiple_of(i * step, step), step)
        acc = {}

        def add(name, s, term):
            acc[name, s] = term if (name, s) not in acc else acc[name, s] + term

        for k in range(count + 1):
            even = k % 2 == 0
            re, im = g_ref[k, rows, :LANES], g_ref[k, rows, LANES:]
            add("first", 0, re)
            mid = round(math.cos(math.pi * half * k / count))
            if mid:
                add("mid", 0, re if mid > 0 else -re)
            mid = round(math.sin(math.pi * half * k / count))
            if mid:
                add("mid", 0, -im if mid > 0 else im)
            for s in range(1, half):
                c, d = math.cos(math.pi * s * k / count), math.sin(math.pi * s * k / count)
                if abs(c) > 1e-9:
                    add("a" if even else "b", s, c * re)
                if abs(d) > 1e-9:
                    add("b" if even else "a", -s, (-d) * im)
        y_ref[0, rows, :] = acc["first", 0].astype(bf16)
        y_ref[half, rows, :] = acc["mid", 0].astype(bf16)
        zero = jnp.zeros((step, LANES), f32)
        for s in range(1, half):
            same = acc.get(("a", s), zero)
            flip = acc.get(("b", s), zero)
            same_sin = acc.get(("a", -s), zero)
            flip_sin = acc.get(("b", -s), zero)
            total, diff = same + same_sin, flip + flip_sin
            y_ref[s, rows, :] = (total + diff).astype(bf16)
            y_ref[count - s, rows, :] = (total - diff).astype(bf16)
        return carry

    lax.fori_loop(first // step, (first + length) // step, body, 0)


def fine_forward(e, tr, ti, table):
    re, im = e[:, :LANES], e[:, LANES:]
    turned = jnp.concatenate([re * tr - im * ti, re * ti + im * tr], axis=1).astype(bf16)
    both = jnp.dot(table, turned, preferred_element_type=f32)
    return (
        both[:FINE, :LANES] - both[FINE:, LANES:],
        both[:FINE, LANES:] + both[FINE:, :LANES],
    )


def next_turn(turn_ref, step_ref):
    tr, ti = turn_ref[:, :LANES], turn_ref[:, LANES:]
    sr, si = step_ref[:, :LANES], step_ref[:, LANES:]
    turn_ref[:, :LANES] = tr * sr - ti * si
    turn_ref[:, LANES:] = tr * si + ti * sr


def filter_kernel(dev_count, x_any, *refs):
    const_hbm, h_ref = refs[:4], refs[4]
    x_ref, first_ref, step_ref, lane_ref, table_ref, e_ref, sem = refs[5:]
    turn_ref = first_ref
    rows = pl.ds(x_any.shape[1] - FINE, FINE)
    pairs = [(x_any.at[:, rows], x_ref)] + list(zip(const_hbm, (first_ref, step_ref, lane_ref, table_ref)))
    for copy in start_all((*pair, sem.at[i]) for i, pair in enumerate(pairs)):
        copy.wait()
    coarse_forward(dev_count, x_ref, lane_ref, e_ref)
    points = 4 * dev_count * FINE

    def body(k, carry):
        re, im = fine_forward(e_ref[k], turn_ref[:, :LANES], turn_ref[:, LANES:], table_ref[...])
        scale = jnp.where((k == 0) | (k == dev_count), 1.0 / points, 2.0 / points).astype(f32)
        h_ref[k, :, :LANES] = re * scale
        h_ref[k, :, LANES:] = im * scale
        next_turn(turn_ref, step_ref)
        return carry

    lax.fori_loop(0, dev_count + 1, body, 0, unroll=dev_count <= 8)


def merge_halves(dev_count, late_first, early_ref, late_ref, x_ref):
    pick = late_first == 1
    low = lane_mask()
    size = FINE // 2
    for s in range(dev_count):
        early, late = early_ref[s].astype(f32), late_ref[s].astype(f32)
        fixed = jnp.where(low, late[size:], early[: PAD // 2])
        early, late = jnp.concatenate([fixed, early[PAD // 2 :]], axis=0), late[:size]
        first, second = jnp.where(pick, late, early), jnp.where(pick, early, late)
        top, bot = pack_pair(jnp.concatenate([first, second], axis=0))
        x_ref[s, :size] = top
        x_ref[s, size:] = bot


def conv_kernel(dev_count, half_ref, early_any, late_any, h_hbm, *refs):
    const_hbm, y_any = refs[:4], refs[4]
    early_ref, late_ref, x_ref, h_ref, first_ref, step_ref, lane_ref, table_ref, e_ref, y_ref, sem, y_sem = refs[5:]
    turn_ref = first_ref
    pairs = [(early_any.at[:, pl.ds(0, FINE // 2)], early_ref), (late_any, late_ref), (const_hbm[2], lane_ref)]
    pairs += [(const_hbm[0], first_ref), (const_hbm[1], step_ref), (const_hbm[3], table_ref), (h_hbm, h_ref)]
    copies = start_all((*pair, sem.at[i]) for i, pair in enumerate(pairs))
    for copy in copies[:3]:
        copy.wait()
    merge_halves(dev_count, half_ref[0], early_ref, late_ref, x_ref)
    coarse_forward(dev_count, x_ref, lane_ref, e_ref)
    for copy in copies[3:]:
        copy.wait()
    sgn = jnp.where(lane_mask(), 1.0, -1.0).astype(f32)

    def body(k, carry):
        tr, ti = turn_ref[:, :LANES], turn_ref[:, LANES:]
        re, im = fine_forward(e_ref[k], tr, ti, table_ref[...])
        hr, hi = h_ref[k, :, :LANES], h_ref[k, :, LANES:]
        prod = jnp.concatenate([re * hr - im * hi, re * hi + im * hr], axis=1).astype(bf16)
        both = jnp.dot(table_ref[...], prod, preferred_element_type=f32)
        re = both[:FINE, :LANES] + both[FINE:, LANES:]
        im = both[:FINE, LANES:] - both[FINE:, :LANES]
        re, im = re * tr + im * ti, (im * tr - re * ti) * sgn
        re, im = pltpu.roll(re, HALF, 1) + sgn * re, pltpu.roll(im, HALF, 1) + sgn * im
        c, d = lane_ref[k, 0:1, :], lane_ref[k, 1:2, :]
        e_ref[k, :, :LANES] = re * c - im * d
        e_ref[k, :, LANES:] = re * d + im * c
        next_turn(turn_ref, step_ref)
        return carry

    lax.fori_loop(0, dev_count + 1, body, 0, unroll=dev_count <= 8)
    sends = []
    for i in range(2):
        rows = pl.ds(i * FINE // 2, FINE // 2)
        coarse_inverse(dev_count, e_ref, y_ref, i * FINE // 2, FINE // 2)
        sends += start_all([(y_ref.at[:, rows], y_any.at[:, rows], y_sem.at[i])])
    for send in sends:
        send.wait()


def tables(dev_count):
    points = 4 * dev_count * FINE
    fine = np.arange(FINE)
    first = np.exp(-2j * np.pi * fine * (2 * dev_count) / points)[:, None] * np.ones(HALF)
    ones = np.ones((FINE, HALF))
    step = np.exp(-2j * np.pi * fine / points)[:, None] * ones
    first = np.concatenate([ones, first.real, 0 * ones, first.imag], axis=1)
    step = np.concatenate([step.real, step.real, step.imag, -step.imag], axis=1)
    turn = 2 * np.pi * np.arange(dev_count + 1)[:, None] * np.ones(HALF) / (4 * dev_count)
    lane = np.stack(
        [
            np.concatenate([np.ones_like(turn), np.cos(turn)], axis=1),
            np.concatenate([np.zeros_like(turn), np.sin(turn)], axis=1),
        ],
        axis=1,
    )
    angle = -2 * np.pi * (fine[:, None] * fine[None, :] % FINE) / FINE
    table = np.concatenate([np.cos(angle), np.sin(angle)], axis=0)
    return (
        jnp.asarray(first, f32),
        jnp.asarray(step, f32),
        jnp.asarray(lane, f32),
        jnp.asarray(table, bf16),
    )


def const_scratch(consts):
    return [pltpu.VMEM(const.shape, const.dtype) for const in consts]


def filter_spectrum(x, consts):
    dev_count = x.shape[0]
    return pl.pallas_call(
        functools.partial(filter_kernel, dev_count),
        in_specs=[ANY_SPEC] + [HBM_SPEC] * 4,
        out_specs=VMEM_SPEC,
        out_shape=jax.ShapeDtypeStruct((dev_count + 1, FINE, 2 * LANES), f32),
        scratch_shapes=[pltpu.VMEM((dev_count, FINE, LANES), bf16)]
        + const_scratch(consts)
        + [pltpu.VMEM((dev_count + 1, FINE, 2 * LANES), f32), pltpu.SemaphoreType.DMA((5,))],
        compiler_params=pltpu.CompilerParams(vmem_limit_bytes=BIG),
        name="filter_spectrum",
    )(x, *consts)


def convolve(half, early, late, spectrum, consts):
    dev_count = early.shape[0]
    return pl.pallas_call(
        functools.partial(conv_kernel, dev_count),
        in_specs=[pl.BlockSpec(memory_space=pltpu.SMEM)] + [ANY_SPEC] * 2 + [HBM_SPEC] * 5,
        out_specs=ANY_SPEC,
        out_shape=jax.ShapeDtypeStruct((dev_count, FINE, LANES), bf16),
        scratch_shapes=[
            pltpu.VMEM((dev_count, FINE // 2, LANES), bf16),
            pltpu.VMEM(late.shape, bf16),
            pltpu.VMEM((dev_count, FINE, LANES), f32),
            pltpu.VMEM(spectrum.shape, f32),
        ]
        + const_scratch(consts)
        + [
            pltpu.VMEM((dev_count + 1, FINE, 2 * LANES), f32),
            pltpu.VMEM((dev_count, FINE, LANES), bf16),
            pltpu.SemaphoreType.DMA((7,)),
            pltpu.SemaphoreType.DMA((2,)),
        ],
        compiler_params=pltpu.CompilerParams(vmem_limit_bytes=BIG),
        name="convolve",
    )(half, early, late, spectrum, *consts)


def query_kernel(count, me_ref, *refs):
    blocks, refs = refs[:count], refs[count:]
    halo_any, w_hbm, tap_hbm, early_any, late_any, skip_hbm, out_any = refs[:7]
    x_ref, w_ref, tap_ref, early_ref, late_ref, skip_ref, rows_ref, out_ref, sem, out_sem = refs[7:]
    each = blocks[0].shape[0]
    length = each * count
    half = length // 2
    early_at = me_ref[1]

    ahead = pl.ds(pl.multiple_of((1 - early_at) * PAD, PAD), PAD)
    pairs = [(halo_any.at[ahead], x_ref.at[pl.ds(0, PAD)])]
    for mask, block in enumerate(blocks):
        first = pl.multiple_of(PAD + (me_ref[0] ^ mask) * each, 16)
        pairs.append((block, x_ref.at[pl.ds(first, each)]))
    pairs += [(w_hbm.at[0], w_ref), (tap_hbm, tap_ref), (skip_hbm, skip_ref)]
    pairs += [(early_any, early_ref), (late_any, late_ref)]
    for copy in start_all((*pair, sem.at[i]) for i, pair in enumerate(pairs)):
        copy.wait()
    rows_ref[...] = jnp.dot(x_ref[...], w_ref[...], preferred_element_type=f32)
    total = tap_ref[0, 0:1] * rows_ref[PAD:]
    for lag in (1, 2):
        total += tap_ref[lag, 0:1] * rows_ref[PAD - lag : PAD - lag + length]
    out_ref[0] = total.astype(bf16)
    rows_ref[PAD:] = total
    early_ref[:PAD] = late_ref[half:]
    for at, g_ref in ((early_at, early_ref), (1 - early_at, late_ref)):
        rows = pl.ds(pl.multiple_of(at * half, half), half)
        query = rows_ref[pl.ds(pl.multiple_of(PAD + at * half, 16), half), :]
        out_ref[1, rows, :] = (query * (skip_ref[...] * g_ref[:half])).astype(bf16)
    start_all([(out_ref, out_any, out_sem)])[0].wait()


def query_terms(me, blocks, halo, weight, taps, early, late, skip):
    _, width, channels = weight.shape
    length = blocks[0].shape[0] * len(blocks)
    skip = skip.reshape(1, channels)
    return pl.pallas_call(
        functools.partial(query_kernel, len(blocks)),
        in_specs=[pl.BlockSpec(memory_space=pltpu.SMEM)] + [ANY_SPEC] * (len(blocks) + 6),
        out_specs=ANY_SPEC,
        out_shape=jax.ShapeDtypeStruct((2, length, channels), bf16),
        scratch_shapes=[
            pltpu.VMEM((PAD + length, width), bf16),
            pltpu.VMEM((width, channels), bf16),
            pltpu.VMEM(taps.shape, f32),
            pltpu.VMEM(early.shape, f32),
            pltpu.VMEM(late.shape, f32),
            pltpu.VMEM(skip.shape, f32),
            pltpu.VMEM((PAD + length, channels), f32),
            pltpu.VMEM((2, length, channels), bf16),
            pltpu.SemaphoreType.DMA((len(blocks) + 6,)),
            pltpu.SemaphoreType.DMA,
        ],
        compiler_params=pltpu.CompilerParams(vmem_limit_bytes=BIG),
        cost_estimate=pl.CostEstimate(flops=COST[2], bytes_accessed=10**5, transcendentals=0),
        name="query_terms",
    )(me, *blocks, halo, weight, taps, early, late, skip)


def finish(conv, terms):
    _, length, channels = terms.shape
    tiles = channels // LANES

    def kernel(c_ref, term_any, out_any, term_ref, out_ref, in_sem, sem):
        cols = [pl.ds(i * LANES, LANES) for i in range(tiles)]
        loads = start_all((term_any.at[:, :, cols[i]], term_ref.at[i], in_sem.at[i]) for i in range(tiles))
        sends = []
        for i in range(tiles):
            top, bot = unpack_pair(c_ref[2 * i].astype(f32), c_ref[2 * i + 1].astype(f32))
            loads[i].wait()
            for j, part in enumerate((top, bot)):
                rows = slice(j * FINE, (j + 1) * FINE)
                out_ref[i, rows] = (term_ref[i, 0, rows].astype(f32) * part + term_ref[i, 1, rows].astype(f32)).astype(bf16)
            sends += start_all([(out_ref.at[i], out_any.at[:, cols[i]], sem.at[i])])
        for send in sends:
            send.wait()

    return pl.pallas_call(
        kernel,
        in_specs=[VMEM_SPEC, ANY_SPEC],
        out_specs=ANY_SPEC,
        out_shape=jax.ShapeDtypeStruct((length, channels), bf16),
        scratch_shapes=[
            pltpu.VMEM((tiles, 2, length, LANES), bf16),
            pltpu.VMEM((tiles, length, LANES), bf16),
            pltpu.SemaphoreType.DMA((tiles,)),
            pltpu.SemaphoreType.DMA((tiles,)),
        ],
        compiler_params=pltpu.CompilerParams(vmem_limit_bytes=FINISH_LIMIT * 1024 * 1024),
        name="finish",
    )(conv, terms)


def local(tokens, norm_gain, in_weight, short_weight, long_filter, skip_gain):
    dev_count = lax.axis_size("context")
    tensor_count = lax.axis_size("tensor")
    channels = in_weight.shape[2]
    packed = channels // dev_count == HALF
    consts = tables(dev_count)
    weight = jnp.transpose(in_weight, (1, 0, 2))
    exchange = functools.partial(
        lax.all_to_all, axis_name="context", split_axis=0, concat_axis=0, tiled=True
    )

    me = lax.axis_index("tensor").astype(jnp.int32)
    mid = tensor_count // 2
    half = (me // mid).reshape(1)
    place = (me % mid).reshape(1)

    def swap(x, bit):
        return lax.ppermute(x, "tensor", [(i, i ^ bit) for i in range(tensor_count)])

    def gathered(block):
        blocks = {0: block}
        bit = mid // 2
        while bit:
            for mask in list(blocks):
                blocks[mask | bit] = swap(blocks[mask], bit)
            bit //= 2
        return [blocks[mask] for mask in range(mid)]

    normed, tail = norm_rows(tokens, norm_gain)
    crossed = swap(normed, mid)
    early_blocks = gathered(normed)

    early_blocks, tail = lax.optimization_barrier((early_blocks, tail))
    late_halo = jnp.zeros_like(tail)
    for j in range(mid):
        pairs = [(c * tensor_count - 1, c * tensor_count + mid + j) for c in range(1, dev_count)]
        pairs += [(c * tensor_count + mid - 1, c * tensor_count + j) for c in range(dev_count)]
        late_halo = late_halo + lax.ppermute(tail, ("context", "tensor"), pairs)
    head = sum(jnp.where(place == mask, block[:PAD], 0) for mask, block in enumerate(early_blocks))
    packs = None
    if packed:
        early_gated, packs = project(
            (1, 2), place, early_blocks, weight, short_weight, COST[0], filt=long_filter
        )
    else:
        early_gated, _ = project((1, 2), place, early_blocks, weight, short_weight, COST[0])
        packs = [pack_any(rows, dev_count) for rows in (early_gated, long_filter)]
        packs = jnp.concatenate(packs, axis=1)
    packs, late_halo = lax.optimization_barrier((packs, late_halo))
    early_halo = swap(late_halo, mid)
    early_sent = exchange(packs)
    crossed, _ = lax.optimization_barrier((crossed, packs))
    late_blocks = gathered(crossed)
    gap = jnp.zeros((PAD - TAIL, tail.shape[1]), bf16)
    late_ext = jnp.concatenate([gap, late_halo, gap, early_halo, head], axis=0)
    late_gated, packs = project((1, 2), place, late_blocks, weight, short_weight, COST[1], ext=late_ext)
    if not packed:
        rows = late_gated.shape[0] - PAD
        packs = [pack_any(late_gated[:rows], dev_count), pack_any(late_gated[rows:], dev_count)]
        packs = jnp.concatenate(packs, axis=1)
    late_sent = exchange(packs)
    spectrum = filter_spectrum(early_sent, consts)
    conv = exchange(convolve(half, early_sent, late_sent, spectrum, consts))
    terms = query_terms(
        jnp.concatenate([me.reshape(1), half]),
        early_blocks + late_blocks,
        late_ext,
        weight,
        short_weight,
        early_gated,
        late_gated,
        skip_gain,
    )
    if packed:
        return finish(conv, terms)
    each = channels // dev_count
    conv = conv.reshape(dev_count, FINE, 2, HALF)[..., :each]
    conv = jnp.transpose(conv, (2, 1, 0, 3)).reshape(2 * FINE, channels).astype(f32)
    return (terms[0].astype(f32) * conv + terms[1].astype(f32)).astype(bf16)


def solution(mesh):
    return jax.shard_map(
        local,
        mesh=mesh,
        in_specs=(
            P(("context", "tensor"), None),
            P(),
            P(None, None, "tensor"),
            P(None, None, "tensor"),
            P("context", "tensor"),
            P("tensor"),
        ),
        out_specs=P("context", "tensor"),
        check_vma=False,
    )
```
